256 devices in a mesh: sim: 64 (over x, y_lo, z), grp: 4 (over y_hi, core).
Axes of the slice: x: 4, y: 4 (y_hi: 2, y_lo: 2; y = y_hi * 2 + y_lo), z: 8, core: 2. Of those that a mesh axis runs over, the one named last changes fastest.
Arguments:
- velocity: float32 [64, 4, 3, 256, 512], P('sim', 'grp'), may hold values from -6 to 6
- slot_of: int32 [64, 4, 256], P('sim', 'grp'), may hold values from 0 to 255, each once within a row
- w_encode: bfloat16 [1024, 256], replicated, may hold values from -0.1875 to 0.1875
- w_conv: bfloat16 [27, 256, 256], replicated, may hold values from -0.078125 to 0.078125
- w_head: bfloat16 [256, 128], replicated, may hold values from -0.375 to 0.375
Outputs:
- velocity_next: float32 [64, 4, 3, 256, 512], P('sim', 'grp')
- grad_encode: float32 [1024, 256], P(None, 'grp')
- grad_conv: float32 [27, 256, 256], P(None, None, 'grp')
- grad_head: float32 [256, 128], P('grp')
The draws below stay inside these ranges and needn't reach their ends.
Inputs may be any that keep to these rules, and one draw needn't show every extreme that they name: `slot_of`: each block's row of 256 entries names every slot once.
All inputs are finite; a program needn't handle non-finite values.
Results may differ from the reference program's by a relative error of at most 0.0085.
Values may be sent and summed in bfloat16 or wider, within the bound.
A program may use at most 128 MiB of HBM per device.

```python
import jax
import jax.numpy as jnp
import numpy as np
from jax import lax

NP = 8
PTS = 512
CH = 256
FEAT = 1024
OUT = 128
TAPS = 27
EX = 2
EY = 4
EZ = 32
STEPS = 2
E_DEV = 256
NXE = 128
NYE = 16
CZ = 8
ELEMS = 65536
N_SIM = 64
N_GRP = 4


def shard_levels(rng, dims, pieces, smallest, high):
    def one(position, shards_of):
        heights = jax.random.uniform(jax.random.fold_in(jax.random.fold_in(rng, 6), position), (shards_of,), jnp.float32, smallest / len(pieces), high / len(pieces))
        return jnp.repeat(jnp.exp(heights), dims[position] // shards_of).reshape((-1,) + (1,) * (len(dims) - position - 1))

    factor_of = one(*pieces[0])
    for cut in pieces[1:]:
        factor_of = factor_of * one(*cut)
    return factor_of


def normal_values(key, shape, scale, limit, split=(), kind=jnp.bfloat16):
    array = scale * jax.random.normal(key, shape, jnp.float32)
    if split:
        array = array * shard_levels(key, shape, split, -0.22, 0.18)
    return jnp.clip(array, -limit, limit).astype(kind)


def setup_inputs(seed: int = 0) -> dict:
    seeds = jax.random.split(jax.random.key(seed), 6)
    velocity = normal_values(seeds[0], (N_SIM, N_GRP, 3, E_DEV, PTS), 1.0, 6.0, ((0, 64), (1, 4)), jnp.float32)
    slot_of = jax.vmap(lambda own: jax.random.permutation(own, E_DEV))(jax.random.split(seeds[1], N_SIM * N_GRP)).reshape((N_SIM, N_GRP, E_DEV)).astype(jnp.int32)
    w_encode = normal_values(seeds[2], (FEAT, CH), FEAT ** -0.5, 0.1875)
    w_conv = normal_values(seeds[3], (TAPS, CH, CH), (27 * CH) ** -0.5, 0.078125)
    w_head = normal_values(seeds[4], (CH, OUT), CH ** -0.5, 0.375)
    return {"velocity": velocity, "slot_of": slot_of, "w_encode": w_encode, "w_conv": w_conv, "w_head": w_head}


VISCOSITY = 0.2
TIME_STEP = 0.005
PENALTY = 100.0
LOSS_WEIGHT = 64.0

def derivative_matrix(count):
    places = np.arange(count)
    points = -np.cos(np.pi * places / (count - 1))
    weights = np.where(places % 2 == 0, 1.0, -1.0)
    weights[0] = weights[0] * 0.5
    weights[count - 1] = weights[count - 1] * 0.5
    identity = np.eye(count)
    spread = points[:, None] - points[None, :] + identity
    deriv = weights[None, :] / weights[:, None] / spread
    deriv = deriv * (1.0 - identity)
    return deriv - identity * deriv.sum(axis=1)[:, None]

def element_tables(count):
    deriv = derivative_matrix(count)
    single = np.eye(count)
    square = np.eye(count * count)
    along_x = np.kron(deriv, square)
    along_y = np.kron(single, np.kron(deriv, single))
    along_z = np.kron(square, deriv)
    laplace = along_x @ along_x + along_y @ along_y + along_z @ along_z
    stencil = np.concatenate([along_x.T, along_y.T, along_z.T, laplace.T], axis=1)
    grid = np.arange(count ** 3).reshape(count, count, count)
    final = count - 1
    chosen = np.concatenate([grid[0].ravel(), grid[final].ravel(), grid[:, 0].ravel(), grid[:, final].ravel(), grid[:, :, 0].ravel(), grid[:, :, final].ravel()])
    select = np.zeros((count ** 3, chosen.size))
    select[chosen, np.arange(chosen.size)] = 1.0
    bottom = np.zeros((count ** 3, count * count))
    for first in range(count):
        for middle in range(count):
            for inner in range(count):
                bottom[grid[first, middle, inner], first * count + inner] = VISCOSITY * deriv[0, middle]
    return (jnp.asarray(stencil, jnp.float32), jnp.asarray(select, jnp.float32), jnp.asarray(bottom, jnp.float32))

def silu_grad(value):
    sigma = jax.nn.sigmoid(value)
    return sigma * (1.0 + value * (1.0 - sigma))

def advance(field, faces, beside, stencil, select):
    points = field.shape[-1]
    derived = jnp.einsum('cxyzp,pq->cxyzq', field, stencil, precision=lax.Precision.HIGHEST)
    advect = field[0][None] * derived[..., 0:points]
    advect = advect + field[1][None] * derived[..., points:2 * points]
    advect = advect + field[2][None] * derived[..., 2 * points:3 * points]
    laplace = derived[..., 3 * points:]
    penalty = jnp.einsum('cxyzq,pq->cxyzp', beside - faces, select, precision=lax.Precision.HIGHEST)
    return field + TIME_STEP * (VISCOSITY * (laplace + PENALTY * penalty) - advect)

def face_part(faces, which):
    width = faces.shape[-1] // 6
    return faces[..., which * width:(which + 1) * width]

def reorder(blocks, slots):
    return jax.vmap(jax.vmap(lambda values, order: values[:, order]))(blocks, slots)

def window(padded, shift_x, shift_y, shift_z, sizes):
    part = padded[:, 1 + shift_x:1 + shift_x + sizes[0], 1 + shift_y:1 + shift_y + sizes[1], 1 + shift_z:1 + shift_z + sizes[2]]
    return part.reshape(-1, padded.shape[-1])

def reference(velocity, slot_of, w_encode, w_conv, w_head):
    stencil, select, bottom = element_tables(NP)
    ordered = reorder(velocity, slot_of)
    field = ordered.reshape(N_SIM, N_GRP, 3, EX, EY, EZ, PTS).transpose(2, 0, 3, 1, 4, 5, 6).reshape(3, NXE, NYE, EZ, PTS)
    for step in range(STEPS):
        faces = jnp.einsum('cxyzp,pq->cxyzq', field, select, precision=lax.Precision.HIGHEST)
        before_x = jnp.roll(face_part(faces, 1), 1, axis=1)
        after_x = jnp.roll(face_part(faces, 0), -1, axis=1)
        zero_layer = jnp.zeros_like(face_part(faces, 2)[:, :, :1])
        below = jnp.concatenate([zero_layer, face_part(faces, 3)[:, :, :-1]], axis=2)
        above = jnp.concatenate([face_part(faces, 2)[:, :, 1:], zero_layer], axis=2)
        before_z = jnp.roll(face_part(faces, 5), 1, axis=3)
        after_z = jnp.roll(face_part(faces, 4), -1, axis=3)
        beside = jnp.concatenate([before_x, after_x, below, above, before_z, after_z], axis=-1)
        field = advance(field, faces, beside, stencil, select)
    back = field.reshape(3, N_SIM, EX, N_GRP, EY, EZ, PTS).transpose(1, 3, 0, 2, 4, 5, 6).reshape(N_SIM, N_GRP, 3, E_DEV, PTS)
    inverse = jnp.argsort(slot_of, axis=-1).astype(jnp.int32)
    velocity_next = reorder(back, inverse)
    snapshot = jnp.concatenate([field[0], field[2]], axis=-1).astype(jnp.bfloat16)
    wall_low = jnp.einsum('xyzp,pq->xyzq', field[0], bottom, precision=lax.Precision.HIGHEST)
    wall_side = jnp.einsum('xyzp,pq->xyzq', field[2], bottom, precision=lax.Precision.HIGHEST)
    target = jnp.concatenate([wall_low, wall_side], axis=-1).astype(jnp.bfloat16)

    def cropped(values):
        shaped = values.reshape(N_SIM, EX, NYE, N_GRP, CZ, values.shape[-1])
        return shaped.transpose(0, 3, 1, 2, 4, 5).reshape(N_SIM * N_GRP, EX, NYE, CZ, values.shape[-1])
    crop_x = cropped(snapshot)
    crop_t = cropped(target).reshape(-1, OUT)
    sizes = (EX, NYE, CZ)
    rows = crop_x.reshape(-1, FEAT)
    z1 = jnp.dot(rows, w_encode, preferred_element_type=jnp.float32)
    h1 = jax.nn.silu(z1).astype(jnp.bfloat16)
    crops = crop_x.shape[0]
    pad_one = jnp.pad(h1.reshape(crops, EX, NYE, CZ, CH), ((0, 0), (1, 1), (1, 1), (1, 1), (0, 0)))
    offsets = [(sx, sy, sz) for sx in (-1, 0, 1) for sy in (-1, 0, 1) for sz in (-1, 0, 1)]
    z2 = jnp.zeros((rows.shape[0], CH), jnp.float32)
    for index, (sx, sy, sz) in enumerate(offsets):
        z2 = z2 + jnp.dot(window(pad_one, sx, sy, sz, sizes), w_conv[index], preferred_element_type=jnp.float32)
    h2 = jax.nn.silu(z2).astype(jnp.bfloat16)
    output = jnp.dot(h2, w_head, preferred_element_type=jnp.float32)
    resid = (LOSS_WEIGHT * (output - crop_t.astype(jnp.float32)) / ELEMS).astype(jnp.bfloat16)
    grad_head = jnp.dot(h2.T, resid, preferred_element_type=jnp.float32)
    dh2 = jnp.dot(resid, w_head.T, preferred_element_type=jnp.float32)
    dz2 = (dh2 * silu_grad(z2)).astype(jnp.bfloat16)
    pad_two = jnp.pad(dz2.reshape(crops, EX, NYE, CZ, CH), ((0, 0), (1, 1), (1, 1), (1, 1), (0, 0)))
    grad_list = []
    dh1 = jnp.zeros((rows.shape[0], CH), jnp.float32)
    for index, (sx, sy, sz) in enumerate(offsets):
        grad_list.append(jnp.dot(window(pad_one, sx, sy, sz, sizes).T, dz2, preferred_element_type=jnp.float32))
        dh1 = dh1 + jnp.dot(window(pad_two, -sx, -sy, -sz, sizes), w_conv[index].T, preferred_element_type=jnp.float32)
    grad_conv = jnp.stack(grad_list)
    dz1 = (dh1 * silu_grad(z1)).astype(jnp.bfloat16)
    grad_encode = jnp.dot(rows.T, dz1, preferred_element_type=jnp.float32)
    return (velocity_next, grad_encode, grad_conv, grad_head)
```

```python
import jax
import jax.numpy as jnp
import ml_dtypes
import numpy as np
from jax import lax
from jax.experimental import pallas as pl
from jax.experimental.pallas import tpu as pltpu
from jax.sharding import PartitionSpec as P

NP = 8
STEPS = 2
VISCOSITY = 0.2
TIME_STEP = 0.005
PENALTY = 100.0
LOSS_WEIGHT = 64.0

MESH = pl.DeviceIdType.MESH
F32 = jnp.float32
BF16 = jnp.bfloat16

GRAD_ROWS = 2048
CONV_ROWS = 1728
ENC_ROW = 1728
HEAD_ROW = 1984
PAD_ROW = 2016


def derivative_matrix(count):
    places = np.arange(count)
    points = -np.cos(np.pi * places / (count - 1))
    weights = np.where(places % 2 == 0, 1.0, -1.0)
    weights[0] = weights[0] * 0.5
    weights[count - 1] = weights[count - 1] * 0.5
    identity = np.eye(count)
    spread = points[:, None] - points[None, :] + identity
    deriv = weights[None, :] / weights[:, None] / spread
    deriv = deriv * (1.0 - identity)
    return deriv - identity * deriv.sum(axis=1)[:, None]


def element_tables(count):
    deriv = derivative_matrix(count)
    single = np.eye(count)
    square = np.eye(count * count)
    along_x = np.kron(deriv, square)
    along_y = np.kron(single, np.kron(deriv, single))
    along_z = np.kron(square, deriv)
    laplace = along_x @ along_x + along_y @ along_y + along_z @ along_z
    grid = np.arange(count**3).reshape(count, count, count)
    final = count - 1
    chosen = np.concatenate(
        [
            grid[0].ravel(),
            grid[final].ravel(),
            grid[:, 0].ravel(),
            grid[:, final].ravel(),
            grid[:, :, 0].ravel(),
            grid[:, :, final].ravel(),
        ]
    )
    select = np.zeros((count**3, chosen.size))
    select[chosen, np.arange(chosen.size)] = 1.0
    bottom = np.zeros((count**3, 2 * count * count))
    for first in range(count):
        for middle in range(count):
            for inner in range(count):
                bottom[grid[first, middle, inner], first * count + inner] = (
                    VISCOSITY * deriv[0, middle]
                )
    diffuse = TIME_STEP * VISCOSITY * (laplace.T - PENALTY * (select @ select.T))
    half = count**3 // 2
    swapped = select.reshape(count**3, 3, 2, count * count)[:, :, ::-1].reshape(count**3, -1)
    small = lambda table: np.asarray(table, ml_dtypes.bfloat16)
    return (
        small(np.concatenate([TIME_STEP * along_x.T, diffuse], axis=1)),
        small(
            TIME_STEP
            * np.concatenate([along_y.T[:half, :half], along_z.T[:half, :half]], axis=1)
        ),
        small(select),
        small(swapped.T),
        np.asarray(bottom, np.float32),
    )


def dot(a, b):
    return lax.dot_general(a, b, (((1,), (0,)), ((), ())), preferred_element_type=F32)


def dot_rows(a, b):
    return lax.dot_general(a, b, (((0,), (0,)), ((), ())), preferred_element_type=F32)


def dot_cols(a, b):
    return lax.dot_general(a, b, (((1,), (1,)), ((), ())), preferred_element_type=F32)


def parts(value):
    high = value.astype(BF16)
    return high, (value - high.astype(F32)).astype(BF16)


def silu_grad(value):
    sigma = jax.nn.sigmoid(value)
    return sigma * (1.0 + value * (1.0 - sigma))


def lanes_low(shape):
    return lax.broadcasted_iota(jnp.int32, shape, len(shape) - 1) < 64


def remote(src, dst, send, recv, device):
    return pltpu.make_async_remote_copy(
        src_ref=src,
        dst_ref=dst,
        send_sem=send,
        recv_sem=recv,
        device_id=device,
        device_id_type=MESH,
    )


def greet(devices):
    barrier = pltpu.get_barrier_semaphore()
    for device in devices:
        pl.semaphore_signal(barrier, inc=1, device_id=device, device_id_type=MESH)
    pl.semaphore_wait(barrier, len(devices))


def flow_kernel(
    sims,
    vel_ref,
    slot_ref,
    wide_ref,
    narrow_ref,
    sel_ref,
    unsel_ref,
    bottom_ref,
    enc_ref,
    out_ref,
    h1_ref,
    z1_ref,
    snap_ref,
    target_ref,
    perm,
    field,
    partial,
    faces,
    send_x,
    send_y,
    recv_x,
    recv_y,
    send_sem,
    recv_sem,
):
    sim = lax.axis_index("sim")
    grp = lax.axis_index("grp")
    right = (lax.rem(sim + 1, sims), grp)
    left = (lax.rem(sim + sims - 1, sims), grp)
    above = (sim, lax.rem(grp + 1, 4))
    below = (sim, lax.rem(grp + 3, 4))
    greet([right, left, above, below])

    owner = lax.broadcasted_iota(jnp.int32, (256, 256), 0)
    by_slot = jnp.where(owner == slot_ref[...], 1.0, 0.0).astype(F32)
    by_place = by_slot.T
    for ix in range(2):
        for iy in range(4):
            for j in range(4):
                old = ix * 128 + iy * 32 + j * 8
                new = j * 64 + iy * 16 + ix * 8
                perm[new : new + 8] = by_place[old : old + 8]
    gather = perm[...].astype(BF16)
    for c in range(3):
        high, low = parts(vel_ref[c])
        field[0, c] = dot(gather, high) + dot(gather, low)

    for step in range(STEPS):
        now, later = step % 2, (step + 1) % 2
        for c in range(3):
            faces[c] = dot(field[now, c].astype(BF16), sel_ref[...])
            along_x = faces[c, :, 0:128].reshape(16, 2, 8, 128)
            along_y = faces[c, :, 128:256].reshape(4, 4, 16, 128)
            send_x[step, 0, c] = along_x[:, 1].reshape(128, 128).astype(BF16)
            send_x[step, 1, c] = along_x[:, 0].reshape(128, 128).astype(BF16)
            send_y[step, 0, c] = along_y[:, 3].reshape(64, 128).astype(BF16)
            send_y[step, 1, c] = along_y[:, 0].reshape(64, 128).astype(BF16)
        copies = []
        for k, (src, dst, device) in enumerate(
            [
                (send_x.at[step, 0], recv_x.at[step, 0], right),
                (send_x.at[step, 1], recv_x.at[step, 1], left),
                (send_y.at[step, 0], recv_y.at[step, 0], above),
                (send_y.at[step, 1], recv_y.at[step, 1], below),
            ]
        ):
            copy = remote(src, dst, send_sem.at[step, k], recv_sem.at[step, k], device)
            copy.start()
            copies.append(copy)
        for c in range(3):
            for row in range(0, 256, 128):
                rows = slice(row, row + 128)
                mine = field[now, c, rows].astype(BF16)
                for h in range(0, 512, 256):
                    cols = slice(h, h + 256)
                    d_x = dot(mine, wide_ref[:, h : h + 256])
                    spread = dot(mine, wide_ref[:, 512 + h : 768 + h])
                    d_y = dot(mine[:, cols], narrow_ref[:, 0:256])
                    d_z = dot(mine[:, cols], narrow_ref[:, 256:512])
                    advect = field[now, 0, rows, cols] * d_x
                    advect = advect + field[now, 1, rows, cols] * d_y
                    advect = advect + field[now, 2, rows, cols] * d_z
                    partial[c, rows, cols] = field[now, c, rows, cols] + (spread - advect)
        for copy in copies:
            copy.wait()
        for c in range(3):
            along_x = faces[c, :, 0:128].reshape(16, 2, 8, 128)
            along_y = faces[c, :, 128:256].reshape(4, 4, 16, 128)
            along_z = faces[c, :, 256:384].reshape(4, 8, 8, 128)
            from_left = recv_x[step, 0, c].astype(F32).reshape(16, 1, 8, 128)
            from_right = recv_x[step, 1, c].astype(F32).reshape(16, 1, 8, 128)
            from_below = recv_y[step, 0, c].astype(F32).reshape(4, 1, 16, 128)
            from_above = recv_y[step, 1, c].astype(F32).reshape(4, 1, 16, 128)
            from_below = jnp.where(grp > 0, from_below, 0.0)
            from_above = jnp.where(grp < 3, from_above, 0.0)
            before = jnp.concatenate([from_left, along_x[:, :1]], axis=1).reshape(256, 128)
            after = jnp.concatenate([along_x[:, 1:], from_right], axis=1).reshape(256, 128)
            low = lanes_low((256, 128))
            beside_x = jnp.where(low, after, before).astype(BF16)
            before = jnp.concatenate([from_below, along_y[:, :3]], axis=1).reshape(256, 128)
            after = jnp.concatenate([along_y[:, 1:], from_above], axis=1).reshape(256, 128)
            beside_y = jnp.where(low, after, before).astype(BF16)
            place = lax.broadcasted_iota(jnp.int32, (32, 8, 128), 1)
            flat_z = along_z.reshape(32, 8, 128)
            behind = jnp.concatenate([along_z[3:], along_z[:3]], axis=0).reshape(32, 8, 128)
            ahead = jnp.concatenate([along_z[1:], along_z[:1]], axis=0).reshape(32, 8, 128)
            before = pltpu.roll(jnp.where(place == 7, behind, flat_z), 1, 1).reshape(256, 128)
            after = pltpu.roll(jnp.where(place == 0, ahead, flat_z), 7, 1).reshape(256, 128)
            beside_z = jnp.where(low, after, before).astype(BF16)
            beside = jnp.concatenate([beside_x, beside_y, beside_z], axis=1)
            for h in range(0, 512, 256):
                cols = slice(h, h + 256)
                pull = dot(beside, unsel_ref[:, cols])
                field[later, c, :, cols] = (
                    partial[c, :, cols] + (TIME_STEP * VISCOSITY * PENALTY) * pull
                )

    final = STEPS % 2
    snap_ref[:, 0:512] = field[final, 0].astype(BF16)
    snap_ref[:, 512:1024] = field[final, 2].astype(BF16)
    z1 = dot(snap_ref[...], enc_ref[...])
    z1_ref[...] = z1
    h1_ref[...] = (z1 * jax.nn.sigmoid(z1)).astype(BF16).reshape(4, 64, 256)
    table_high, table_low = parts(bottom_ref[...])
    stress = []
    for c in (0, 2):
        high, low = parts(field[final, c])
        stress.append(dot(high, table_high) + dot(high, table_low) + dot(low, table_high))
    side = pltpu.roll(stress[1], 64, 1)
    both = jnp.where(lanes_low((256, 128)), stress[0], side).astype(BF16)
    target_ref[...] = both.reshape(4, 64, 128)
    scatter = perm[...].T.astype(BF16)
    for c in range(3):
        high, low = parts(field[final, c])
        out_ref[c] = dot(scatter, high) + dot(scatter, low)


def variants(value, width):
    place = lax.broadcasted_iota(jnp.int32, (32, 8, width), 1)
    flat = value.reshape(32, 8, width)
    along_z = {
        -1: jnp.where(place == 0, 0.0, pltpu.roll(flat, 1, 1)),
        0: flat,
        1: jnp.where(place == 7, 0.0, pltpu.roll(flat, 7, 1)),
    }
    for dz in (-1, 0, 1):
        full = along_z[dz].reshape(16, 2, 8, width)
        none = jnp.zeros((16, 1, 8, width), F32)
        yield -1, dz, jnp.concatenate([none, full[:, :1]], axis=1).reshape(256, width)
        yield 0, dz, full.reshape(256, width)
        yield 1, dz, jnp.concatenate([full[:, 1:], none], axis=1).reshape(256, width)


def train_kernel(
    h1_ref,
    target_ref,
    z1_ref,
    snap_ref,
    conv_ref,
    head_ref,
    out_ref,
    crop_h,
    crop_t,
    all_h,
    shifted,
    dz2_buf,
    all_dz2,
    shifted_low,
    shifted_high,
    taps,
    dh1_buf,
    all_dh1,
    enc_buf,
    all_enc,
    head_buf,
    all_head,
    send_sem,
    recv_sem,
):
    sim = lax.axis_index("sim")
    grp = lax.axis_index("grp")
    peers = [lax.rem(grp + d, 4) for d in (1, 2, 3)]
    greet([(sim, peer) for peer in peers])

    def block(index):
        return pl.ds(pl.multiple_of(index * 64, 64), 64)

    def exchange(kind, pairs):
        copies = []
        for d, (src, dst) in enumerate(pairs):
            copy = remote(src, dst, send_sem.at[kind, d], recv_sem.at[kind, d], (sim, peers[d]))
            copy.start()
            copies.append(copy)
        return copies

    h_copies = exchange(0, [(h1_ref.at[p], crop_h.at[grp]) for p in peers])
    t_copies = exchange(1, [(target_ref.at[p], crop_t.at[grp]) for p in peers])
    crop_h[grp] = h1_ref[grp]
    crop_t[grp] = target_ref[grp]
    all_h[:, grp] = h1_ref[...]
    whole = [(h1_ref, all_h.at[:, grp]) for p in peers]

    for k in range(9):
        shifted[k, 0:16] = jnp.zeros((16, 256), BF16)
        shifted[k, 272:288] = jnp.zeros((16, 256), BF16)
        for j in range(4):
            shifted_low[k, j, 0:16] = jnp.zeros((16, 128), BF16)
            shifted_low[k, j, 272:288] = jnp.zeros((16, 128), BF16)
            shifted_high[k, j, 0:16] = jnp.zeros((16, 128), BF16)
            shifted_high[k, j, 272:288] = jnp.zeros((16, 128), BF16)

    a_copies = exchange(2, whole)
    for copy in h_copies:
        copy.wait()
    value = crop_h[...].reshape(256, 256).astype(F32)
    for dx, dz, moved in variants(value, 256):
        shifted[3 * (dx + 1) + dz + 1, 16:272] = moved.astype(BF16)
    z2 = jnp.zeros((256, 256), F32)
    for dx in (-1, 0, 1):
        for dy in (-1, 0, 1):
            for dz in (-1, 0, 1):
                tap = 9 * (dx + 1) + 3 * (dy + 1) + dz + 1
                start = 16 * (1 + dy)
                z2 = z2 + dot(
                    shifted[3 * (dx + 1) + dz + 1, start : start + 256], conv_ref[tap]
                )
    h2 = (z2 * jax.nn.sigmoid(z2)).astype(BF16)
    output = dot(h2, head_ref[...])
    for copy in t_copies:
        copy.wait()
    target = crop_t[...].reshape(256, 128).astype(F32)
    resid = ((output - target) * (LOSS_WEIGHT / 65536.0)).astype(BF16)
    dz2 = (dot_cols(resid, head_ref[...]) * silu_grad(z2)).astype(BF16)
    dz2_buf[0] = dz2[:, 0:128]
    dz2_buf[1] = dz2[:, 128:256]
    all_dz2[grp] = dz2_buf[grp // 2]
    z_copies = exchange(3, [(dz2_buf.at[p // 2], all_dz2.at[grp]) for p in peers])
    head_buf[...] = dot_rows(h2, resid).astype(BF16).reshape(4, 64, 128)
    g_copies = exchange(4, [(head_buf.at[p], all_head.at[d]) for d, p in enumerate(peers)])

    for dx, dz, moved in variants(dz2.astype(F32), 256):
        shifted[3 * (dx + 1) + dz + 1, 16:272] = moved.astype(BF16)
    dh1 = jnp.zeros((256, 256), F32)
    for dx in (-1, 0, 1):
        for dy in (-1, 0, 1):
            for dz in (-1, 0, 1):
                tap = 9 * (dx + 1) + 3 * (dy + 1) + dz + 1
                start = 16 * (1 - dy)
                dh1 = dh1 + dot_cols(
                    shifted[3 * (1 - dx) + 1 - dz, start : start + 256], conv_ref[tap]
                )
    dh1_buf[...] = dh1.astype(BF16).reshape(4, 64, 256)
    all_dh1[grp] = dh1_buf[grp]
    d_copies = exchange(5, [(dh1_buf.at[p], all_dh1.at[grp]) for p in peers])

    for copy in z_copies:
        copy.wait()
    low = lanes_low((256, 128))
    for j in range(4):
        value = all_dz2[j].astype(F32)
        turned = pltpu.roll(value, 64, 1)
        first = lax.rem(grp, 2) == 0
        here = jnp.where(low, jnp.where(first, value, turned), jnp.where(first, turned, value))
        for dx, dz, moved in variants(here, 128):
            k = 3 * (dx + 1) + dz + 1
            shifted_low[k, j, 16:272] = jnp.where(low, moved, 0.0).astype(BF16)
            shifted_high[k, j, 16:272] = jnp.where(low, 0.0, moved).astype(BF16)
    for copy in a_copies:
        copy.wait()

    def tap_place(tap):
        dx, dy, dz = tap // 9 - 1, tap // 3 % 3 - 1, tap % 3 - 1
        return 3 * (1 - dx) + 1 - dz, 16 * (1 - dy)

    def conv_grad(pairs):
        for place, pair in enumerate(pairs):
            for j in range(4):
                k, start = tap_place(2 * pair)
                value = shifted_low[k, j, start : start + 256]
                if 2 * pair + 1 < 27:
                    k, start = tap_place(2 * pair + 1)
                    value = value + shifted_high[k, j, start : start + 256]
                taps[j * 256 : j * 256 + 256, place * 128 : place * 128 + 128] = value
        width = 128 * len(pairs)
        grad = dot_rows(taps[:, 0:width], all_h[...].reshape(1024, 256))
        first = 128 * pairs[0]
        last = min(first + width, CONV_ROWS)
        out_ref[first:last] = grad[: last - first]

    conv_grad([0, 1, 2, 3])
    conv_grad([4, 5, 6, 7])
    for copy in d_copies:
        copy.wait()
    dz1 = (all_dh1[...].reshape(256, 256).astype(F32) * silu_grad(z1_ref[...])).astype(BF16)
    for b in range(4):
        enc_buf[b] = dot_rows(dz1, snap_ref[:, b * 256 : b * 256 + 256])
    own_block = block(grp)
    for d, p in enumerate(peers):
        for b in range(4):
            all_enc[0, d, b] = enc_buf[b, block(p)].astype(BF16)
    e_copies = exchange(6, [(all_enc.at[0, d], all_enc.at[1, d]) for d in range(3)])
    conv_grad([8, 9, 10, 11])
    conv_grad([12, 13])
    for copy in e_copies + g_copies:
        copy.wait()
    for b in range(4):
        total = enc_buf[b, own_block]
        for d in range(3):
            total = total + all_enc[1, d, b].astype(F32)
        out_ref[ENC_ROW + b * 64 : ENC_ROW + b * 64 + 64] = total
    total = head_buf[grp].astype(F32)
    for d in range(3):
        total = total + all_head[d].astype(F32)
    out_ref[HEAD_ROW:PAD_ROW, 0:128] = total[0:32]
    out_ref[HEAD_ROW:PAD_ROW, 128:256] = total[32:64]
    out_ref[PAD_ROW:GRAD_ROWS] = jnp.zeros((GRAD_ROWS - PAD_ROW, 256), F32)


def reduce_kernel(
    grad_ref,
    conv_ref,
    enc_ref,
    head_ref,
    work,
    recv_x,
    work_z,
    recv_z,
    work_y,
    recv_y,
    sum_x,
    sum_z,
    result,
    send_sem,
    recv_sem,
):
    sim = lax.axis_index("sim")
    grp = lax.axis_index("grp")
    x, y, z = sim // 16, lax.rem(sim // 8, 2), lax.rem(sim, 8)
    peers_x = [lax.rem(x + d, 4) for d in range(1, 4)]
    peers_z = [lax.rem(z + d, 8) for d in range(1, 8)]
    dev_x = [(p * 16 + y * 8 + z, grp) for p in peers_x]
    dev_z = [(x * 16 + y * 8 + p, grp) for p in peers_z]
    dev_y = (x * 16 + (1 - y) * 8 + z, grp)
    greet(dev_x + dev_z + [dev_y])

    def rows(index, count):
        return pl.ds(pl.multiple_of(index * count, count), count)

    def start(base, triples):
        copies = []
        for d, (src, dst, device) in enumerate(triples):
            copy = remote(src, dst, send_sem.at[base + d], recv_sem.at[base + d], device)
            copy.start()
            copies.append(copy)
        return copies

    def finish(copies):
        for copy in copies:
            copy.wait()

    work[...] = grad_ref[...].astype(BF16)
    copies = start(
        0, [(work.at[rows(peers_x[d], 512)], recv_x.at[d], dev_x[d]) for d in range(3)]
    )
    finish(copies)
    total = grad_ref[rows(x, 512)]
    for d in range(3):
        total = total + recv_x[d].astype(F32)
    sum_x[...] = total
    work_z[...] = total.astype(BF16)
    copies = start(
        3, [(work_z.at[rows(peers_z[d], 64)], recv_z.at[d], dev_z[d]) for d in range(7)]
    )
    finish(copies)
    total = sum_x[rows(z, 64)]
    for d in range(7):
        total = total + recv_z[d].astype(F32)
    sum_z[...] = total
    work_y[...] = total.astype(BF16)
    finish(start(10, [(work_y.at[rows(1 - y, 32)], recv_y, dev_y)]))
    total = sum_z[rows(y, 32)] + recv_y[...].astype(F32)
    base = x * 512 + z * 64
    mine = pl.ds(pl.multiple_of(base + y * 32, 32), 32)
    result[mine] = total.astype(BF16)
    finish(start(11, [(result.at[mine], result.at[mine], dev_y)]))
    mine = pl.ds(pl.multiple_of(base, 64), 64)
    finish(start(12, [(result.at[mine], result.at[mine], dev_z[d]) for d in range(7)]))
    mine = rows(x, 512)
    finish(start(19, [(result.at[mine], result.at[mine], dev_x[d]) for d in range(3)]))
    conv_ref[...] = result[0:CONV_ROWS].astype(F32)
    for b in range(4):
        enc_ref[:, b * 256 : b * 256 + 256] = result[
            ENC_ROW + b * 64 : ENC_ROW + b * 64 + 64
        ].astype(F32)
    head_ref[0:32] = result[HEAD_ROW:PAD_ROW, 0:128].astype(F32)
    head_ref[32:64] = result[HEAD_ROW:PAD_ROW, 128:256].astype(F32)


VM = pl.BlockSpec(memory_space=pltpu.VMEM)


def shaped(shape, dtype):
    return jax.ShapeDtypeStruct(shape, dtype)


def reduced(grads):
    dma = pltpu.SemaphoreType.DMA
    return pl.pallas_call(
        reduce_kernel,
        out_shape=(
            shaped((CONV_ROWS, 256), F32),
            shaped((64, 1024), F32),
            shaped((64, 128), F32),
        ),
        in_specs=[VM],
        out_specs=(VM, VM, VM),
        scratch_shapes=[
            pltpu.VMEM((GRAD_ROWS, 256), BF16),
            pltpu.VMEM((3, 512, 256), BF16),
            pltpu.VMEM((512, 256), BF16),
            pltpu.VMEM((7, 64, 256), BF16),
            pltpu.VMEM((64, 256), BF16),
            pltpu.VMEM((32, 256), BF16),
            pltpu.VMEM((512, 256), F32),
            pltpu.VMEM((64, 256), F32),
            pltpu.VMEM((GRAD_ROWS, 256), BF16),
            dma((22,)),
            dma((22,)),
        ],
        compiler_params=pltpu.CompilerParams(
            collective_id=2, has_side_effects=True, vmem_limit_bytes=32 * 2**20
        ),
    )(grads)


def body(velocity, slot_of, w_encode, w_conv, w_head):
    wide, narrow, select, unselect, bottom = element_tables(NP)
    dma = pltpu.SemaphoreType.DMA
    flow = pl.pallas_call(
        lambda *refs: flow_kernel(lax.axis_size("sim"), *refs),
        name="flow",
        out_shape=(
            shaped((3, 256, 512), F32),
            shaped((4, 64, 256), BF16),
            shaped((256, 256), F32),
            shaped((256, 1024), BF16),
            shaped((4, 64, 128), BF16),
        ),
        in_specs=[VM] * 8,
        out_specs=(VM,) * 5,
        scratch_shapes=[
            pltpu.VMEM((256, 256), F32),
            pltpu.VMEM((2, 3, 256, 512), F32),
            pltpu.VMEM((3, 256, 512), F32),
            pltpu.VMEM((3, 256, 384), F32),
            pltpu.VMEM((STEPS, 2, 3, 128, 128), BF16),
            pltpu.VMEM((STEPS, 2, 3, 64, 128), BF16),
            pltpu.VMEM((STEPS, 2, 3, 128, 128), BF16),
            pltpu.VMEM((STEPS, 2, 3, 64, 128), BF16),
            dma((STEPS, 4)),
            dma((STEPS, 4)),
        ],
        compiler_params=pltpu.CompilerParams(
            collective_id=0, has_side_effects=True, vmem_limit_bytes=48 * 2**20
        ),
    )
    velocity_next, h1, z1, snapshot, target = flow(
        velocity[0, 0], slot_of[0], wide, narrow, select, unselect, bottom, w_encode
    )
    train = pl.pallas_call(
        train_kernel,
        name="train",
        out_shape=shaped((GRAD_ROWS, 256), F32),
        in_specs=[VM] * 6,
        out_specs=VM,
        scratch_shapes=[
            pltpu.VMEM((4, 64, 256), BF16),
            pltpu.VMEM((4, 64, 128), BF16),
            pltpu.VMEM((4, 4, 64, 256), BF16),
            pltpu.VMEM((9, 288, 256), BF16),
            pltpu.VMEM((2, 256, 128), BF16),
            pltpu.VMEM((4, 256, 128), BF16),
            pltpu.VMEM((9, 4, 288, 128), BF16),
            pltpu.VMEM((9, 4, 288, 128), BF16),
            pltpu.VMEM((1024, 512), BF16),
            pltpu.VMEM((4, 64, 256), BF16),
            pltpu.VMEM((4, 64, 256), BF16),
            pltpu.VMEM((4, 256, 256), F32),
            pltpu.VMEM((2, 3, 4, 64, 256), BF16),
            pltpu.VMEM((4, 64, 128), BF16),
            pltpu.VMEM((3, 64, 128), BF16),
            dma((7, 3)),
            dma((7, 3)),
        ],
        compiler_params=pltpu.CompilerParams(
            collective_id=1, has_side_effects=True, vmem_limit_bytes=48 * 2**20
        ),
    )
    grads = train(h1, target, z1, snapshot, w_conv, w_head)
    conv, encode, head = reduced(grads)
    return (
        velocity_next[None, None],
        encode.T,
        conv.reshape(27, 64, 256).transpose(0, 2, 1),
        head,
    )


def solution(mesh):
    placed = (P("sim", "grp", None, None, None), P("sim", "grp", None), P(), P(), P())
    return jax.shard_map(
        body,
        mesh=mesh,
        in_specs=placed,
        out_specs=(
            P("sim", "grp", None, None, None),
            P(None, "grp"),
            P(None, None, "grp"),
            P("grp", None),
        ),
        check_vma=False,
    )
```

```python
import jax
import jax.numpy as jnp
import ml_dtypes
import numpy as np
from jax import lax
from jax.experimental import pallas as pl
from jax.experimental.pallas import tpu as pltpu
from jax.sharding import PartitionSpec as P

NP = 8
STEPS = 2
VISCOSITY = 0.2
TIME_STEP = 0.005
PENALTY = 100.0
LOSS_WEIGHT = 64.0

MESH = pl.DeviceIdType.MESH
F32 = jnp.float32
BF16 = jnp.bfloat16

CONV_ROWS = 1728
PARTS = 4


def derivative_matrix(count):
    places = np.arange(count)
    points = -np.cos(np.pi * places / (count - 1))
    weights = np.where(places % 2 == 0, 1.0, -1.0)
    weights[0] = weights[0] * 0.5
    weights[count - 1] = weights[count - 1] * 0.5
    identity = np.eye(count)
    spread = points[:, None] - points[None, :] + identity
    deriv = weights[None, :] / weights[:, None] / spread
    deriv = deriv * (1.0 - identity)
    return deriv - identity * deriv.sum(axis=1)[:, None]


def element_tables(count):
    deriv = derivative_matrix(count)
    single = np.eye(count)
    square = np.eye(count * count)
    along_x = np.kron(deriv, square)
    along_y = np.kron(single, np.kron(deriv, single))
    along_z = np.kron(square, deriv)
    laplace = along_x @ along_x + along_y @ along_y + along_z @ along_z
    grid = np.arange(count**3).reshape(count, count, count)
    final = count - 1
    chosen = np.concatenate(
        [
            grid[0].ravel(),
            grid[final].ravel(),
            grid[:, 0].ravel(),
            grid[:, final].ravel(),
            grid[:, :, 0].ravel(),
            grid[:, :, final].ravel(),
        ]
    )
    select = np.zeros((count**3, chosen.size))
    select[chosen, np.arange(chosen.size)] = 1.0
    bottom = np.zeros((count**3, 2 * count * count))
    for first in range(count):
        for middle in range(count):
            for inner in range(count):
                bottom[grid[first, middle, inner], first * count + inner] = (
                    VISCOSITY * deriv[0, middle]
                )
    diffuse = TIME_STEP * VISCOSITY * (laplace.T - PENALTY * (select @ select.T))
    half = count**3 // 2
    swapped = select.reshape(count**3, 3, 2, count * count)[:, :, ::-1].reshape(count**3, -1)
    small = lambda table: np.asarray(table, ml_dtypes.bfloat16)
    return (
        small(np.concatenate([TIME_STEP * along_x.T, diffuse], axis=1)),
        small(
            TIME_STEP
            * np.concatenate([along_y.T[:half, :half], along_z.T[:half, :half]], axis=1)
        ),
        small(select),
        small(swapped.T),
        np.asarray(bottom, np.float32),
    )


def dot(a, b):
    return lax.dot_general(a, b, (((1,), (0,)), ((), ())), preferred_element_type=F32)


def dot_rows(a, b):
    return lax.dot_general(a, b, (((0,), (0,)), ((), ())), preferred_element_type=F32)


def dot_cols(a, b):
    return lax.dot_general(a, b, (((1,), (1,)), ((), ())), preferred_element_type=F32)


def parts(value):
    high = value.astype(BF16)
    return high, (value - high.astype(F32)).astype(BF16)


def silu_grad(value):
    sigma = jax.nn.sigmoid(value)
    return sigma * (1.0 + value * (1.0 - sigma))


def lanes_low(shape):
    return lax.broadcasted_iota(jnp.int32, shape, len(shape) - 1) < 64


def remote(src, dst, send, recv, device):
    return pltpu.make_async_remote_copy(
        src_ref=src,
        dst_ref=dst,
        send_sem=send,
        recv_sem=recv,
        device_id=device,
        device_id_type=MESH,
    )


def greet(devices):
    barrier = pltpu.get_barrier_semaphore()
    for device in devices:
        pl.semaphore_signal(barrier, inc=1, device_id=device, device_id_type=MESH)
    pl.semaphore_wait(barrier, len(devices))


def variants(value, width):
    place = lax.broadcasted_iota(jnp.int32, (32, 8, width), 1)
    flat = value.reshape(32, 8, width)
    along_z = {
        -1: jnp.where(place == 0, 0.0, pltpu.roll(flat, 1, 1)),
        0: flat,
        1: jnp.where(place == 7, 0.0, pltpu.roll(flat, 7, 1)),
    }
    for dz in (-1, 0, 1):
        full = along_z[dz].reshape(16, 2, 8, width)
        none = jnp.zeros((16, 1, 8, width), F32)
        yield -1, dz, jnp.concatenate([none, full[:, :1]], axis=1).reshape(256, width)
        yield 0, dz, full.reshape(256, width)
        yield 1, dz, jnp.concatenate([full[:, 1:], none], axis=1).reshape(256, width)


def step_kernel(
    sims,
    vel_hbm,
    slot_hbm,
    wide_hbm,
    narrow_hbm,
    sel_hbm,
    unsel_hbm,
    bottom_hbm,
    enc_hbm,
    conv_hbm,
    head_hbm,
    out_ref,
    result,
    vel_ref,
    slot_ref,
    wide_ref,
    narrow_ref,
    sel_ref,
    unsel_ref,
    bottom_ref,
    enc_ref,
    conv_ref,
    head_ref,
    load_sem,
    perm,
    field,
    partial,
    faces,
    send_x,
    send_y,
    recv_x,
    recv_y,
    halo_send,
    halo_recv,
    h1_ref,
    z1_ref,
    snap_ref,
    target_ref,
    crop_h,
    crop_t,
    all_h,
    shifted,
    dz2_buf,
    all_dz2,
    shifted_low,
    shifted_high,
    taps,
    dh1_buf,
    all_dh1,
    enc_buf,
    enc_out,
    all_enc,
    head_buf,
    all_head,
    grp_send,
    grp_recv,
    work,
    recv_first,
    work_second,
    recv_second,
    sum_send,
    sum_recv,
):
    sim = lax.axis_index("sim")
    grp = lax.axis_index("grp")

    loads = []
    for k, (src, dst) in enumerate(
        [
            (slot_hbm, slot_ref),
            (vel_hbm, vel_ref),
            (sel_hbm, sel_ref),
            (wide_hbm, wide_ref),
            (narrow_hbm, narrow_ref),
            (unsel_hbm, unsel_ref),
            (enc_hbm, enc_ref),
            (bottom_hbm, bottom_ref),
            (conv_hbm, conv_ref),
            (head_hbm, head_ref),
        ]
    ):
        copy = pltpu.make_async_copy(src, dst, load_sem.at[k])
        copy.start()
        loads.append(copy)

    right = (lax.rem(sim + 1, sims), grp)
    left = (lax.rem(sim + sims - 1, sims), grp)
    above = (sim, lax.rem(grp + 1, 4))
    below = (sim, lax.rem(grp + 3, 4))
    peers = [lax.rem(grp + d, 4) for d in (1, 2, 3)]
    plane, depth = sim // 8, lax.rem(sim, 8)
    peers_plane = [lax.rem(plane + d, 8) for d in range(1, 8)]
    peers_depth = [lax.rem(depth + d, 8) for d in range(1, 8)]
    dev_plane = [(p * 8 + depth, grp) for p in peers_plane]
    dev_depth = [(plane * 8 + p, grp) for p in peers_depth]
    greet([left, right] + [(sim, peer) for peer in peers] + dev_plane + dev_depth)

    loads[0].wait()
    owner = lax.broadcasted_iota(jnp.int32, (256, 256), 0)
    by_slot = jnp.where(owner == slot_ref[...], 1.0, 0.0).astype(F32)
    by_place = by_slot.T
    for ix in range(2):
        for iy in range(4):
            for j in range(4):
                old = ix * 128 + iy * 32 + j * 8
                new = j * 64 + iy * 16 + ix * 8
                perm[new : new + 8] = by_place[old : old + 8]
    gather = perm[...].astype(BF16)
    loads[1].wait()
    for c in range(3):
        high, low = parts(vel_ref[c])
        field[0, c] = dot(gather, high) + dot(gather, low)
    for copy in loads[2:6]:
        copy.wait()

    for step in range(STEPS):
        now, later = step % 2, (step + 1) % 2
        for c in range(3):
            faces[c] = dot(field[now, c].astype(BF16), sel_ref[...])
            along_x = faces[c, :, 0:128].reshape(16, 2, 8, 128)
            along_y = faces[c, :, 128:256].reshape(4, 4, 16, 128)
            send_x[step, 0, c] = along_x[:, 1].reshape(128, 128).astype(BF16)
            send_x[step, 1, c] = along_x[:, 0].reshape(128, 128).astype(BF16)
            send_y[step, 0, c] = along_y[:, 3].reshape(64, 128).astype(BF16)
            send_y[step, 1, c] = along_y[:, 0].reshape(64, 128).astype(BF16)
        copies = []
        for k, (src, dst, device) in enumerate(
            [
                (send_x.at[step, 0], recv_x.at[step, 0], right),
                (send_x.at[step, 1], recv_x.at[step, 1], left),
                (send_y.at[step, 0], recv_y.at[step, 0], above),
                (send_y.at[step, 1], recv_y.at[step, 1], below),
            ]
        ):
            copy = remote(src, dst, halo_send.at[step, k], halo_recv.at[step, k], device)
            copy.start()
            copies.append(copy)
        for c in range(3):
            for row in range(0, 256, 128):
                rows = slice(row, row + 128)
                mine = field[now, c, rows].astype(BF16)
                for h in range(0, 512, 256):
                    cols = slice(h, h + 256)
                    d_x = dot(mine, wide_ref[:, h : h + 256])
                    spread = dot(mine, wide_ref[:, 512 + h : 768 + h])
                    d_y = dot(mine[:, cols], narrow_ref[:, 0:256])
                    d_z = dot(mine[:, cols], narrow_ref[:, 256:512])
                    advect = field[now, 0, rows, cols] * d_x
                    advect = advect + field[now, 1, rows, cols] * d_y
                    advect = advect + field[now, 2, rows, cols] * d_z
                    partial[c, rows, cols] = field[now, c, rows, cols] + (spread - advect)
        for copy in copies:
            copy.wait()
        for c in range(3):
            along_x = faces[c, :, 0:128].reshape(16, 2, 8, 128)
            along_y = faces[c, :, 128:256].reshape(4, 4, 16, 128)
            along_z = faces[c, :, 256:384].reshape(4, 8, 8, 128)
            from_left = recv_x[step, 0, c].astype(F32).reshape(16, 1, 8, 128)
            from_right = recv_x[step, 1, c].astype(F32).reshape(16, 1, 8, 128)
            from_below = recv_y[step, 0, c].astype(F32).reshape(4, 1, 16, 128)
            from_above = recv_y[step, 1, c].astype(F32).reshape(4, 1, 16, 128)
            from_below = jnp.where(grp > 0, from_below, 0.0)
            from_above = jnp.where(grp < 3, from_above, 0.0)
            before = jnp.concatenate([from_left, along_x[:, :1]], axis=1).reshape(256, 128)
            after = jnp.concatenate([along_x[:, 1:], from_right], axis=1).reshape(256, 128)
            low = lanes_low((256, 128))
            beside_x = jnp.where(low, after, before).astype(BF16)
            before = jnp.concatenate([from_below, along_y[:, :3]], axis=1).reshape(256, 128)
            after = jnp.concatenate([along_y[:, 1:], from_above], axis=1).reshape(256, 128)
            beside_y = jnp.where(low, after, before).astype(BF16)
            place = lax.broadcasted_iota(jnp.int32, (32, 8, 128), 1)
            flat_z = along_z.reshape(32, 8, 128)
            behind = jnp.concatenate([along_z[3:], along_z[:3]], axis=0).reshape(32, 8, 128)
            ahead = jnp.concatenate([along_z[1:], along_z[:1]], axis=0).reshape(32, 8, 128)
            before = pltpu.roll(jnp.where(place == 7, behind, flat_z), 1, 1).reshape(256, 128)
            after = pltpu.roll(jnp.where(place == 0, ahead, flat_z), 7, 1).reshape(256, 128)
            beside_z = jnp.where(low, after, before).astype(BF16)
            beside = jnp.concatenate([beside_x, beside_y, beside_z], axis=1)
            for h in range(0, 512, 256):
                cols = slice(h, h + 256)
                pull = dot(beside, unsel_ref[:, cols])
                field[later, c, :, cols] = (
                    partial[c, :, cols] + (TIME_STEP * VISCOSITY * PENALTY) * pull
                )

    final = STEPS % 2
    snap_ref[:, 0:512] = field[final, 0].astype(BF16)
    snap_ref[:, 512:1024] = field[final, 2].astype(BF16)
    for copy in loads[6:]:
        copy.wait()

    def block(index):
        return pl.ds(pl.multiple_of(index * 64, 64), 64)

    def exchange(kind, pairs):
        copies = []
        for d, (src, dst) in enumerate(pairs):
            copy = remote(src, dst, grp_send.at[kind, d], grp_recv.at[kind, d], (sim, peers[d]))
            copy.start()
            copies.append(copy)
        return copies

    z1 = dot(snap_ref[...], enc_ref[...])
    z1_ref[...] = z1
    h1_ref[...] = (z1 * jax.nn.sigmoid(z1)).astype(BF16).reshape(4, 64, 256)
    h_copies = exchange(0, [(h1_ref.at[p], crop_h.at[grp]) for p in peers])
    table_high, table_low = parts(bottom_ref[...])
    stress = []
    for c in (0, 2):
        high, low = parts(field[final, c])
        stress.append(dot(high, table_high) + dot(high, table_low) + dot(low, table_high))
    side = pltpu.roll(stress[1], 64, 1)
    both = jnp.where(lanes_low((256, 128)), stress[0], side).astype(BF16)
    target_ref[...] = both.reshape(4, 64, 128)
    t_copies = exchange(1, [(target_ref.at[p], crop_t.at[grp]) for p in peers])
    a_copies = exchange(2, [(h1_ref, all_h.at[:, grp]) for p in peers])
    crop_h[grp] = h1_ref[grp]
    crop_t[grp] = target_ref[grp]
    all_h[:, grp] = h1_ref[...]
    for k in range(9):
        shifted[k, 0:16] = jnp.zeros((16, 256), BF16)
        shifted[k, 272:288] = jnp.zeros((16, 256), BF16)
        for j in range(4):
            shifted_low[k, j, 0:16] = jnp.zeros((16, 128), BF16)
            shifted_low[k, j, 272:288] = jnp.zeros((16, 128), BF16)
            shifted_high[k, j, 0:16] = jnp.zeros((16, 128), BF16)
            shifted_high[k, j, 272:288] = jnp.zeros((16, 128), BF16)
    scatter = perm[...].T.astype(BF16)
    for c in range(3):
        high, low = parts(field[final, c])
        out_ref[c] = dot(scatter, high) + dot(scatter, low)

    for copy in h_copies:
        copy.wait()
    value = crop_h[...].reshape(256, 256).astype(F32)
    for dx, dz, moved in variants(value, 256):
        shifted[3 * (dx + 1) + dz + 1, 16:272] = moved.astype(BF16)
    z2 = jnp.zeros((256, 256), F32)
    for dx in (-1, 0, 1):
        for dy in (-1, 0, 1):
            for dz in (-1, 0, 1):
                tap = 9 * (dx + 1) + 3 * (dy + 1) + dz + 1
                start = 16 * (1 + dy)
                z2 = z2 + dot(
                    shifted[3 * (dx + 1) + dz + 1, start : start + 256], conv_ref[tap]
                )
    h2 = (z2 * jax.nn.sigmoid(z2)).astype(BF16)
    output = dot(h2, head_ref[...])
    for copy in t_copies:
        copy.wait()
    target = crop_t[...].reshape(256, 128).astype(F32)
    resid = ((output - target) * (LOSS_WEIGHT / 65536.0)).astype(BF16)
    dz2 = (dot_cols(resid, head_ref[...]) * silu_grad(z2)).astype(BF16)
    dz2_buf[0] = dz2[:, 0:128]
    dz2_buf[1] = dz2[:, 128:256]
    all_dz2[grp] = dz2_buf[grp // 2]
    z_copies = exchange(3, [(dz2_buf.at[p // 2], all_dz2.at[grp]) for p in peers])
    head_buf[...] = dot_rows(h2, resid).astype(BF16).reshape(4, 64, 128)
    g_copies = exchange(4, [(head_buf.at[p], all_head.at[d]) for d, p in enumerate(peers)])

    for dx, dz, moved in variants(dz2.astype(F32), 256):
        shifted[3 * (dx + 1) + dz + 1, 16:272] = moved.astype(BF16)
    dh1 = jnp.zeros((256, 256), F32)
    for dx in (-1, 0, 1):
        for dy in (-1, 0, 1):
            for dz in (-1, 0, 1):
                tap = 9 * (dx + 1) + 3 * (dy + 1) + dz + 1
                start = 16 * (1 - dy)
                dh1 = dh1 + dot_cols(
                    shifted[3 * (1 - dx) + 1 - dz, start : start + 256], conv_ref[tap]
                )
    dh1_buf[...] = dh1.astype(BF16).reshape(4, 64, 256)
    all_dh1[grp] = dh1_buf[grp]
    d_copies = exchange(5, [(dh1_buf.at[p], all_dh1.at[grp]) for p in peers])

    for copy in z_copies:
        copy.wait()
    low = lanes_low((256, 128))
    for j in range(4):
        value = all_dz2[j].astype(F32)
        turned = pltpu.roll(value, 64, 1)
        first = lax.rem(grp, 2) == 0
        here = jnp.where(low, jnp.where(first, value, turned), jnp.where(first, turned, value))
        for dx, dz, moved in variants(here, 128):
            k = 3 * (dx + 1) + dz + 1
            shifted_low[k, j, 16:272] = jnp.where(low, moved, 0.0).astype(BF16)
            shifted_high[k, j, 16:272] = jnp.where(low, 0.0, moved).astype(BF16)
    for copy in a_copies:
        copy.wait()

    def tap_place(tap):
        dx, dy, dz = tap // 9 - 1, tap // 3 % 3 - 1, tap % 3 - 1
        return 3 * (1 - dx) + 1 - dz, 16 * (1 - dy)

    def conv_grad(part):
        pairs = range(4 * part, min(4 * part + 4, 14))
        for place, pair in enumerate(pairs):
            for j in range(4):
                k, start = tap_place(2 * pair)
                value = shifted_low[k, j, start : start + 256]
                if 2 * pair + 1 < 27:
                    k, start = tap_place(2 * pair + 1)
                    value = value + shifted_high[k, j, start : start + 256]
                taps[j * 256 : j * 256 + 256, place * 128 : place * 128 + 128] = value
        width = 128 * len(pairs)
        grad = dot_rows(taps[:, 0:width], all_h[...].reshape(1024, 256)).astype(BF16)
        count = min(512, CONV_ROWS - 512 * part)
        for half in range(2):
            work[part, 32 * half : 32 * half + count // 16] = grad[
                0:count, 128 * half : 128 * half + 128
            ].reshape(count // 16, 16, 128)

    def spread(part, phase, triples):
        copies = []
        for d, (src, dst, device) in enumerate(triples):
            copy = remote(
                src, dst, sum_send.at[part, phase, d], sum_recv.at[part, phase, d], device
            )
            copy.start()
            copies.append(copy)
        return copies

    depth_way = (depth, peers_depth, dev_depth)
    plane_way = (plane, peers_plane, dev_plane)
    ways = [(depth_way, plane_way)] + [(plane_way, depth_way)] * (PARTS - 1)
    flying = {}

    def eight(index):
        return pl.ds(pl.multiple_of(index * 8, 8), 8)

    def advance(part, phase):
        (a, first, dev_first), (b, second, dev_second) = ways[part]
        if phase > 0:
            for copy in flying[part]:
                copy.wait()
        if phase == 0:
            triples = [
                (work.at[part, eight(first[d])], recv_first.at[part, d], dev_first[d])
                for d in range(7)
            ]
        if phase == 1:
            total = work[part, eight(a)].astype(F32)
            for d in range(7):
                total = total + recv_first[part, d].astype(F32)
            work_second[part] = total.astype(BF16)
            triples = [
                (work_second.at[part, second[d]], recv_second.at[part, d], dev_second[d])
                for d in range(7)
            ]
        if phase == 2:
            total = work_second[part, b].astype(F32)
            for d in range(7):
                total = total + recv_second[part, d].astype(F32)
            mine = a * 8 + b
            result[part, mine] = total.astype(BF16)
            triples = [
                (result.at[part, mine], result.at[part, mine], dev_second[d]) for d in range(7)
            ]
        if phase == 3:
            mine = eight(a)
            triples = [
                (result.at[part, mine], result.at[part, mine], dev_first[d]) for d in range(7)
            ]
        if phase < 4:
            flying[part] = spread(part, phase, triples)

    conv_grad(0)
    advance(0, 0)
    for copy in d_copies:
        copy.wait()
    dz1 = (all_dh1[...].reshape(256, 256).astype(F32) * silu_grad(z1_ref[...])).astype(BF16)
    for b in range(4):
        enc_buf[b] = dot_rows(dz1, snap_ref[:, b * 256 : b * 256 + 256])
    for d, p in enumerate(peers):
        for b in range(4):
            enc_out[d, b] = enc_buf[b, block(p)].astype(BF16)
    e_copies = exchange(6, [(enc_out.at[d], all_enc.at[d]) for d in range(3)])
    conv_grad(1)
    advance(1, 0)
    conv_grad(2)
    advance(2, 0)
    advance(0, 1)
    conv_grad(3)
    for copy in e_copies + g_copies:
        copy.wait()
    for b in range(4):
        total = enc_buf[b, block(grp)]
        for d in range(3):
            total = total + all_enc[d, b].astype(F32)
        total = total.astype(BF16)
        for half in range(2):
            place = 32 * half + 12 + 4 * b
            work[3, place : place + 4] = total[:, 128 * half : 128 * half + 128].reshape(4, 16, 128)
    total = head_buf[grp].astype(F32)
    for d in range(3):
        total = total + all_head[d].astype(F32)
    total = total.astype(BF16).reshape(4, 16, 128)
    for half in range(2):
        work[3, 32 * half + 28 : 32 * half + 30] = total[2 * half : 2 * half + 2]
        work[3, 32 * half + 30 : 32 * half + 32] = jnp.zeros((2, 16, 128), BF16)
    advance(3, 0)
    for part, phase in ORDER:
        advance(part, phase)


ORDER = [
    (1, 1), (0, 2), (2, 1), (3, 1), (1, 2), (0, 3), (2, 2), (3, 2),
    (1, 3), (2, 3), (3, 3), (0, 4), (1, 4), (2, 4), (3, 4),
]


def finish_kernel(result, vel_in, conv_ref, enc_ref, head_ref, vel_ref):
    vel_ref[...] = vel_in[...]
    for part in range(PARTS):
        count = min(512, CONV_ROWS - 512 * part)
        for half in range(2):
            lanes = slice(128 * half, 128 * half + 128)
            value = result[part, 32 * half : 32 * half + count // 16].astype(F32)
            conv_ref[512 * part : 512 * part + count, lanes] = value.reshape(count, 128)
    for half in range(2):
        for b in range(4):
            place = 32 * half + 12 + 4 * b
            value = result[3, place : place + 4].astype(F32).reshape(64, 128)
            enc_ref[:, 256 * b + 128 * half : 256 * b + 128 * half + 128] = value
        value = result[3, 32 * half + 28 : 32 * half + 30].astype(F32).reshape(32, 128)
        head_ref[32 * half : 32 * half + 32] = value


VM = pl.BlockSpec(memory_space=pltpu.VMEM)
HB = pl.BlockSpec(memory_space=pltpu.HBM)


def shaped(shape, dtype):
    return jax.ShapeDtypeStruct(shape, dtype)


def body(velocity, slot_of, w_encode, w_conv, w_head):
    tables = element_tables(NP)
    dma = pltpu.SemaphoreType.DMA
    vm = pltpu.VMEM
    inputs = (velocity[0, 0], slot_of[0], *tables, w_encode, w_conv, w_head)
    velocity_next, result = pl.pallas_call(
        lambda *refs: step_kernel(lax.axis_size("sim"), *refs),
        name="step",
        out_shape=(shaped((3, 256, 512), F32), shaped((PARTS, 64, 16, 128), BF16)),
        in_specs=[HB] * len(inputs),
        out_specs=(VM, VM),
        scratch_shapes=[
            vm((3, 256, 512), F32),
            vm((1, 256), jnp.int32),
            *[vm(table.shape, table.dtype) for table in tables],
            vm((1024, 256), BF16),
            vm((27, 256, 256), BF16),
            vm((256, 128), BF16),
            dma((len(inputs),)),
            vm((256, 256), F32),
            vm((2, 3, 256, 512), F32),
            vm((3, 256, 512), F32),
            vm((3, 256, 384), F32),
            vm((STEPS, 2, 3, 128, 128), BF16),
            vm((STEPS, 2, 3, 64, 128), BF16),
            vm((STEPS, 2, 3, 128, 128), BF16),
            vm((STEPS, 2, 3, 64, 128), BF16),
            dma((STEPS, 4)),
            dma((STEPS, 4)),
            vm((4, 64, 256), BF16),
            vm((256, 256), F32),
            vm((256, 1024), BF16),
            vm((4, 64, 128), BF16),
            vm((4, 64, 256), BF16),
            vm((4, 64, 128), BF16),
            vm((4, 4, 64, 256), BF16),
            vm((9, 288, 256), BF16),
            vm((2, 256, 128), BF16),
            vm((4, 256, 128), BF16),
            vm((9, 4, 288, 128), BF16),
            vm((9, 4, 288, 128), BF16),
            vm((1024, 512), BF16),
            vm((4, 64, 256), BF16),
            vm((4, 64, 256), BF16),
            vm((4, 256, 256), F32),
            vm((3, 4, 64, 256), BF16),
            vm((3, 4, 64, 256), BF16),
            vm((4, 64, 128), BF16),
            vm((3, 64, 128), BF16),
            dma((7, 3)),
            dma((7, 3)),
            vm((PARTS, 64, 16, 128), BF16),
            vm((PARTS, 7, 8, 16, 128), BF16),
            vm((PARTS, 8, 16, 128), BF16),
            vm((PARTS, 7, 16, 128), BF16),
            dma((PARTS, 4, 7)),
            dma((PARTS, 4, 7)),
        ],
        compiler_params=pltpu.CompilerParams(
            collective_id=0, has_side_effects=True, vmem_limit_bytes=56 * 2**20
        ),
    )(*inputs)
    conv, encode, head, velocity_next = pl.pallas_call(
        finish_kernel,
        name="finish",
        out_shape=(
            shaped((CONV_ROWS, 256), F32),
            shaped((64, 1024), F32),
            shaped((64, 128), F32),
            shaped((3, 256, 512), F32),
        ),
        in_specs=[VM, VM],
        out_specs=(VM, VM, VM, VM),
        compiler_params=pltpu.CompilerParams(vmem_limit_bytes=16 * 2**20),
    )(result, velocity_next)
    return (
        velocity_next[None, None],
        encode.T,
        conv.reshape(27, 64, 256).transpose(0, 2, 1),
        head,
    )


def solution(mesh):
    placed = (P("sim", "grp", None, None, None), P("sim", "grp", None), P(), P(), P())
    return jax.shard_map(
        body,
        mesh=mesh,
        in_specs=placed,
        out_specs=(
            P("sim", "grp", None, None, None),
            P(None, "grp"),
            P(None, None, "grp"),
            P("grp", None),
        ),
        check_vma=False,
    )
```

```python
import jax
import jax.numpy as jnp
import ml_dtypes
import numpy as np
from jax import lax
from jax.experimental import pallas as pl
from jax.experimental.pallas import tpu as pltpu
from jax.sharding import PartitionSpec as P

NP = 8
STEPS = 2
VISCOSITY = 0.2
TIME_STEP = 0.005
PENALTY = 100.0
LOSS_WEIGHT = 64.0

MESH = pl.DeviceIdType.MESH
F32 = jnp.float32
BF16 = jnp.bfloat16

CONV_ROWS = 1728
PARTS = 4


def derivative_matrix(count):
    places = np.arange(count)
    points = -np.cos(np.pi * places / (count - 1))
    weights = np.where(places % 2 == 0, 1.0, -1.0)
    weights[0] = weights[0] * 0.5
    weights[count - 1] = weights[count - 1] * 0.5
    identity = np.eye(count)
    spread = points[:, None] - points[None, :] + identity
    deriv = weights[None, :] / weights[:, None] / spread
    deriv = deriv * (1.0 - identity)
    return deriv - identity * deriv.sum(axis=1)[:, None]


def element_tables(count):
    deriv = derivative_matrix(count)
    single = np.eye(count)
    square = np.eye(count * count)
    along_x = np.kron(deriv, square)
    along_y = np.kron(single, np.kron(deriv, single))
    along_z = np.kron(square, deriv)
    laplace = along_x @ along_x + along_y @ along_y + along_z @ along_z
    grid = np.arange(count**3).reshape(count, count, count)
    final = count - 1
    chosen = np.concatenate(
        [
            grid[0].ravel(),
            grid[final].ravel(),
            grid[:, 0].ravel(),
            grid[:, final].ravel(),
            grid[:, :, 0].ravel(),
            grid[:, :, final].ravel(),
        ]
    )
    select = np.zeros((count**3, chosen.size))
    select[chosen, np.arange(chosen.size)] = 1.0
    bottom = np.zeros((count**3, 2 * count * count))
    for first in range(count):
        for middle in range(count):
            for inner in range(count):
                bottom[grid[first, middle, inner], first * count + inner] = (
                    VISCOSITY * deriv[0, middle]
                )
    diffuse = TIME_STEP * VISCOSITY * (laplace.T - PENALTY * (select @ select.T))
    half = count**3 // 2
    swapped = select.reshape(count**3, 3, 2, count * count)[:, :, ::-1].reshape(count**3, -1)
    small = lambda table: np.asarray(table, ml_dtypes.bfloat16)
    return (
        small(np.concatenate([TIME_STEP * along_x.T, diffuse], axis=1)),
        small(
            TIME_STEP
            * np.concatenate([along_y.T[:half, :half], along_z.T[:half, :half]], axis=1)
        ),
        small(select),
        small(swapped.T),
        np.asarray(bottom, np.float32),
    )


def dot(a, b):
    return lax.dot_general(a, b, (((1,), (0,)), ((), ())), preferred_element_type=F32)


def dot_rows(a, b):
    return lax.dot_general(a, b, (((0,), (0,)), ((), ())), preferred_element_type=F32)


def dot_cols(a, b):
    return lax.dot_general(a, b, (((1,), (1,)), ((), ())), preferred_element_type=F32)


def parts(value):
    high = value.astype(BF16)
    return high, (value - high.astype(F32)).astype(BF16)


def silu_grad(value):
    sigma = jax.nn.sigmoid(value)
    return sigma * (1.0 + value * (1.0 - sigma))


def lanes_low(shape):
    return lax.broadcasted_iota(jnp.int32, shape, len(shape) - 1) < 64


def remote(src, dst, send, recv, device):
    return pltpu.make_async_remote_copy(
        src_ref=src,
        dst_ref=dst,
        send_sem=send,
        recv_sem=recv,
        device_id=device,
        device_id_type=MESH,
    )


def variants(value, width):
    place = lax.broadcasted_iota(jnp.int32, (32, 8, width), 1)
    flat = value.reshape(32, 8, width)
    along_z = {
        -1: jnp.where(place == 0, 0.0, pltpu.roll(flat, 1, 1)),
        0: flat,
        1: jnp.where(place == 7, 0.0, pltpu.roll(flat, 7, 1)),
    }
    for dz in (-1, 0, 1):
        full = along_z[dz].reshape(16, 2, 8, width)
        none = jnp.zeros((16, 1, 8, width), F32)
        yield -1, dz, jnp.concatenate([none, full[:, :1]], axis=1).reshape(256, width)
        yield 0, dz, full.reshape(256, width)
        yield 1, dz, jnp.concatenate([full[:, 1:], none], axis=1).reshape(256, width)


def step_kernel(
    sims,
    vel_hbm,
    slot_hbm,
    wide_hbm,
    narrow_hbm,
    sel_hbm,
    unsel_hbm,
    bottom_hbm,
    enc_hbm,
    conv_hbm,
    head_hbm,
    out_hbm,
    result_hbm,
    result,
    vel_ref,
    slot_ref,
    wide_ref,
    narrow_ref,
    sel_ref,
    unsel_ref,
    bottom_ref,
    enc_ref,
    conv_ref,
    head_ref,
    load_sem,
    store_sem,
    perm,
    field,
    partial,
    faces,
    send_x,
    send_y,
    recv_x,
    recv_y,
    halo_send,
    halo_recv,
    h1_ref,
    snap_ref,
    target_ref,
    crop_h,
    crop_t,
    crop_s,
    all_h,
    shifted,
    dz2_buf,
    all_dz2,
    shifted_low,
    shifted_high,
    taps,
    enc_buf,
    enc_out,
    all_enc,
    head_buf,
    all_head,
    grp_send,
    grp_recv,
    work,
    recv_first,
    work_second,
    recv_second,
    sum_send,
    sum_recv,
):
    sim = lax.axis_index("sim")
    grp = lax.axis_index("grp")

    sources = [
        (slot_hbm, slot_ref),
        (vel_hbm.at[0], vel_ref.at[0]),
        (vel_hbm.at[1], vel_ref.at[1]),
        (vel_hbm.at[2], vel_ref.at[2]),
        (sel_hbm, sel_ref),
        (wide_hbm, wide_ref),
        (narrow_hbm, narrow_ref),
        (unsel_hbm, unsel_ref),
        (enc_hbm, enc_ref),
        (bottom_hbm, bottom_ref),
        (conv_hbm, conv_ref),
        (head_hbm, head_ref),
    ]
    loads = [
        pltpu.make_async_copy(src, dst, load_sem.at[k]) for k, (src, dst) in enumerate(sources)
    ]
    for copy in loads[:8]:
        copy.start()

    right = (lax.rem(sim + 1, sims), grp)
    left = (lax.rem(sim + sims - 1, sims), grp)
    above = (sim, lax.rem(grp + 1, 4))
    below = (sim, lax.rem(grp + 3, 4))
    peers = [lax.rem(grp + d, 4) for d in (1, 2, 3)]
    plane, depth = sim // 8, lax.rem(sim, 8)
    peers_plane = [lax.rem(plane + d, 8) for d in range(1, 8)]
    peers_depth = [lax.rem(depth + d, 8) for d in range(1, 8)]
    dev_plane = [(p * 8 + depth, grp) for p in peers_plane]
    dev_depth = [(plane * 8 + p, grp) for p in peers_depth]
    friends = [left, right] + [(sim, peer) for peer in peers] + dev_plane + dev_depth
    barrier = pltpu.get_barrier_semaphore()
    for device in friends:
        pl.semaphore_signal(barrier, inc=1, device_id=device, device_id_type=MESH)

    loads[0].wait()
    owner = lax.broadcasted_iota(jnp.int32, (256, 256), 0)
    by_slot = jnp.where(owner == slot_ref[...], 1.0, 0.0).astype(F32)
    by_place = by_slot.T
    for ix in range(2):
        for iy in range(4):
            for j in range(4):
                old = ix * 128 + iy * 32 + j * 8
                new = j * 64 + iy * 16 + ix * 8
                perm[new : new + 8] = by_place[old : old + 8]
    gather = perm[...].astype(BF16)
    for copy in loads[8:]:
        copy.start()
    for c in range(3):
        loads[1 + c].wait()
        high, low = parts(vel_ref[c])
        field[0, c] = dot(gather, high) + dot(gather, low)
    for copy in loads[4:8]:
        copy.wait()

    for step in range(STEPS):
        now, later = step % 2, (step + 1) % 2
        for c in range(3):
            faces[c] = dot(field[now, c].astype(BF16), sel_ref[...])
            along_x = faces[c, :, 0:128].reshape(16, 2, 8, 128)
            along_y = faces[c, :, 128:256].reshape(4, 4, 16, 128)
            send_x[step, 0, c] = along_x[:, 1].reshape(128, 128).astype(BF16)
            send_x[step, 1, c] = along_x[:, 0].reshape(128, 128).astype(BF16)
            send_y[step, 0, c] = along_y[:, 3].reshape(64, 128).astype(BF16)
            send_y[step, 1, c] = along_y[:, 0].reshape(64, 128).astype(BF16)
        if step == 0:
            pl.semaphore_wait(barrier, len(friends))
        copies = []
        for k, (src, dst, device) in enumerate(
            [
                (send_x.at[step, 0], recv_x.at[step, 0], right),
                (send_x.at[step, 1], recv_x.at[step, 1], left),
                (send_y.at[step, 0], recv_y.at[step, 0], above),
                (send_y.at[step, 1], recv_y.at[step, 1], below),
            ]
        ):
            copy = remote(src, dst, halo_send.at[step, k], halo_recv.at[step, k], device)
            copy.start()
            copies.append(copy)
        for c in range(3):
            for row in range(0, 256, 128):
                rows = slice(row, row + 128)
                mine = field[now, c, rows].astype(BF16)
                for h in range(0, 512, 256):
                    cols = slice(h, h + 256)
                    d_x = dot(mine, wide_ref[:, h : h + 256])
                    spread = dot(mine, wide_ref[:, 512 + h : 768 + h])
                    d_y = dot(mine[:, cols], narrow_ref[:, 0:256])
                    d_z = dot(mine[:, cols], narrow_ref[:, 256:512])
                    advect = field[now, 0, rows, cols] * d_x
                    advect = advect + field[now, 1, rows, cols] * d_y
                    advect = advect + field[now, 2, rows, cols] * d_z
                    partial[c, rows, cols] = field[now, c, rows, cols] + (spread - advect)
        for copy in copies:
            copy.wait()
        for c in range(3):
            along_x = faces[c, :, 0:128].reshape(16, 2, 8, 128)
            along_y = faces[c, :, 128:256].reshape(4, 4, 16, 128)
            along_z = faces[c, :, 256:384].reshape(4, 8, 8, 128)
            from_left = recv_x[step, 0, c].astype(F32).reshape(16, 1, 8, 128)
            from_right = recv_x[step, 1, c].astype(F32).reshape(16, 1, 8, 128)
            from_below = recv_y[step, 0, c].astype(F32).reshape(4, 1, 16, 128)
            from_above = recv_y[step, 1, c].astype(F32).reshape(4, 1, 16, 128)
            from_below = jnp.where(grp > 0, from_below, 0.0)
            from_above = jnp.where(grp < 3, from_above, 0.0)
            before = jnp.concatenate([from_left, along_x[:, :1]], axis=1).reshape(256, 128)
            after = jnp.concatenate([along_x[:, 1:], from_right], axis=1).reshape(256, 128)
            low = lanes_low((256, 128))
            beside_x = jnp.where(low, after, before).astype(BF16)
            before = jnp.concatenate([from_below, along_y[:, :3]], axis=1).reshape(256, 128)
            after = jnp.concatenate([along_y[:, 1:], from_above], axis=1).reshape(256, 128)
            beside_y = jnp.where(low, after, before).astype(BF16)
            place = lax.broadcasted_iota(jnp.int32, (32, 8, 128), 1)
            flat_z = along_z.reshape(32, 8, 128)
            behind = jnp.concatenate([along_z[3:], along_z[:3]], axis=0).reshape(32, 8, 128)
            ahead = jnp.concatenate([along_z[1:], along_z[:1]], axis=0).reshape(32, 8, 128)
            before = pltpu.roll(jnp.where(place == 7, behind, flat_z), 1, 1).reshape(256, 128)
            after = pltpu.roll(jnp.where(place == 0, ahead, flat_z), 7, 1).reshape(256, 128)
            beside_z = jnp.where(low, after, before).astype(BF16)
            beside = jnp.concatenate([beside_x, beside_y, beside_z], axis=1)
            for h in range(0, 512, 256):
                cols = slice(h, h + 256)
                pull = dot(beside, unsel_ref[:, cols])
                field[later, c, :, cols] = (
                    partial[c, :, cols] + (TIME_STEP * VISCOSITY * PENALTY) * pull
                )

    final = STEPS % 2
    snap_ref[:, :, 0:512] = field[final, 0].astype(BF16).reshape(4, 64, 512)
    snap_ref[:, :, 512:1024] = field[final, 2].astype(BF16).reshape(4, 64, 512)
    for copy in loads[8:10]:
        copy.wait()

    def block(index):
        return pl.ds(pl.multiple_of(index * 64, 64), 64)

    def exchange(kind, pairs):
        copies = []
        for d, (src, dst) in enumerate(pairs):
            copy = remote(src, dst, grp_send.at[kind, d], grp_recv.at[kind, d], (sim, peers[d]))
            copy.start()
            copies.append(copy)
        return copies

    z1 = dot(snap_ref[...].reshape(256, 1024), enc_ref[...])
    h1_ref[...] = (z1 * jax.nn.sigmoid(z1)).astype(BF16).reshape(4, 64, 256)
    h_copies = exchange(0, [(h1_ref.at[p], crop_h.at[grp]) for p in peers])
    table_high, table_low = parts(bottom_ref[...])
    stress = []
    for c in (0, 2):
        high, low = parts(field[final, c])
        stress.append(dot(high, table_high) + dot(high, table_low) + dot(low, table_high))
    side = pltpu.roll(stress[1], 64, 1)
    both = jnp.where(lanes_low((256, 128)), stress[0], side).astype(BF16)
    target_ref[...] = both.reshape(4, 64, 128)
    t_copies = exchange(1, [(target_ref.at[p], crop_t.at[grp]) for p in peers])
    s_copies = exchange(5, [(snap_ref.at[p], crop_s.at[grp]) for p in peers])
    mate = grp + 1 - 2 * lax.rem(grp, 2)
    across = lax.rem(grp + 2, 4)
    a_copies = []
    for d, p in enumerate((mate, across)):
        copy = remote(
            h1_ref, all_h.at[:, grp], grp_send.at[2, d], grp_recv.at[2, d], (sim, p)
        )
        copy.start()
        a_copies.append(copy)
    crop_h[grp] = h1_ref[grp]
    crop_t[grp] = target_ref[grp]
    crop_s[grp] = snap_ref[grp]
    all_h[:, grp] = h1_ref[...]
    for k in range(9):
        shifted[k, 0:16] = jnp.zeros((16, 256), BF16)
        shifted[k, 272:288] = jnp.zeros((16, 256), BF16)
        for j in range(4):
            shifted_low[k, j, 0:16] = jnp.zeros((16, 128), BF16)
            shifted_low[k, j, 272:288] = jnp.zeros((16, 128), BF16)
            shifted_high[k, j, 0:16] = jnp.zeros((16, 128), BF16)
            shifted_high[k, j, 272:288] = jnp.zeros((16, 128), BF16)
    scatter = perm[...].T.astype(BF16)
    for c in range(3):
        high, low = parts(field[final, c])
        vel_ref[c] = dot(scatter, high) + dot(scatter, low)
    stores = [pltpu.make_async_copy(vel_ref, out_hbm, store_sem.at[0])]
    stores[0].start()

    for copy in h_copies:
        copy.wait()
    for copy in loads[10:]:
        copy.wait()
    value = crop_h[...].reshape(256, 256).astype(F32)
    for dx, dz, moved in variants(value, 256):
        shifted[3 * (dx + 1) + dz + 1, 16:272] = moved.astype(BF16)
    sums = [jnp.zeros((256, 256), F32)] * 2
    for dx in (-1, 0, 1):
        for dy in (-1, 0, 1):
            for dz in (-1, 0, 1):
                tap = 9 * (dx + 1) + 3 * (dy + 1) + dz + 1
                start = 16 * (1 + dy)
                sums[tap % 2] = sums[tap % 2] + dot(
                    shifted[3 * (dx + 1) + dz + 1, start : start + 256], conv_ref[tap]
                )
    z2 = sums[0] + sums[1]
    a_copies[1].wait()
    relay = remote(
        all_h.at[:, across],
        all_h.at[:, across],
        grp_send.at[2, 2],
        grp_recv.at[2, 2],
        (sim, mate),
    )
    relay.start()
    a_copies = [a_copies[0], relay]
    h2 = (z2 * jax.nn.sigmoid(z2)).astype(BF16)
    output = dot(h2, head_ref[...])
    for copy in t_copies:
        copy.wait()
    target = crop_t[...].reshape(256, 128).astype(F32)
    resid = ((output - target) * (LOSS_WEIGHT / 65536.0)).astype(BF16)
    dz2 = (dot_cols(resid, head_ref[...]) * silu_grad(z2)).astype(BF16)
    dz2_buf[0] = dz2[:, 0:128]
    dz2_buf[1] = dz2[:, 128:256]
    all_dz2[grp] = dz2_buf[grp // 2]
    z_copies = exchange(3, [(dz2_buf.at[p // 2], all_dz2.at[grp]) for p in peers])
    head_buf[...] = dot_rows(h2, resid).astype(BF16).reshape(4, 64, 128)
    g_copies = exchange(4, [(head_buf.at[p], all_head.at[d]) for d, p in enumerate(peers)])

    for dx, dz, moved in variants(dz2.astype(F32), 256):
        shifted[3 * (dx + 1) + dz + 1, 16:272] = moved.astype(BF16)
    sums = [jnp.zeros((256, 256), F32)] * 2
    for dx in (-1, 0, 1):
        for dy in (-1, 0, 1):
            for dz in (-1, 0, 1):
                tap = 9 * (dx + 1) + 3 * (dy + 1) + dz + 1
                start = 16 * (1 - dy)
                sums[tap % 2] = sums[tap % 2] + dot_cols(
                    shifted[3 * (1 - dx) + 1 - dz, start : start + 256], conv_ref[tap]
                )
    for copy in s_copies:
        copy.wait()
    rows = crop_s[...].reshape(256, 1024)
    dz1 = ((sums[0] + sums[1]) * silu_grad(dot(rows, enc_ref[...]))).astype(BF16)
    for b in range(4):
        enc_buf[b] = dot_rows(dz1, rows[:, b * 256 : b * 256 + 256])
    for d, p in enumerate(peers):
        for b in range(4):
            enc_out[d, b] = enc_buf[b, block(p)].astype(BF16)
    e_copies = exchange(6, [(enc_out.at[d], all_enc.at[d]) for d in range(3)])

    for copy in z_copies:
        copy.wait()
    low = lanes_low((256, 128))
    for j in range(4):
        value = all_dz2[j].astype(F32)
        turned = pltpu.roll(value, 64, 1)
        first = lax.rem(grp, 2) == 0
        here = jnp.where(low, jnp.where(first, value, turned), jnp.where(first, turned, value))
        for dx, dz, moved in variants(here, 128):
            k = 3 * (dx + 1) + dz + 1
            shifted_low[k, j, 16:272] = jnp.where(low, moved, 0.0).astype(BF16)
            shifted_high[k, j, 16:272] = jnp.where(low, 0.0, moved).astype(BF16)
    for copy in a_copies:
        copy.wait()

    def tap_place(tap):
        dx, dy, dz = tap // 9 - 1, tap // 3 % 3 - 1, tap % 3 - 1
        return 3 * (1 - dx) + 1 - dz, 16 * (1 - dy)

    def conv_grad(part):
        pairs = range(4 * part, min(4 * part + 4, 14))
        for place, pair in enumerate(pairs):
            for j in range(4):
                k, start = tap_place(2 * pair)
                value = shifted_low[k, j, start : start + 256]
                if 2 * pair + 1 < 27:
                    k, start = tap_place(2 * pair + 1)
                    value = value + shifted_high[k, j, start : start + 256]
                taps[j * 256 : j * 256 + 256, place * 128 : place * 128 + 128] = value
        width = 128 * len(pairs)
        grad = dot_rows(taps[:, 0:width], all_h[...].reshape(1024, 256)).astype(BF16)
        count = min(512, CONV_ROWS - 512 * part)
        for half in range(2):
            work[part, 32 * half : 32 * half + count // 16] = grad[
                0:count, 128 * half : 128 * half + 128
            ].reshape(count // 16, 16, 128)

    def spread(part, phase, triples):
        copies = []
        for d, (src, dst, device) in enumerate(triples):
            copy = remote(
                src, dst, sum_send.at[part, phase, d], sum_recv.at[part, phase, d], device
            )
            copy.start()
            copies.append(copy)
        return copies

    depth_way = (depth, peers_depth, dev_depth)
    plane_way = (plane, peers_plane, dev_plane)
    ways = [(depth_way, plane_way)] + [(plane_way, depth_way)] * (PARTS - 1)
    flying = {}

    def eight(index):
        return pl.ds(pl.multiple_of(index * 8, 8), 8)

    def advance(part, phase):
        (a, first, dev_first), (b, second, dev_second) = ways[part]
        if phase > 0:
            for copy in flying[part]:
                copy.wait()
        if phase == 0:
            triples = [
                (work.at[part, eight(first[d])], recv_first.at[part, d], dev_first[d])
                for d in range(7)
            ]
        if phase == 1:
            total = work[part, eight(a)].astype(F32)
            for d in range(7):
                total = total + recv_first[part, d].astype(F32)
            work_second[part] = total.astype(BF16)
            triples = [
                (work_second.at[part, second[d]], recv_second.at[part, d], dev_second[d])
                for d in range(7)
            ]
        if phase == 2:
            total = work_second[part, b].astype(F32)
            for d in range(7):
                total = total + recv_second[part, d].astype(F32)
            mine = a * 8 + b
            result[part, mine] = total.astype(BF16)
            triples = [
                (result.at[part, mine], result.at[part, mine], dev_second[d]) for d in range(7)
            ]
        if phase == 3:
            mine = eight(a)
            triples = [
                (result.at[part, mine], result.at[part, mine], dev_first[d]) for d in range(7)
            ]
        if phase < 4:
            flying[part] = spread(part, phase, triples)
        else:
            copy = pltpu.make_async_copy(
                result.at[part], result_hbm.at[part], store_sem.at[1 + part]
            )
            copy.start()
            stores.append(copy)

    conv_grad(0)
    advance(0, 0)
    conv_grad(1)
    advance(1, 0)
    conv_grad(2)
    advance(2, 0)
    advance(0, 1)
    conv_grad(3)
    for copy in e_copies + g_copies:
        copy.wait()
    for b in range(4):
        total = enc_buf[b, block(grp)]
        for d in range(3):
            total = total + all_enc[d, b].astype(F32)
        total = total.astype(BF16)
        for half in range(2):
            place = 32 * half + 12 + 4 * b
            work[3, place : place + 4] = total[:, 128 * half : 128 * half + 128].reshape(4, 16, 128)
    total = head_buf[grp].astype(F32)
    for d in range(3):
        total = total + all_head[d].astype(F32)
    total = total.astype(BF16).reshape(4, 16, 128)
    for half in range(2):
        work[3, 32 * half + 28 : 32 * half + 30] = total[2 * half : 2 * half + 2]
        work[3, 32 * half + 30 : 32 * half + 32] = jnp.zeros((2, 16, 128), BF16)
    advance(3, 0)
    for part, phase in ORDER:
        advance(part, phase)
    for copy in stores:
        copy.wait()


ORDER = [
    (1, 1), (0, 2), (2, 1), (3, 1), (1, 2), (0, 3), (2, 2), (3, 2),
    (1, 3), (2, 3), (3, 3), (0, 4), (1, 4), (2, 4), (3, 4),
]


def finish_kernel(
    result_hbm,
    vel_in,
    conv_hbm,
    enc_hbm,
    head_hbm,
    vel_out,
    result,
    vel_ref,
    conv_ref,
    enc_ref,
    head_ref,
    load_sem,
    store_sem,
):
    loads = [
        pltpu.make_async_copy(result_hbm.at[part], result.at[part], load_sem.at[part])
        for part in range(PARTS)
    ]
    loads.append(pltpu.make_async_copy(vel_in, vel_ref, load_sem.at[PARTS]))
    for copy in loads:
        copy.start()
    stores = []

    def store(src, dst):
        copy = pltpu.make_async_copy(src, dst, store_sem.at[len(stores)])
        copy.start()
        stores.append(copy)

    for part in range(PARTS):
        loads[part].wait()
        count = min(512, CONV_ROWS - 512 * part)
        for half in range(2):
            lanes = slice(128 * half, 128 * half + 128)
            value = result[part, 32 * half : 32 * half + count // 16].astype(F32)
            conv_ref[512 * part : 512 * part + count, lanes] = value.reshape(count, 128)
        span = pl.ds(512 * part, count)
        store(conv_ref.at[span], conv_hbm.at[span])
    loads[PARTS].wait()
    store(vel_ref, vel_out)
    for half in range(2):
        for b in range(4):
            place = 32 * half + 12 + 4 * b
            value = result[3, place : place + 4].astype(F32).reshape(64, 128)
            enc_ref[:, 256 * b + 128 * half : 256 * b + 128 * half + 128] = value
        value = result[3, 32 * half + 28 : 32 * half + 30].astype(F32).reshape(32, 128)
        head_ref[32 * half : 32 * half + 32] = value
    store(enc_ref, enc_hbm)
    store(head_ref, head_hbm)
    for copy in stores:
        copy.wait()


VM = pl.BlockSpec(memory_space=pltpu.VMEM)
HB = pl.BlockSpec(memory_space=pltpu.HBM)


def shaped(shape, dtype):
    return jax.ShapeDtypeStruct(shape, dtype)


def body(velocity, slot_of, w_encode, w_conv, w_head):
    tables = element_tables(NP)
    dma = pltpu.SemaphoreType.DMA
    vm = pltpu.VMEM
    inputs = (velocity[0, 0], slot_of[0], *tables, w_encode, w_conv, w_head)
    velocity_next, result = pl.pallas_call(
        lambda *refs: step_kernel(lax.axis_size("sim"), *refs),
        name="step",
        out_shape=(shaped((3, 256, 512), F32), shaped((PARTS, 64, 16, 128), BF16)),
        in_specs=[HB] * len(inputs),
        out_specs=(HB, HB),
        scratch_shapes=[
            vm((PARTS, 64, 16, 128), BF16),
            vm((3, 256, 512), F32),
            vm((1, 256), jnp.int32),
            *[vm(table.shape, table.dtype) for table in tables],
            vm((1024, 256), BF16),
            vm((27, 256, 256), BF16),
            vm((256, 128), BF16),
            dma((len(inputs) + 2,)),
            dma((1 + PARTS,)),
            vm((256, 256), F32),
            vm((2, 3, 256, 512), F32),
            vm((3, 256, 512), F32),
            vm((3, 256, 384), F32),
            vm((STEPS, 2, 3, 128, 128), BF16),
            vm((STEPS, 2, 3, 64, 128), BF16),
            vm((STEPS, 2, 3, 128, 128), BF16),
            vm((STEPS, 2, 3, 64, 128), BF16),
            dma((STEPS, 4)),
            dma((STEPS, 4)),
            vm((4, 64, 256), BF16),
            vm((4, 64, 1024), BF16),
            vm((4, 64, 128), BF16),
            vm((4, 64, 256), BF16),
            vm((4, 64, 128), BF16),
            vm((4, 64, 1024), BF16),
            vm((4, 4, 64, 256), BF16),
            vm((9, 288, 256), BF16),
            vm((2, 256, 128), BF16),
            vm((4, 256, 128), BF16),
            vm((9, 4, 288, 128), BF16),
            vm((9, 4, 288, 128), BF16),
            vm((1024, 512), BF16),
            vm((4, 256, 256), F32),
            vm((3, 4, 64, 256), BF16),
            vm((3, 4, 64, 256), BF16),
            vm((4, 64, 128), BF16),
            vm((3, 64, 128), BF16),
            dma((7, 3)),
            dma((7, 3)),
            vm((PARTS, 64, 16, 128), BF16),
            vm((PARTS, 7, 8, 16, 128), BF16),
            vm((PARTS, 8, 16, 128), BF16),
            vm((PARTS, 7, 16, 128), BF16),
            dma((PARTS, 4, 7)),
            dma((PARTS, 4, 7)),
        ],
        compiler_params=pltpu.CompilerParams(
            collective_id=0, has_side_effects=True, vmem_limit_bytes=62 * 2**20
        ),
    )(*inputs)
    conv, encode, head, velocity_next = pl.pallas_call(
        finish_kernel,
        name="finish",
        out_shape=(
            shaped((CONV_ROWS, 256), F32),
            shaped((64, 1024), F32),
            shaped((64, 128), F32),
            shaped((3, 256, 512), F32),
        ),
        in_specs=[HB, HB],
        out_specs=(HB, HB, HB, HB),
        scratch_shapes=[
            vm((PARTS, 64, 16, 128), BF16),
            vm((3, 256, 512), F32),
            vm((CONV_ROWS, 256), F32),
            vm((64, 1024), F32),
            vm((64, 128), F32),
            dma((PARTS + 1,)),
            dma((PARTS + 3,)),
        ],
        compiler_params=pltpu.CompilerParams(vmem_limit_bytes=62 * 2**20),
    )(result, velocity_next)
    return (
        velocity_next[None, None],
        encode.T,
        conv.reshape(27, 64, 256).transpose(0, 2, 1),
        head,
    )


def solution(mesh):
    placed = (P("sim", "grp", None, None, None), P("sim", "grp", None), P(), P(), P())
    return jax.shard_map(
        body,
        mesh=mesh,
        in_specs=placed,
        out_specs=(
            P("sim", "grp", None, None, None),
            P(None, "grp"),
            P(None, None, "grp"),
            P("grp", None),
        ),
        check_vma=False,
    )
```

```python
import jax
import jax.numpy as jnp
import ml_dtypes
import numpy as np
from jax import lax
from jax.experimental import pallas as pl
from jax.experimental.pallas import tpu as pltpu
from jax.sharding import PartitionSpec as P

NP = 8
STEPS = 2
VISCOSITY = 0.2
TIME_STEP = 0.005
PENALTY = 100.0
LOSS_WEIGHT = 64.0

MESH = pl.DeviceIdType.MESH
F32 = jnp.float32
BF16 = jnp.bfloat16

CONV_ROWS = 1728
PARTS = 3


def derivative_matrix(count):
    places = np.arange(count)
    points = -np.cos(np.pi * places / (count - 1))
    weights = np.where(places % 2 == 0, 1.0, -1.0)
    weights[0] = weights[0] * 0.5
    weights[count - 1] = weights[count - 1] * 0.5
    identity = np.eye(count)
    spread = points[:, None] - points[None, :] + identity
    deriv = weights[None, :] / weights[:, None] / spread
    deriv = deriv * (1.0 - identity)
    return deriv - identity * deriv.sum(axis=1)[:, None]


def element_tables(count):
    deriv = derivative_matrix(count)
    single = np.eye(count)
    square = np.eye(count * count)
    along_x = np.kron(deriv, square)
    along_y = np.kron(single, np.kron(deriv, single))
    along_z = np.kron(square, deriv)
    laplace = along_x @ along_x + along_y @ along_y + along_z @ along_z
    grid = np.arange(count**3).reshape(count, count, count)
    final = count - 1
    chosen = np.concatenate(
        [
            grid[0].ravel(),
            grid[final].ravel(),
            grid[:, 0].ravel(),
            grid[:, final].ravel(),
            grid[:, :, 0].ravel(),
            grid[:, :, final].ravel(),
        ]
    )
    select = np.zeros((count**3, chosen.size))
    select[chosen, np.arange(chosen.size)] = 1.0
    bottom = np.zeros((count**3, 2 * count * count))
    for first in range(count):
        for middle in range(count):
            for inner in range(count):
                bottom[grid[first, middle, inner], first * count + inner] = (
                    VISCOSITY * deriv[0, middle]
                )
    diffuse = TIME_STEP * VISCOSITY * (laplace.T - PENALTY * (select @ select.T))
    half = count**3 // 2
    swapped = select.reshape(count**3, 3, 2, count * count)[:, :, ::-1].reshape(count**3, -1)
    small = lambda table: np.asarray(table, ml_dtypes.bfloat16)
    return (
        small(np.concatenate([TIME_STEP * along_x.T, diffuse], axis=1)),
        small(
            TIME_STEP
            * np.concatenate([along_y.T[:half, :half], along_z.T[:half, :half]], axis=1)
        ),
        small(select),
        small(swapped.T),
        np.asarray(bottom, np.float32),
    )


def dot(a, b):
    return lax.dot_general(a, b, (((1,), (0,)), ((), ())), preferred_element_type=F32)


def dot_rows(a, b):
    return lax.dot_general(a, b, (((0,), (0,)), ((), ())), preferred_element_type=F32)


def dot_cols(a, b):
    return lax.dot_general(a, b, (((1,), (1,)), ((), ())), preferred_element_type=F32)


def parts(value):
    high = value.astype(BF16)
    return high, (value - high.astype(F32)).astype(BF16)


def silu_grad(value):
    sigma = jax.nn.sigmoid(value)
    return sigma * (1.0 + value * (1.0 - sigma))


def lanes_low(shape):
    return lax.broadcasted_iota(jnp.int32, shape, len(shape) - 1) < 64


def remote(src, dst, send, recv, device):
    return pltpu.make_async_remote_copy(
        src_ref=src,
        dst_ref=dst,
        send_sem=send,
        recv_sem=recv,
        device_id=device,
        device_id_type=MESH,
    )


def variants(value, width):
    place = lax.broadcasted_iota(jnp.int32, (32, 8, width), 1)
    flat = value.reshape(32, 8, width)
    along_z = {
        -1: jnp.where(place == 0, 0.0, pltpu.roll(flat, 1, 1)),
        0: flat,
        1: jnp.where(place == 7, 0.0, pltpu.roll(flat, 7, 1)),
    }
    for dz in (-1, 0, 1):
        full = along_z[dz].reshape(16, 2, 8, width)
        none = jnp.zeros((16, 1, 8, width), F32)
        yield -1, dz, jnp.concatenate([none, full[:, :1]], axis=1).reshape(256, width)
        yield 0, dz, full.reshape(256, width)
        yield 1, dz, jnp.concatenate([full[:, 1:], none], axis=1).reshape(256, width)


def step_kernel(
    sims,
    vel_hbm,
    slot_hbm,
    wide_hbm,
    narrow_hbm,
    sel_hbm,
    unsel_hbm,
    bottom_hbm,
    enc_hbm,
    conv_hbm,
    head_hbm,
    out_hbm,
    result_hbm,
    small_hbm,
    enc_grad_hbm,
    result,
    vel_ref,
    slot_ref,
    wide_ref,
    narrow_ref,
    sel_ref,
    unsel_ref,
    bottom_ref,
    enc_ref,
    conv_ref,
    head_ref,
    load_sem,
    store_sem,
    perm,
    field,
    partial,
    faces,
    send_x,
    send_y,
    recv_x,
    recv_y,
    halo_send,
    halo_recv,
    h1_ref,
    z1_ref,
    snap_ref,
    target_ref,
    crop_h,
    crop_t,
    all_h,
    shifted,
    dz2_buf,
    all_dz2,
    shifted_low,
    shifted_high,
    taps,
    dh1_buf,
    all_dh1,
    enc_buf,
    enc_out,
    enc_in,
    head_buf,
    all_head,
    grp_send,
    grp_recv,
    work,
    recv_first,
    work_second,
    recv_second,
    sum_send,
    sum_recv,
    small,
    small_recv,
    small_piece,
    small_layers,
    small_ready,
    enc_half,
    enc_recv,
    enc_piece,
    enc_layers,
    enc_ready,
    tail_send,
    tail_recv,
):
    sim = lax.axis_index("sim")
    grp = lax.axis_index("grp")

    sources = [
        (slot_hbm, slot_ref),
        (vel_hbm.at[0], vel_ref.at[0]),
        (vel_hbm.at[1], vel_ref.at[1]),
        (vel_hbm.at[2], vel_ref.at[2]),
        (sel_hbm, sel_ref),
        (wide_hbm, wide_ref),
        (narrow_hbm, narrow_ref),
        (unsel_hbm, unsel_ref),
        (enc_hbm, enc_ref),
        (bottom_hbm, bottom_ref),
        (conv_hbm, conv_ref),
        (head_hbm, head_ref),
    ]
    loads = [
        pltpu.make_async_copy(src, dst, load_sem.at[k]) for k, (src, dst) in enumerate(sources)
    ]
    for copy in loads[:8]:
        copy.start()

    right = (lax.rem(sim + 1, sims), grp)
    left = (lax.rem(sim + sims - 1, sims), grp)
    above = (sim, lax.rem(grp + 1, 4))
    below = (sim, lax.rem(grp + 3, 4))
    peers = [lax.rem(grp + d, 4) for d in (1, 2, 3)]
    plane, depth = sim // 8, lax.rem(sim, 8)
    peers_plane = [lax.rem(plane + d, 8) for d in range(1, 8)]
    peers_depth = [lax.rem(depth + d, 8) for d in range(1, 8)]
    dev_plane = [(p * 8 + depth, grp) for p in peers_plane]
    dev_depth = [(plane * 8 + p, grp) for p in peers_depth]
    mate = grp + 1 - 2 * lax.rem(grp, 2)
    across = lax.rem(grp + 2, 4)
    wide_plane = [
        (lax.rem(plane + d, 8) * 8 + depth, across if turn else grp)
        for turn in (0, 1)
        for d in range(8)
    ][1:]
    friends = [left, right, (sim, mate), (sim, lax.rem(mate + 2, 4))] + wide_plane + dev_depth
    barrier = pltpu.get_barrier_semaphore()
    for device in friends:
        pl.semaphore_signal(barrier, inc=1, device_id=device, device_id_type=MESH)

    loads[0].wait()
    owner = lax.broadcasted_iota(jnp.int32, (256, 256), 0)
    by_slot = jnp.where(owner == slot_ref[...], 1.0, 0.0).astype(F32)
    by_place = by_slot.T
    for ix in range(2):
        for iy in range(4):
            for j in range(4):
                old = ix * 128 + iy * 32 + j * 8
                new = j * 64 + iy * 16 + ix * 8
                perm[new : new + 8] = by_place[old : old + 8]
    gather = perm[...].astype(BF16)
    for copy in loads[8:]:
        copy.start()
    for c in range(3):
        loads[1 + c].wait()
        high, low = parts(vel_ref[c])
        field[0, c] = dot(gather, high) + dot(gather, low)
    for copy in loads[4:8]:
        copy.wait()

    for step in range(STEPS):
        now, later = step % 2, (step + 1) % 2
        for c in range(3):
            faces[c] = dot(field[now, c].astype(BF16), sel_ref[...])
            along_x = faces[c, :, 0:128].reshape(16, 2, 8, 128)
            along_y = faces[c, :, 128:256].reshape(4, 4, 16, 128)
            send_x[step, 0, c] = along_x[:, 1].reshape(128, 128).astype(BF16)
            send_x[step, 1, c] = along_x[:, 0].reshape(128, 128).astype(BF16)
            send_y[step, 0, c] = along_y[:, 3].reshape(64, 128).astype(BF16)
            send_y[step, 1, c] = along_y[:, 0].reshape(64, 128).astype(BF16)
        if step == 0:
            pl.semaphore_wait(barrier, len(friends))
        copies = []
        for k, (src, dst, device) in enumerate(
            [
                (send_x.at[step, 0], recv_x.at[step, 0], right),
                (send_x.at[step, 1], recv_x.at[step, 1], left),
                (send_y.at[step, 0], recv_y.at[step, 0], above),
                (send_y.at[step, 1], recv_y.at[step, 1], below),
            ]
        ):
            copy = remote(src, dst, halo_send.at[step, k], halo_recv.at[step, k], device)
            copy.start()
            copies.append(copy)
        for c in range(3):
            for row in range(0, 256, 128):
                rows = slice(row, row + 128)
                mine = field[now, c, rows].astype(BF16)
                for h in range(0, 512, 256):
                    cols = slice(h, h + 256)
                    d_x = dot(mine, wide_ref[:, h : h + 256])
                    spread = dot(mine, wide_ref[:, 512 + h : 768 + h])
                    d_y = dot(mine[:, cols], narrow_ref[:, 0:256])
                    d_z = dot(mine[:, cols], narrow_ref[:, 256:512])
                    advect = field[now, 0, rows, cols] * d_x
                    advect = advect + field[now, 1, rows, cols] * d_y
                    advect = advect + field[now, 2, rows, cols] * d_z
                    partial[c, rows, cols] = field[now, c, rows, cols] + (spread - advect)
        for copy in copies:
            copy.wait()
        for c in range(3):
            along_x = faces[c, :, 0:128].reshape(16, 2, 8, 128)
            along_y = faces[c, :, 128:256].reshape(4, 4, 16, 128)
            along_z = faces[c, :, 256:384].reshape(4, 8, 8, 128)
            from_left = recv_x[step, 0, c].astype(F32).reshape(16, 1, 8, 128)
            from_right = recv_x[step, 1, c].astype(F32).reshape(16, 1, 8, 128)
            from_below = recv_y[step, 0, c].astype(F32).reshape(4, 1, 16, 128)
            from_above = recv_y[step, 1, c].astype(F32).reshape(4, 1, 16, 128)
            from_below = jnp.where(grp > 0, from_below, 0.0)
            from_above = jnp.where(grp < 3, from_above, 0.0)
            before = jnp.concatenate([from_left, along_x[:, :1]], axis=1).reshape(256, 128)
            after = jnp.concatenate([along_x[:, 1:], from_right], axis=1).reshape(256, 128)
            low = lanes_low((256, 128))
            beside_x = jnp.where(low, after, before).astype(BF16)
            before = jnp.concatenate([from_below, along_y[:, :3]], axis=1).reshape(256, 128)
            after = jnp.concatenate([along_y[:, 1:], from_above], axis=1).reshape(256, 128)
            beside_y = jnp.where(low, after, before).astype(BF16)
            place = lax.broadcasted_iota(jnp.int32, (32, 8, 128), 1)
            flat_z = along_z.reshape(32, 8, 128)
            behind = jnp.concatenate([along_z[3:], along_z[:3]], axis=0).reshape(32, 8, 128)
            ahead = jnp.concatenate([along_z[1:], along_z[:1]], axis=0).reshape(32, 8, 128)
            before = pltpu.roll(jnp.where(place == 7, behind, flat_z), 1, 1).reshape(256, 128)
            after = pltpu.roll(jnp.where(place == 0, ahead, flat_z), 7, 1).reshape(256, 128)
            beside_z = jnp.where(low, after, before).astype(BF16)
            beside = jnp.concatenate([beside_x, beside_y, beside_z], axis=1)
            for h in range(0, 512, 256):
                cols = slice(h, h + 256)
                pull = dot(beside, unsel_ref[:, cols])
                field[later, c, :, cols] = (
                    partial[c, :, cols] + (TIME_STEP * VISCOSITY * PENALTY) * pull
                )

    final = STEPS % 2
    snap_ref[:, 0:512] = field[final, 0].astype(BF16)
    snap_ref[:, 512:1024] = field[final, 2].astype(BF16)
    for copy in loads[8:10]:
        copy.wait()

    def block(index):
        return pl.ds(pl.multiple_of(index * 64, 64), 64)

    def exchange(kind, pairs):
        copies = []
        for d, (src, dst) in enumerate(pairs):
            copy = remote(src, dst, grp_send.at[kind, d], grp_recv.at[kind, d], (sim, peers[d]))
            copy.start()
            copies.append(copy)
        return copies

    z1 = dot(snap_ref[...], enc_ref[...])
    z1_ref[...] = z1
    h1_ref[...] = (z1 * jax.nn.sigmoid(z1)).astype(BF16).reshape(4, 64, 256)
    h_copies = exchange(0, [(h1_ref.at[p], crop_h.at[grp]) for p in peers])
    table_high, table_low = parts(bottom_ref[...])
    stress = []
    for c in (0, 2):
        high, low = parts(field[final, c])
        stress.append(dot(high, table_high) + dot(high, table_low) + dot(low, table_high))
    side = pltpu.roll(stress[1], 64, 1)
    both = jnp.where(lanes_low((256, 128)), stress[0], side).astype(BF16)
    target_ref[...] = both.reshape(4, 64, 128)
    t_copies = exchange(1, [(target_ref.at[p], crop_t.at[grp]) for p in peers])
    a_copies = []
    for d, p in enumerate((mate, across)):
        copy = remote(
            h1_ref, all_h.at[:, grp], grp_send.at[2, d], grp_recv.at[2, d], (sim, p)
        )
        copy.start()
        a_copies.append(copy)
    crop_h[grp] = h1_ref[grp]
    crop_t[grp] = target_ref[grp]
    all_h[:, grp] = h1_ref[...]
    for k in range(9):
        shifted[k, 0:16] = jnp.zeros((16, 256), BF16)
        shifted[k, 272:288] = jnp.zeros((16, 256), BF16)
        for j in range(4):
            shifted_low[k, j, 0:16] = jnp.zeros((16, 128), BF16)
            shifted_low[k, j, 272:288] = jnp.zeros((16, 128), BF16)
            shifted_high[k, j, 0:16] = jnp.zeros((16, 128), BF16)
            shifted_high[k, j, 272:288] = jnp.zeros((16, 128), BF16)
    scatter = perm[...].T.astype(BF16)
    for c in range(3):
        high, low = parts(field[final, c])
        vel_ref[c] = dot(scatter, high) + dot(scatter, low)
    stores = [pltpu.make_async_copy(vel_ref, out_hbm, store_sem.at[0])]
    stores[0].start()

    for copy in h_copies:
        copy.wait()
    for copy in loads[10:]:
        copy.wait()
    value = crop_h[...].reshape(256, 256).astype(F32)
    for dx, dz, moved in variants(value, 256):
        shifted[3 * (dx + 1) + dz + 1, 16:272] = moved.astype(BF16)
    sums = [jnp.zeros((256, 256), F32)] * 2
    for dx in (-1, 0, 1):
        for dy in (-1, 0, 1):
            for dz in (-1, 0, 1):
                tap = 9 * (dx + 1) + 3 * (dy + 1) + dz + 1
                start = 16 * (1 + dy)
                sums[tap % 2] = sums[tap % 2] + dot(
                    shifted[3 * (dx + 1) + dz + 1, start : start + 256], conv_ref[tap]
                )
    z2 = sums[0] + sums[1]
    a_copies[1].wait()
    relay = remote(
        all_h.at[:, across],
        all_h.at[:, across],
        grp_send.at[2, 2],
        grp_recv.at[2, 2],
        (sim, mate),
    )
    relay.start()
    a_copies = [a_copies[0], relay]
    h2 = (z2 * jax.nn.sigmoid(z2)).astype(BF16)
    output = dot(h2, head_ref[...])
    for copy in t_copies:
        copy.wait()
    target = crop_t[...].reshape(256, 128).astype(F32)
    resid = ((output - target) * (LOSS_WEIGHT / 65536.0)).astype(BF16)
    dz2 = (dot_cols(resid, head_ref[...]) * silu_grad(z2)).astype(BF16)
    low = lanes_low((128, 128))
    for j in range(4):
        lanes = slice(128 * (j // 2), 128 * (j // 2) + 128)
        upper, under = dz2[0:128, lanes].astype(F32), dz2[128:256, lanes].astype(F32)
        if j % 2 == 0:
            packed = jnp.where(low, upper, pltpu.roll(under, 64, 1))
        else:
            packed = jnp.where(low, pltpu.roll(upper, 64, 1), under)
        dz2_buf[j] = packed.astype(BF16)
    all_dz2[grp] = dz2_buf[grp]
    z_copies = exchange(3, [(dz2_buf.at[p], all_dz2.at[grp]) for p in peers])
    head_buf[...] = dot_rows(h2, resid).astype(BF16).reshape(4, 64, 128)
    g_copies = exchange(4, [(head_buf.at[p], all_head.at[d]) for d, p in enumerate(peers)])

    for dx, dz, moved in variants(dz2.astype(F32), 256):
        shifted[3 * (dx + 1) + dz + 1, 16:272] = moved.astype(BF16)
    sums = [jnp.zeros((256, 256), F32)] * 2
    for dx in (-1, 0, 1):
        for dy in (-1, 0, 1):
            for dz in (-1, 0, 1):
                tap = 9 * (dx + 1) + 3 * (dy + 1) + dz + 1
                start = 16 * (1 - dy)
                sums[tap % 2] = sums[tap % 2] + dot_cols(
                    shifted[3 * (1 - dx) + 1 - dz, start : start + 256], conv_ref[tap]
                )
    dh1_buf[...] = (sums[0] + sums[1]).astype(BF16).reshape(4, 64, 256)
    all_dh1[grp] = dh1_buf[grp]
    d_copies = exchange(5, [(dh1_buf.at[p], all_dh1.at[grp]) for p in peers])

    for copy in z_copies:
        copy.wait()
    for j in range(4):
        value = all_dz2[j].astype(F32)
        turned = pltpu.roll(value, 64, 1)
        here = jnp.concatenate(
            [jnp.where(low, value, turned), jnp.where(low, turned, value)], axis=0
        )
        for dx, dz, moved in variants(here, 128):
            k = 3 * (dx + 1) + dz + 1
            side = lanes_low((256, 128))
            shifted_low[k, j, 16:272] = jnp.where(side, moved, 0.0).astype(BF16)
            shifted_high[k, j, 16:272] = jnp.where(side, 0.0, moved).astype(BF16)
    for copy in a_copies:
        copy.wait()

    def tap_place(tap):
        dx, dy, dz = tap // 9 - 1, tap // 3 % 3 - 1, tap % 3 - 1
        return 3 * (1 - dx) + 1 - dz, 16 * (1 - dy)

    def conv_grad(part):
        pairs = range(4 * part, min(4 * part + 4, 14))
        for place, pair in enumerate(pairs):
            for j in range(4):
                k, start = tap_place(2 * pair)
                value = shifted_low[k, j, start : start + 256]
                if 2 * pair + 1 < 27:
                    k, start = tap_place(2 * pair + 1)
                    value = value + shifted_high[k, j, start : start + 256]
                taps[j * 256 : j * 256 + 256, place * 128 : place * 128 + 128] = value
        width = 128 * len(pairs)
        grad = dot_rows(taps[:, 0:width], all_h[...].reshape(1024, 256)).astype(BF16)
        if part == PARTS:
            for half in range(2):
                lanes = slice(128 * half, 128 * half + 128)
                small[half * 3 : half * 3 + 3] = grad[0:192, lanes].reshape(3, 4, 16, 128)
            return
        count = 512
        for half in range(2):
            work[part, 32 * half : 32 * half + count // 16] = grad[
                0:count, 128 * half : 128 * half + 128
            ].reshape(count // 16, 16, 128)

    def spread(part, phase, triples):
        copies = []
        for d, (src, dst, device) in enumerate(triples):
            copy = remote(
                src, dst, sum_send.at[part, phase, d], sum_recv.at[part, phase, d], device
            )
            copy.start()
            copies.append(copy)
        return copies

    depth_way = (depth, peers_depth, dev_depth)
    plane_way = (plane, peers_plane, dev_plane)
    ways = [(depth_way, plane_way)] + [(plane_way, depth_way)] * 2
    flying = {}

    def eight(index):
        return pl.ds(pl.multiple_of(index * 8, 8), 8)

    def advance(part, phase):
        (a, first, dev_first), (b, second, dev_second) = ways[part]
        if phase > 0:
            for copy in flying[part]:
                copy.wait()
        if phase == 0:
            triples = [
                (work.at[part, eight(first[d])], recv_first.at[part, d], dev_first[d])
                for d in range(7)
            ]
        if phase == 1:
            total = work[part, eight(a)].astype(F32)
            for d in range(7):
                total = total + recv_first[part, d].astype(F32)
            work_second[part] = total.astype(BF16)
            triples = [
                (work_second.at[part, second[d]], recv_second.at[part, d], dev_second[d])
                for d in range(7)
            ]
        if phase == 2:
            total = work_second[part, b].astype(F32)
            for d in range(7):
                total = total + recv_second[part, d].astype(F32)
            mine = a * 8 + b
            result[part, mine] = total.astype(BF16)
            triples = [
                (result.at[part, mine], result.at[part, mine], dev_second[d]) for d in range(7)
            ]
        if phase == 3:
            mine = eight(a)
            triples = [
                (result.at[part, mine], result.at[part, mine], dev_first[d]) for d in range(7)
            ]
        if phase < 4:
            flying[part] = spread(part, phase, triples)
        else:
            copy = pltpu.make_async_copy(
                result.at[part], result_hbm.at[part], store_sem.at[1 + part]
            )
            copy.start()
            stores.append(copy)

    tail = {}

    def settle(which, phase):
        piece, layers, ready = tails[which]
        if phase > 0:
            for copy in tail[which]:
                copy.wait()

        def spread_small(triples):
            copies = []
            for d, (src, dst, device) in enumerate(triples):
                copy = remote(
                    src,
                    dst,
                    tail_send.at[which, phase, d],
                    tail_recv.at[which, phase, d],
                    device,
                )
                copy.start()
                copies.append(copy)
            return copies

        if phase == 0:
            if which == 0:
                tail[which] = spread_small(
                    [
                        (small.at[peers_plane[d]], small_recv.at[d], dev_plane[d])
                        for d in range(7)
                    ]
                )
            else:
                triples = []
                for turn in (0, 1):
                    side = lax.rem(grp // 2 + turn, 2)
                    for d in range(8):
                        if turn or d:
                            triples.append(
                                (
                                    enc_half.at[side, lax.rem(plane + d, 8)],
                                    enc_recv.at[8 * turn + d - 1],
                                    wide_plane[8 * turn + d - 1],
                                )
                            )
                tail[which] = spread_small(triples)
        if phase == 1:
            if which == 0:
                total = small[plane].astype(F32)
                for d in range(7):
                    total = total + small_recv[d].astype(F32)
            else:
                total = enc_half[grp // 2, plane].astype(F32)
                for d in range(15):
                    total = total + enc_recv[d].astype(F32)
            piece[...] = total.astype(BF16)
            layers[depth] = piece[...]
            tail[which] = spread_small(
                [(piece, layers.at[depth], dev_depth[d]) for d in range(7)]
            )
        if phase == 2:
            total = layers[0].astype(F32)
            for d in range(1, 8):
                total = total + layers[d].astype(F32)
            ready[plane] = total.astype(BF16)
            tail[which] = spread_small(
                [(ready.at[plane], ready.at[plane], dev_plane[d]) for d in range(7)]
            )
        if phase == 3:
            copy = pltpu.make_async_copy(
                ready, (small_hbm, enc_grad_hbm)[which], store_sem.at[1 + PARTS + which]
            )
            copy.start()
            stores.append(copy)

    tails = (
        (small_piece, small_layers, small_ready),
        (enc_piece, enc_layers, enc_ready),
    )

    for part in range(PARTS):
        conv_grad(part)
        advance(part, 0)
    conv_grad(PARTS)
    for copy in g_copies:
        copy.wait()
    total = head_buf[grp].astype(F32)
    for d in range(3):
        total = total + all_head[d].astype(F32)
    small[6] = total.astype(BF16).reshape(4, 16, 128)
    small[7] = jnp.zeros((4, 16, 128), BF16)
    settle(0, 0)

    for copy in d_copies:
        copy.wait()
    dz1 = (all_dh1[...].reshape(256, 256).astype(F32) * silu_grad(z1_ref[...])).astype(BF16)
    for b in range(4):
        grad = dot_rows(dz1, snap_ref[:, b * 256 : b * 256 + 256])
        enc_buf[:, b] = grad.reshape(4, 64, 256)
    theirs = lax.rem(mate, 2)
    ours = lax.rem(grp, 2)
    for side in range(2):
        enc_out[side] = enc_buf[2 * side + theirs].astype(BF16)
    m_copy = remote(enc_out, enc_in, grp_send.at[6, 0], grp_recv.at[6, 0], (sim, mate))
    m_copy.start()
    m_copy.wait()
    for side in range(2):
        for b in range(4):
            total = enc_buf[2 * side + ours, b] + enc_in[side, b].astype(F32)
            for half in range(2):
                enc_half[side, 2 * b + half] = total[:, 128 * half : 128 * half + 128].astype(
                    BF16
                )
    settle(1, 0)
    for part, phase in ORDER:
        if part < PARTS:
            advance(part, phase)
        else:
            settle(part - PARTS, phase)
    for copy in stores:
        copy.wait()


ORDER = [
    (1, 1), (0, 1), (2, 1), (3, 1), (4, 1),
    (1, 2), (0, 2), (2, 2), (3, 2), (4, 2),
    (1, 3), (0, 3), (2, 3), (3, 3), (4, 3),
    (1, 4), (0, 4), (2, 4),
]


def finish_kernel(
    result_hbm,
    small_hbm,
    enc_grad_hbm,
    vel_in,
    conv_hbm,
    enc_hbm,
    head_hbm,
    vel_out,
    result,
    small,
    enc_grad,
    vel_ref,
    conv_ref,
    enc_ref,
    head_ref,
    load_sem,
    store_sem,
):
    pairs = [(result_hbm.at[part], result.at[part]) for part in range(PARTS)]
    pairs += [(small_hbm, small), (enc_grad_hbm, enc_grad), (vel_in, vel_ref)]
    loads = [
        pltpu.make_async_copy(src, dst, load_sem.at[k]) for k, (src, dst) in enumerate(pairs)
    ]
    for copy in loads:
        copy.start()
    stores = []

    def store(src, dst):
        copy = pltpu.make_async_copy(src, dst, store_sem.at[len(stores)])
        copy.start()
        stores.append(copy)

    for part in range(PARTS):
        loads[part].wait()
        for half in range(2):
            lanes = slice(128 * half, 128 * half + 128)
            value = result[part, 32 * half : 32 * half + 32].astype(F32)
            conv_ref[512 * part : 512 * part + 512, lanes] = value.reshape(512, 128)
        span = pl.ds(512 * part, 512)
        store(conv_ref.at[span], conv_hbm.at[span])
    loads[PARTS].wait()
    for half in range(2):
        lanes = slice(128 * half, 128 * half + 128)
        value = small[3 * half : 3 * half + 3].astype(F32).reshape(192, 128)
        conv_ref[512 * PARTS : CONV_ROWS, lanes] = value
    span = pl.ds(512 * PARTS, 192)
    store(conv_ref.at[span], conv_hbm.at[span])
    head_ref[...] = small[6].astype(F32).reshape(64, 128)
    store(head_ref, head_hbm)
    loads[PARTS + 1].wait()
    for b in range(8):
        enc_ref[:, 128 * b : 128 * b + 128] = enc_grad[b].astype(F32)
    store(enc_ref, enc_hbm)
    loads[PARTS + 2].wait()
    store(vel_ref, vel_out)
    for copy in stores:
        copy.wait()


VM = pl.BlockSpec(memory_space=pltpu.VMEM)
HB = pl.BlockSpec(memory_space=pltpu.HBM)


def shaped(shape, dtype):
    return jax.ShapeDtypeStruct(shape, dtype)


def body(velocity, slot_of, w_encode, w_conv, w_head):
    tables = element_tables(NP)
    dma = pltpu.SemaphoreType.DMA
    vm = pltpu.VMEM
    inputs = (velocity[0, 0], slot_of[0], *tables, w_encode, w_conv, w_head)
    velocity_next, result, small, enc_grad = pl.pallas_call(
        lambda *refs: step_kernel(lax.axis_size("sim"), *refs),
        name="step",
        out_shape=(
            shaped((3, 256, 512), F32),
            shaped((PARTS, 64, 16, 128), BF16),
            shaped((8, 4, 16, 128), BF16),
            shaped((8, 64, 128), BF16),
        ),
        in_specs=[HB] * len(inputs),
        out_specs=(HB,) * 4,
        scratch_shapes=[
            vm((PARTS, 64, 16, 128), BF16),
            vm((3, 256, 512), F32),
            vm((1, 256), jnp.int32),
            *[vm(table.shape, table.dtype) for table in tables],
            vm((1024, 256), BF16),
            vm((27, 256, 256), BF16),
            vm((256, 128), BF16),
            dma((len(inputs) + 2,)),
            dma((3 + PARTS,)),
            vm((256, 256), F32),
            vm((2, 3, 256, 512), F32),
            vm((3, 256, 512), F32),
            vm((3, 256, 384), F32),
            vm((STEPS, 2, 3, 128, 128), BF16),
            vm((STEPS, 2, 3, 64, 128), BF16),
            vm((STEPS, 2, 3, 128, 128), BF16),
            vm((STEPS, 2, 3, 64, 128), BF16),
            dma((STEPS, 4)),
            dma((STEPS, 4)),
            vm((4, 64, 256), BF16),
            vm((256, 256), F32),
            vm((256, 1024), BF16),
            vm((4, 64, 128), BF16),
            vm((4, 64, 256), BF16),
            vm((4, 64, 128), BF16),
            vm((4, 4, 64, 256), BF16),
            vm((9, 288, 256), BF16),
            vm((4, 128, 128), BF16),
            vm((4, 128, 128), BF16),
            vm((9, 4, 288, 128), BF16),
            vm((9, 4, 288, 128), BF16),
            vm((1024, 512), BF16),
            vm((4, 64, 256), BF16),
            vm((4, 64, 256), BF16),
            vm((4, 4, 64, 256), F32),
            vm((2, 4, 64, 256), BF16),
            vm((2, 4, 64, 256), BF16),
            vm((4, 64, 128), BF16),
            vm((3, 64, 128), BF16),
            dma((7, 3)),
            dma((7, 3)),
            vm((PARTS, 64, 16, 128), BF16),
            vm((PARTS, 7, 8, 16, 128), BF16),
            vm((PARTS, 8, 16, 128), BF16),
            vm((PARTS, 7, 16, 128), BF16),
            dma((PARTS, 4, 7)),
            dma((PARTS, 4, 7)),
            vm((8, 4, 16, 128), BF16),
            vm((7, 4, 16, 128), BF16),
            vm((4, 16, 128), BF16),
            vm((8, 4, 16, 128), BF16),
            vm((8, 4, 16, 128), BF16),
            vm((2, 8, 64, 128), BF16),
            vm((15, 64, 128), BF16),
            vm((64, 128), BF16),
            vm((8, 64, 128), BF16),
            vm((8, 64, 128), BF16),
            dma((2, 3, 15)),
            dma((2, 3, 15)),
        ],
        compiler_params=pltpu.CompilerParams(
            collective_id=0, has_side_effects=True, vmem_limit_bytes=62 * 2**20
        ),
    )(*inputs)
    conv, encode, head, velocity_next = pl.pallas_call(
        finish_kernel,
        name="finish",
        out_shape=(
            shaped((CONV_ROWS, 256), F32),
            shaped((64, 1024), F32),
            shaped((64, 128), F32),
            shaped((3, 256, 512), F32),
        ),
        in_specs=[HB] * 4,
        out_specs=(HB,) * 4,
        scratch_shapes=[
            vm((PARTS, 64, 16, 128), BF16),
            vm((8, 4, 16, 128), BF16),
            vm((8, 64, 128), BF16),
            vm((3, 256, 512), F32),
            vm((CONV_ROWS, 256), F32),
            vm((64, 1024), F32),
            vm((64, 128), F32),
            dma((PARTS + 3,)),
            dma((PARTS + 4,)),
        ],
        compiler_params=pltpu.CompilerParams(vmem_limit_bytes=62 * 2**20),
    )(result, small, enc_grad, velocity_next)
    return (
        velocity_next[None, None],
        encode.T,
        conv.reshape(27, 64, 256).transpose(0, 2, 1),
        head,
    )


def solution(mesh):
    placed = (P("sim", "grp", None, None, None), P("sim", "grp", None), P(), P(), P())
    return jax.shard_map(
        body,
        mesh=mesh,
        in_specs=placed,
        out_specs=(
            P("sim", "grp", None, None, None),
            P(None, "grp"),
            P(None, None, "grp"),
            P("grp", None),
        ),
        check_vma=False,
    )
```

```python
import jax
import jax.numpy as jnp
import ml_dtypes
import numpy as np
from jax import lax
from jax.experimental import pallas as pl
from jax.experimental.pallas import tpu as pltpu
from jax.sharding import PartitionSpec as P

NP = 8
STEPS = 2
VISCOSITY = 0.2
TIME_STEP = 0.005
PENALTY = 100.0
LOSS_WEIGHT = 64.0

MESH = pl.DeviceIdType.MESH
F32 = jnp.float32
BF16 = jnp.bfloat16

CONV_ROWS = 1728
PARTS = 3


def derivative_matrix(count):
    places = np.arange(count)
    points = -np.cos(np.pi * places / (count - 1))
    weights = np.where(places % 2 == 0, 1.0, -1.0)
    weights[0] = weights[0] * 0.5
    weights[count - 1] = weights[count - 1] * 0.5
    identity = np.eye(count)
    spread = points[:, None] - points[None, :] + identity
    deriv = weights[None, :] / weights[:, None] / spread
    deriv = deriv * (1.0 - identity)
    return deriv - identity * deriv.sum(axis=1)[:, None]


def element_tables(count):
    deriv = derivative_matrix(count)
    single = np.eye(count)
    square = np.eye(count * count)
    along_x = np.kron(deriv, square)
    along_y = np.kron(single, np.kron(deriv, single))
    along_z = np.kron(square, deriv)
    laplace = along_x @ along_x + along_y @ along_y + along_z @ along_z
    grid = np.arange(count**3).reshape(count, count, count)
    final = count - 1
    chosen = np.concatenate(
        [
            grid[0].ravel(),
            grid[final].ravel(),
            grid[:, 0].ravel(),
            grid[:, final].ravel(),
            grid[:, :, 0].ravel(),
            grid[:, :, final].ravel(),
        ]
    )
    select = np.zeros((count**3, chosen.size))
    select[chosen, np.arange(chosen.size)] = 1.0
    bottom = np.zeros((count**3, 2 * count * count))
    for first in range(count):
        for middle in range(count):
            for inner in range(count):
                bottom[grid[first, middle, inner], first * count + inner] = (
                    VISCOSITY * deriv[0, middle]
                )
    diffuse = TIME_STEP * VISCOSITY * (laplace.T - PENALTY * (select @ select.T))
    half = count**3 // 2
    small = lambda table: np.asarray(table, ml_dtypes.bfloat16)
    return (
        small(np.concatenate([TIME_STEP * along_x.T, diffuse], axis=1)),
        small(
            TIME_STEP
            * np.concatenate([along_y.T[:half, :half], along_z.T[:half, :half]], axis=1)
        ),
        small(select),
        np.asarray(bottom, np.float32),
    )


def dot(a, b):
    return lax.dot_general(a, b, (((1,), (0,)), ((), ())), preferred_element_type=F32)


def dot_rows(a, b):
    return lax.dot_general(a, b, (((0,), (0,)), ((), ())), preferred_element_type=F32)


def dot_cols(a, b):
    return lax.dot_general(a, b, (((1,), (1,)), ((), ())), preferred_element_type=F32)


def parts(value):
    high = value.astype(BF16)
    return high, (value - high.astype(F32)).astype(BF16)


def silu_grad(value):
    sigma = jax.nn.sigmoid(value)
    return sigma * (1.0 + value * (1.0 - sigma))


def lanes_low(shape):
    return lax.broadcasted_iota(jnp.int32, shape, len(shape) - 1) < 64


def packed_rows(value, high):
    half = value.shape[0] // 2
    turned = pltpu.roll(value[half:], 64, 1)
    low = lanes_low((half, 128))
    packed = jnp.where(low, turned, value[:half]) if high else jnp.where(low, value[:half], turned)
    return packed.astype(BF16)


def swap_halves(value):
    return pltpu.roll(value, 64, 1).astype(BF16)


def spread_rows(packed):
    value = packed.astype(F32)
    return jnp.concatenate([value, pltpu.roll(value, 64, 1)], axis=0)


def remote(src, dst, send, recv, device):
    return pltpu.make_async_remote_copy(
        src_ref=src,
        dst_ref=dst,
        send_sem=send,
        recv_sem=recv,
        device_id=device,
        device_id_type=MESH,
    )


def variants(value, width):
    place = lax.broadcasted_iota(jnp.int32, (32, 8, width), 1)
    flat = value.reshape(32, 8, width)
    along_z = {
        -1: jnp.where(place == 0, 0.0, pltpu.roll(flat, 1, 1)),
        0: flat,
        1: jnp.where(place == 7, 0.0, pltpu.roll(flat, 7, 1)),
    }
    for dz in (-1, 0, 1):
        full = along_z[dz].reshape(16, 2, 8, width)
        none = jnp.zeros((16, 1, 8, width), F32)
        yield -1, dz, jnp.concatenate([none, full[:, :1]], axis=1).reshape(256, width)
        yield 0, dz, full.reshape(256, width)
        yield 1, dz, jnp.concatenate([full[:, 1:], none], axis=1).reshape(256, width)


def step_kernel(
    sims,
    vel_hbm,
    slot_hbm,
    wide_hbm,
    narrow_hbm,
    sel_hbm,
    bottom_hbm,
    enc_hbm,
    conv_hbm,
    head_hbm,
    out_hbm,
    result_hbm,
    small_hbm,
    enc_grad_hbm,
    result,
    vel_ref,
    slot_ref,
    wide_ref,
    narrow_ref,
    sel_ref,
    bottom_ref,
    enc_ref,
    conv_ref,
    head_ref,
    load_sem,
    store_sem,
    perm,
    field,
    partial,
    faces,
    send_x,
    send_y,
    recv_x,
    recv_y,
    halo_send,
    halo_recv,
    h1_ref,
    z1_ref,
    snap_ref,
    target_ref,
    crop_h,
    crop_t,
    all_h,
    shifted,
    dz2_buf,
    all_dz2,
    shifted_low,
    shifted_high,
    taps,
    dh1_buf,
    all_dh1,
    enc_buf,
    enc_out,
    enc_in,
    head_buf,
    all_head,
    grp_send,
    grp_recv,
    work,
    recv_first,
    work_second,
    recv_second,
    sum_send,
    sum_recv,
    small,
    small_recv,
    small_piece,
    small_layers,
    small_ready,
    enc_half,
    enc_recv,
    enc_piece,
    enc_layers,
    enc_ready,
    tail_send,
    tail_recv,
):
    sim = lax.axis_index("sim")
    grp = lax.axis_index("grp")

    sources = [
        (slot_hbm, slot_ref),
        (vel_hbm.at[0], vel_ref.at[0]),
        (vel_hbm.at[1], vel_ref.at[1]),
        (vel_hbm.at[2], vel_ref.at[2]),
        (sel_hbm, sel_ref),
        (wide_hbm, wide_ref),
        (narrow_hbm, narrow_ref),
        (enc_hbm, enc_ref),
        (bottom_hbm, bottom_ref),
        (conv_hbm, conv_ref),
        (head_hbm, head_ref),
    ]
    loads = [
        pltpu.make_async_copy(src, dst, load_sem.at[k]) for k, (src, dst) in enumerate(sources)
    ]
    for copy in loads[:7]:
        copy.start()

    right = (lax.rem(sim + 1, sims), grp)
    left = (lax.rem(sim + sims - 1, sims), grp)
    above = (sim, lax.rem(grp + 1, 4))
    below = (sim, lax.rem(grp + 3, 4))
    peers = [lax.rem(grp + d, 4) for d in (1, 2, 3)]
    plane, depth = sim // 8, lax.rem(sim, 8)
    peers_plane = [lax.rem(plane + d, 8) for d in range(1, 8)]
    peers_depth = [lax.rem(depth + d, 8) for d in range(1, 8)]
    dev_plane = [(p * 8 + depth, grp) for p in peers_plane]
    dev_depth = [(plane * 8 + p, grp) for p in peers_depth]
    mate = grp + 1 - 2 * lax.rem(grp, 2)
    across = lax.rem(grp + 2, 4)
    wide_plane = [
        (lax.rem(plane + d, 8) * 8 + depth, across if turn else grp)
        for turn in (0, 1)
        for d in range(8)
    ][1:]
    friends = dev_depth + wide_plane + [left, right, (sim, lax.rem(mate + 2, 4)), (sim, mate)]
    barrier = pltpu.get_barrier_semaphore()
    for device in friends:
        pl.semaphore_signal(barrier, inc=1, device_id=device, device_id_type=MESH)

    loads[0].wait()
    owner = lax.broadcasted_iota(jnp.int32, (256, 256), 0)
    by_slot = jnp.where(owner == slot_ref[...], 1.0, 0.0).astype(F32)
    by_place = by_slot.T
    for ix in range(2):
        for iy in range(4):
            for j in range(4):
                old = ix * 128 + iy * 32 + j * 8
                new = j * 64 + iy * 16 + ix * 8
                perm[new : new + 8] = by_place[old : old + 8]
    gather = perm[...].astype(BF16)
    for copy in loads[7:]:
        copy.start()
    for c in range(3):
        loads[1 + c].wait()
        high, low = parts(vel_ref[c])
        field[0, c] = dot(gather, high) + dot(gather, low)
    loads[4].wait()
    flights = {}

    def emit(step, c):
        faces[c] = dot(field[step % 2, c].astype(BF16), sel_ref[...])
        along_x = faces[c, :, 0:128].reshape(16, 2, 8, 128)
        along_y = faces[c, :, 128:256].reshape(4, 4, 16, 128)
        send_x[step, 0, c] = packed_rows(along_x[:, 1].reshape(128, 128), True)
        send_x[step, 1, c] = packed_rows(along_x[:, 0].reshape(128, 128), False)
        send_y[step, 0, c] = packed_rows(along_y[:, 3].reshape(64, 128), True)
        send_y[step, 1, c] = packed_rows(along_y[:, 0].reshape(64, 128), False)
        if step == 0 and c == 0:
            pl.semaphore_wait(barrier, len(friends))
        copies = []
        for k, (src, dst, device) in enumerate(
            [
                (send_x.at[step, 0, c], recv_x.at[step, 0, c], right),
                (send_x.at[step, 1, c], recv_x.at[step, 1, c], left),
                (send_y.at[step, 0, c], recv_y.at[step, 0, c], above),
                (send_y.at[step, 1, c], recv_y.at[step, 1, c], below),
            ]
        ):
            copy = remote(
                src, dst, halo_send.at[step, c, k], halo_recv.at[step, c, k], device
            )
            copy.start()
            copies.append(copy)
        flights[step, c] = copies

    for c in range(3):
        emit(0, c)
    for copy in loads[5:7]:
        copy.wait()
    for step in range(STEPS):
        now, later = step % 2, (step + 1) % 2
        for c in range(3):
            for row in range(0, 256, 128):
                rows = slice(row, row + 128)
                mine = field[now, c, rows].astype(BF16)
                for h in range(0, 512, 256):
                    cols = slice(h, h + 256)
                    d_x = dot(mine, wide_ref[:, h : h + 256])
                    spread = dot(mine, wide_ref[:, 512 + h : 768 + h])
                    d_y = dot(mine[:, cols], narrow_ref[:, 0:256])
                    d_z = dot(mine[:, cols], narrow_ref[:, 256:512])
                    advect = field[now, 0, rows, cols] * d_x
                    advect = advect + field[now, 1, rows, cols] * d_y
                    advect = advect + field[now, 2, rows, cols] * d_z
                    partial[c, rows, cols] = field[now, c, rows, cols] + (spread - advect)
        for c in range(3):
            for copy in flights[step, c]:
                copy.wait()
            along_x = faces[c, :, 0:128].reshape(16, 2, 8, 128)
            along_y = faces[c, :, 128:256].reshape(4, 4, 16, 128)
            along_z = faces[c, :, 256:384].reshape(4, 8, 8, 128)
            from_left = spread_rows(recv_x[step, 0, c]).reshape(16, 1, 8, 128)
            from_right = spread_rows(recv_x[step, 1, c]).reshape(16, 1, 8, 128)
            from_below = spread_rows(recv_y[step, 0, c]).reshape(4, 1, 16, 128)
            from_above = spread_rows(recv_y[step, 1, c]).reshape(4, 1, 16, 128)
            from_below = jnp.where(grp > 0, from_below, 0.0)
            from_above = jnp.where(grp < 3, from_above, 0.0)
            before = jnp.concatenate([from_left, along_x[:, :1]], axis=1).reshape(256, 128)
            after = jnp.concatenate([along_x[:, 1:], from_right], axis=1).reshape(256, 128)
            low = lanes_low((256, 128))
            beside_x = swap_halves(jnp.where(low, after, before))
            before = jnp.concatenate([from_below, along_y[:, :3]], axis=1).reshape(256, 128)
            after = jnp.concatenate([along_y[:, 1:], from_above], axis=1).reshape(256, 128)
            beside_y = swap_halves(jnp.where(low, after, before))
            place = lax.broadcasted_iota(jnp.int32, (32, 8, 128), 1)
            flat_z = along_z.reshape(32, 8, 128)
            behind = jnp.concatenate([along_z[3:], along_z[:3]], axis=0).reshape(32, 8, 128)
            ahead = jnp.concatenate([along_z[1:], along_z[:1]], axis=0).reshape(32, 8, 128)
            before = pltpu.roll(jnp.where(place == 7, behind, flat_z), 1, 1).reshape(256, 128)
            after = pltpu.roll(jnp.where(place == 0, ahead, flat_z), 7, 1).reshape(256, 128)
            beside_z = swap_halves(jnp.where(low, after, before))
            beside = jnp.concatenate([beside_x, beside_y, beside_z], axis=1)
            for h in range(0, 512, 256):
                cols = slice(h, h + 256)
                pull = dot_cols(beside, sel_ref[cols])
                field[later, c, :, cols] = (
                    partial[c, :, cols] + (TIME_STEP * VISCOSITY * PENALTY) * pull
                )
            if step + 1 < STEPS:
                emit(step + 1, c)

    final = STEPS % 2
    snap_ref[:, 0:512] = field[final, 0].astype(BF16)
    snap_ref[:, 512:1024] = field[final, 2].astype(BF16)
    for copy in loads[7:9]:
        copy.wait()

    def block(index):
        return pl.ds(pl.multiple_of(index * 64, 64), 64)

    def exchange(kind, pairs):
        copies = []
        for d, (src, dst) in enumerate(pairs):
            copy = remote(src, dst, grp_send.at[kind, d], grp_recv.at[kind, d], (sim, peers[d]))
            copy.start()
            copies.append(copy)
        return copies

    z1 = dot(snap_ref[...], enc_ref[...])
    z1_ref[...] = z1
    h1_ref[...] = (z1 * jax.nn.sigmoid(z1)).astype(BF16).reshape(4, 64, 256)
    h_copies = exchange(0, [(h1_ref.at[p], crop_h.at[grp]) for p in peers])
    table_high, table_low = parts(bottom_ref[...])
    stress = []
    for c in (0, 2):
        high, low = parts(field[final, c])
        stress.append(dot(high, table_high) + dot(high, table_low) + dot(low, table_high))
    side = pltpu.roll(stress[1], 64, 1)
    both = jnp.where(lanes_low((256, 128)), stress[0], side).astype(BF16)
    target_ref[...] = both.reshape(4, 64, 128)
    t_copies = exchange(1, [(target_ref.at[p], crop_t.at[grp]) for p in peers])
    a_copies = []
    for d, p in enumerate((mate, across)):
        copy = remote(
            h1_ref, all_h.at[:, grp], grp_send.at[2, d], grp_recv.at[2, d], (sim, p)
        )
        copy.start()
        a_copies.append(copy)
    crop_h[grp] = h1_ref[grp]
    crop_t[grp] = target_ref[grp]
    all_h[:, grp] = h1_ref[...]
    for k in range(9):
        shifted[k, 0:16] = jnp.zeros((16, 256), BF16)
        shifted[k, 272:288] = jnp.zeros((16, 256), BF16)
        for j in range(4):
            shifted_low[k, j, 0:16] = jnp.zeros((16, 128), BF16)
            shifted_low[k, j, 272:288] = jnp.zeros((16, 128), BF16)
            shifted_high[k, j, 0:16] = jnp.zeros((16, 128), BF16)
            shifted_high[k, j, 272:288] = jnp.zeros((16, 128), BF16)
    scatter = perm[...].T.astype(BF16)
    for c in range(3):
        high, low = parts(field[final, c])
        vel_ref[c] = dot(scatter, high) + dot(scatter, low)
    stores = [pltpu.make_async_copy(vel_ref, out_hbm, store_sem.at[0])]
    stores[0].start()

    for copy in h_copies:
        copy.wait()
    for copy in loads[9:]:
        copy.wait()
    value = crop_h[...].reshape(256, 256).astype(F32)
    for dx, dz, moved in variants(value, 256):
        shifted[3 * (dx + 1) + dz + 1, 16:272] = moved.astype(BF16)
    sums = [jnp.zeros((256, 256), F32)] * 2
    for dx in (-1, 0, 1):
        for dy in (-1, 0, 1):
            for dz in (-1, 0, 1):
                tap = 9 * (dx + 1) + 3 * (dy + 1) + dz + 1
                start = 16 * (1 + dy)
                sums[tap % 2] = sums[tap % 2] + dot(
                    shifted[3 * (dx + 1) + dz + 1, start : start + 256], conv_ref[tap]
                )
    z2 = sums[0] + sums[1]
    a_copies[1].wait()
    relay = remote(
        all_h.at[:, across],
        all_h.at[:, across],
        grp_send.at[2, 2],
        grp_recv.at[2, 2],
        (sim, mate),
    )
    relay.start()
    a_copies = [a_copies[0], relay]
    h2 = (z2 * jax.nn.sigmoid(z2)).astype(BF16)
    output = dot(h2, head_ref[...])
    for copy in t_copies:
        copy.wait()
    target = crop_t[...].reshape(256, 128).astype(F32)
    resid = ((output - target) * (LOSS_WEIGHT / 65536.0)).astype(BF16)
    dz2 = (dot_cols(resid, head_ref[...]) * silu_grad(z2)).astype(BF16)
    low = lanes_low((128, 128))
    for j in range(4):
        lanes = slice(128 * (j // 2), 128 * (j // 2) + 128)
        upper, under = dz2[0:128, lanes].astype(F32), dz2[128:256, lanes].astype(F32)
        if j % 2 == 0:
            packed = jnp.where(low, upper, pltpu.roll(under, 64, 1))
        else:
            packed = jnp.where(low, pltpu.roll(upper, 64, 1), under)
        dz2_buf[j] = packed.astype(BF16)
    all_dz2[grp] = dz2_buf[grp]
    z_copies = exchange(3, [(dz2_buf.at[p], all_dz2.at[grp]) for p in peers])
    head_buf[...] = dot_rows(h2, resid).astype(BF16).reshape(4, 64, 128)
    g_copies = exchange(4, [(head_buf.at[p], all_head.at[d]) for d, p in enumerate(peers)])

    for dx, dz, moved in variants(dz2.astype(F32), 256):
        shifted[3 * (dx + 1) + dz + 1, 16:272] = moved.astype(BF16)
    sums = [jnp.zeros((256, 256), F32)] * 2
    for dx in (-1, 0, 1):
        for dy in (-1, 0, 1):
            for dz in (-1, 0, 1):
                tap = 9 * (dx + 1) + 3 * (dy + 1) + dz + 1
                start = 16 * (1 - dy)
                sums[tap % 2] = sums[tap % 2] + dot_cols(
                    shifted[3 * (1 - dx) + 1 - dz, start : start + 256], conv_ref[tap]
                )
    dh1_buf[...] = (sums[0] + sums[1]).astype(BF16).reshape(4, 64, 256)
    all_dh1[grp] = dh1_buf[grp]
    d_copies = exchange(5, [(dh1_buf.at[p], all_dh1.at[grp]) for p in peers])

    for copy in z_copies:
        copy.wait()
    for j in range(4):
        value = all_dz2[j].astype(F32)
        turned = pltpu.roll(value, 64, 1)
        here = jnp.concatenate(
            [jnp.where(low, value, turned), jnp.where(low, turned, value)], axis=0
        )
        for dx, dz, moved in variants(here, 128):
            k = 3 * (dx + 1) + dz + 1
            side = lanes_low((256, 128))
            shifted_low[k, j, 16:272] = jnp.where(side, moved, 0.0).astype(BF16)
            shifted_high[k, j, 16:272] = jnp.where(side, 0.0, moved).astype(BF16)
    for copy in a_copies:
        copy.wait()

    def tap_place(tap):
        dx, dy, dz = tap // 9 - 1, tap // 3 % 3 - 1, tap % 3 - 1
        return 3 * (1 - dx) + 1 - dz, 16 * (1 - dy)

    def conv_grad(part):
        pairs = range(4 * part, min(4 * part + 4, 14))
        for place, pair in enumerate(pairs):
            for j in range(4):
                k, start = tap_place(2 * pair)
                value = shifted_low[k, j, start : start + 256]
                if 2 * pair + 1 < 27:
                    k, start = tap_place(2 * pair + 1)
                    value = value + shifted_high[k, j, start : start + 256]
                taps[j * 256 : j * 256 + 256, place * 128 : place * 128 + 128] = value
        width = 128 * len(pairs)
        grad = dot_rows(taps[:, 0:width], all_h[...].reshape(1024, 256)).astype(BF16)
        if part == PARTS:
            for half in range(2):
                lanes = slice(128 * half, 128 * half + 128)
                small[half * 3 : half * 3 + 3] = grad[0:192, lanes].reshape(3, 4, 16, 128)
            return
        count = 512
        for half in range(2):
            work[part, 32 * half : 32 * half + count // 16] = grad[
                0:count, 128 * half : 128 * half + 128
            ].reshape(count // 16, 16, 128)

    def spread(part, phase, triples):
        copies = []
        for d, (src, dst, device) in enumerate(triples):
            copy = remote(
                src, dst, sum_send.at[part, phase, d], sum_recv.at[part, phase, d], device
            )
            copy.start()
            copies.append(copy)
        return copies

    depth_way = (depth, peers_depth, dev_depth)
    plane_way = (plane, peers_plane, dev_plane)
    ways = [(depth_way, plane_way)] + [(plane_way, depth_way)] * 2
    flying = {}

    def eight(index):
        return pl.ds(pl.multiple_of(index * 8, 8), 8)

    def advance(part, phase):
        (a, first, dev_first), (b, second, dev_second) = ways[part]
        if phase > 0:
            for copy in flying[part]:
                copy.wait()
        if phase == 0:
            triples = [
                (work.at[part, eight(first[d])], recv_first.at[part, d], dev_first[d])
                for d in range(7)
            ]
        if phase == 1:
            total = work[part, eight(a)].astype(F32)
            for d in range(7):
                total = total + recv_first[part, d].astype(F32)
            work_second[part] = total.astype(BF16)
            triples = [
                (work_second.at[part, second[d]], recv_second.at[part, d], dev_second[d])
                for d in range(7)
            ]
        if phase == 2:
            total = work_second[part, b].astype(F32)
            for d in range(7):
                total = total + recv_second[part, d].astype(F32)
            mine = a * 8 + b
            result[part, mine] = total.astype(BF16)
            triples = [
                (result.at[part, mine], result.at[part, mine], dev_second[d]) for d in range(7)
            ]
        if phase == 3:
            mine = eight(a)
            triples = [
                (result.at[part, mine], result.at[part, mine], dev_first[d]) for d in range(7)
            ]
        if phase < 4:
            flying[part] = spread(part, phase, triples)
        else:
            copy = pltpu.make_async_copy(
                result.at[part], result_hbm.at[part], store_sem.at[1 + part]
            )
            copy.start()
            stores.append(copy)

    tail = {}

    def settle(which, phase):
        piece, layers, ready = tails[which]
        if phase > 0:
            for copy in tail[which]:
                copy.wait()

        def spread_small(triples):
            copies = []
            for d, (src, dst, device) in enumerate(triples):
                copy = remote(
                    src,
                    dst,
                    tail_send.at[which, phase, d],
                    tail_recv.at[which, phase, d],
                    device,
                )
                copy.start()
                copies.append(copy)
            return copies

        if phase == 0:
            if which == 0:
                tail[which] = spread_small(
                    [
                        (small.at[peers_depth[d]], small_recv.at[d], dev_depth[d])
                        for d in range(7)
                    ]
                )
            else:
                triples = []
                for turn in (0, 1):
                    side = lax.rem(grp // 2 + turn, 2)
                    for d in range(8):
                        if turn or d:
                            triples.append(
                                (
                                    enc_half.at[side, lax.rem(plane + d, 8)],
                                    enc_recv.at[8 * turn + d - 1],
                                    wide_plane[8 * turn + d - 1],
                                )
                            )
                tail[which] = spread_small(triples)
        if phase == 1:
            if which == 0:
                total = small[depth].astype(F32)
                for d in range(7):
                    total = total + small_recv[d].astype(F32)
            else:
                total = enc_half[grp // 2, plane].astype(F32)
                for d in range(15):
                    total = total + enc_recv[d].astype(F32)
            piece[...] = total.astype(BF16)
            place, devices = later_way[which]
            layers[place] = piece[...]
            tail[which] = spread_small(
                [(piece, layers.at[place], devices[d]) for d in range(7)]
            )
        if phase == 2:
            total = layers[0].astype(F32)
            for d in range(1, 8):
                total = total + layers[d].astype(F32)
            place, devices = later_way[1 - which]
            ready[place] = total.astype(BF16)
            tail[which] = spread_small(
                [(ready.at[place], ready.at[place], devices[d]) for d in range(7)]
            )
        if phase == 3:
            copy = pltpu.make_async_copy(
                ready, (small_hbm, enc_grad_hbm)[which], store_sem.at[1 + PARTS + which]
            )
            copy.start()
            stores.append(copy)

    later_way = ((plane, dev_plane), (depth, dev_depth))
    tails = (
        (small_piece, small_layers, small_ready),
        (enc_piece, enc_layers, enc_ready),
    )

    for part in (1, 2, 0):
        conv_grad(part)
        advance(part, 0)
    conv_grad(PARTS)
    for copy in g_copies:
        copy.wait()
    total = head_buf[grp].astype(F32)
    for d in range(3):
        total = total + all_head[d].astype(F32)
    small[6] = total.astype(BF16).reshape(4, 16, 128)
    small[7] = jnp.zeros((4, 16, 128), BF16)
    settle(0, 0)

    for copy in d_copies:
        copy.wait()
    dz1 = (all_dh1[...].reshape(256, 256).astype(F32) * silu_grad(z1_ref[...])).astype(BF16)
    for b in range(4):
        grad = dot_rows(dz1, snap_ref[:, b * 256 : b * 256 + 256])
        enc_buf[:, b] = grad.reshape(4, 64, 256)
    theirs = lax.rem(mate, 2)
    ours = lax.rem(grp, 2)
    for side in range(2):
        enc_out[side] = enc_buf[2 * side + theirs].astype(BF16)
    m_copy = remote(enc_out, enc_in, grp_send.at[6, 0], grp_recv.at[6, 0], (sim, mate))
    m_copy.start()
    m_copy.wait()
    for side in range(2):
        for b in range(4):
            total = enc_buf[2 * side + ours, b] + enc_in[side, b].astype(F32)
            for half in range(2):
                enc_half[side, 2 * b + half] = total[:, 128 * half : 128 * half + 128].astype(
                    BF16
                )
    settle(1, 0)
    for part, phase in ORDER:
        if part < PARTS:
            advance(part, phase)
        else:
            settle(part - PARTS, phase)
    for copy in stores:
        copy.wait()


ORDER = [
    (1, 1), (3, 1), (2, 1), (0, 1), (4, 1),
    (1, 2), (3, 2), (0, 2), (2, 2), (4, 2),
    (1, 3), (0, 3), (2, 3), (4, 3), (3, 3),
    (1, 4), (0, 4), (2, 4),
]


def finish_kernel(
    result_hbm,
    small_hbm,
    enc_grad_hbm,
    vel_in,
    conv_hbm,
    enc_hbm,
    head_hbm,
    vel_out,
    result,
    small,
    enc_grad,
    vel_ref,
    conv_ref,
    enc_ref,
    head_ref,
    load_sem,
    store_sem,
):
    pairs = [(vel_in.at[c], vel_ref.at[c]) for c in range(3)]
    pairs += [(result_hbm.at[part], result.at[part]) for part in range(PARTS)]
    pairs += [(small_hbm, small), (enc_grad_hbm, enc_grad)]
    loads = [
        pltpu.make_async_copy(src, dst, load_sem.at[k]) for k, (src, dst) in enumerate(pairs)
    ]
    for copy in loads:
        copy.start()
    stores = []

    def store(src, dst):
        copy = pltpu.make_async_copy(src, dst, store_sem.at[len(stores)])
        copy.start()
        stores.append(copy)

    for c in range(3):
        loads[c].wait()
        store(vel_ref.at[c], vel_out.at[c])
    for part in range(PARTS):
        loads[3 + part].wait()
        for half in range(2):
            lanes = slice(128 * half, 128 * half + 128)
            value = result[part, 32 * half : 32 * half + 32].astype(F32)
            conv_ref[512 * part : 512 * part + 512, lanes] = value.reshape(512, 128)
        span = pl.ds(512 * part, 512)
        store(conv_ref.at[span], conv_hbm.at[span])
    loads[3 + PARTS].wait()
    for half in range(2):
        lanes = slice(128 * half, 128 * half + 128)
        value = small[3 * half : 3 * half + 3].astype(F32).reshape(192, 128)
        conv_ref[512 * PARTS : CONV_ROWS, lanes] = value
    span = pl.ds(512 * PARTS, 192)
    store(conv_ref.at[span], conv_hbm.at[span])
    head_ref[...] = small[6].astype(F32).reshape(64, 128)
    store(head_ref, head_hbm)
    loads[4 + PARTS].wait()
    for b in range(8):
        enc_ref[:, 128 * b : 128 * b + 128] = enc_grad[b].astype(F32)
    store(enc_ref, enc_hbm)
    for copy in stores:
        copy.wait()


VM = pl.BlockSpec(memory_space=pltpu.VMEM)
HB = pl.BlockSpec(memory_space=pltpu.HBM)


def shaped(shape, dtype):
    return jax.ShapeDtypeStruct(shape, dtype)


def body(velocity, slot_of, w_encode, w_conv, w_head):
    tables = element_tables(NP)
    dma = pltpu.SemaphoreType.DMA
    vm = pltpu.VMEM
    inputs = (velocity[0, 0], slot_of[0], *tables, w_encode, w_conv, w_head)
    velocity_next, result, small, enc_grad = pl.pallas_call(
        lambda *refs: step_kernel(lax.axis_size("sim"), *refs),
        name="step",
        out_shape=(
            shaped((3, 256, 512), F32),
            shaped((PARTS, 64, 16, 128), BF16),
            shaped((8, 4, 16, 128), BF16),
            shaped((8, 64, 128), BF16),
        ),
        in_specs=[HB] * len(inputs),
        out_specs=(HB,) * 4,
        scratch_shapes=[
            vm((PARTS, 64, 16, 128), BF16),
            vm((3, 256, 512), F32),
            vm((1, 256), jnp.int32),
            *[vm(table.shape, table.dtype) for table in tables],
            vm((1024, 256), BF16),
            vm((27, 256, 256), BF16),
            vm((256, 128), BF16),
            dma((len(inputs) + 2,)),
            dma((3 + PARTS,)),
            vm((256, 256), F32),
            vm((2, 3, 256, 512), F32),
            vm((3, 256, 512), F32),
            vm((3, 256, 384), F32),
            vm((STEPS, 2, 3, 64, 128), BF16),
            vm((STEPS, 2, 3, 32, 128), BF16),
            vm((STEPS, 2, 3, 64, 128), BF16),
            vm((STEPS, 2, 3, 32, 128), BF16),
            dma((STEPS, 3, 4)),
            dma((STEPS, 3, 4)),
            vm((4, 64, 256), BF16),
            vm((256, 256), F32),
            vm((256, 1024), BF16),
            vm((4, 64, 128), BF16),
            vm((4, 64, 256), BF16),
            vm((4, 64, 128), BF16),
            vm((4, 4, 64, 256), BF16),
            vm((9, 288, 256), BF16),
            vm((4, 128, 128), BF16),
            vm((4, 128, 128), BF16),
            vm((9, 4, 288, 128), BF16),
            vm((9, 4, 288, 128), BF16),
            vm((1024, 512), BF16),
            vm((4, 64, 256), BF16),
            vm((4, 64, 256), BF16),
            vm((4, 4, 64, 256), F32),
            vm((2, 4, 64, 256), BF16),
            vm((2, 4, 64, 256), BF16),
            vm((4, 64, 128), BF16),
            vm((3, 64, 128), BF16),
            dma((7, 3)),
            dma((7, 3)),
            vm((PARTS, 64, 16, 128), BF16),
            vm((PARTS, 7, 8, 16, 128), BF16),
            vm((PARTS, 8, 16, 128), BF16),
            vm((PARTS, 7, 16, 128), BF16),
            dma((PARTS, 4, 7)),
            dma((PARTS, 4, 7)),
            vm((8, 4, 16, 128), BF16),
            vm((7, 4, 16, 128), BF16),
            vm((4, 16, 128), BF16),
            vm((8, 4, 16, 128), BF16),
            vm((8, 4, 16, 128), BF16),
            vm((2, 8, 64, 128), BF16),
            vm((15, 64, 128), BF16),
            vm((64, 128), BF16),
            vm((8, 64, 128), BF16),
            vm((8, 64, 128), BF16),
            dma((2, 3, 15)),
            dma((2, 3, 15)),
        ],
        compiler_params=pltpu.CompilerParams(
            collective_id=0, has_side_effects=True, vmem_limit_bytes=62 * 2**20
        ),
    )(*inputs)
    conv, encode, head, velocity_next = pl.pallas_call(
        finish_kernel,
        name="finish",
        out_shape=(
            shaped((CONV_ROWS, 256), F32),
            shaped((64, 1024), F32),
            shaped((64, 128), F32),
            shaped((3, 256, 512), F32),
        ),
        in_specs=[HB] * 4,
        out_specs=(HB,) * 4,
        scratch_shapes=[
            vm((PARTS, 64, 16, 128), BF16),
            vm((8, 4, 16, 128), BF16),
            vm((8, 64, 128), BF16),
            vm((3, 256, 512), F32),
            vm((CONV_ROWS, 256), F32),
            vm((64, 1024), F32),
            vm((64, 128), F32),
            dma((PARTS + 5,)),
            dma((PARTS + 6,)),
        ],
        compiler_params=pltpu.CompilerParams(vmem_limit_bytes=62 * 2**20),
    )(result, small, enc_grad, velocity_next)
    return (
        velocity_next[None, None],
        encode.T,
        conv.reshape(27, 64, 256).transpose(0, 2, 1),
        head,
    )


def solution(mesh):
    placed = (P("sim", "grp", None, None, None), P("sim", "grp", None), P(), P(), P())
    return jax.shard_map(
        body,
        mesh=mesh,
        in_specs=placed,
        out_specs=(
            P("sim", "grp", None, None, None),
            P(None, "grp"),
            P(None, None, "grp"),
            P("grp", None),
        ),
        check_vma=False,
    )
```

```python
import jax
import jax.numpy as jnp
import ml_dtypes
import numpy as np
from jax import lax
from jax.experimental import pallas as pl
from jax.experimental.pallas import tpu as pltpu
from jax.sharding import PartitionSpec as P

NP = 8
STEPS = 2
VISCOSITY = 0.2
TIME_STEP = 0.005
PENALTY = 100.0
LOSS_WEIGHT = 64.0

MESH = pl.DeviceIdType.MESH
F32 = jnp.float32
BF16 = jnp.bfloat16

CONV_ROWS = 1728
PARTS = 3


def derivative_matrix(count):
    places = np.arange(count)
    points = -np.cos(np.pi * places / (count - 1))
    weights = np.where(places % 2 == 0, 1.0, -1.0)
    weights[0] = weights[0] * 0.5
    weights[count - 1] = weights[count - 1] * 0.5
    identity = np.eye(count)
    spread = points[:, None] - points[None, :] + identity
    deriv = weights[None, :] / weights[:, None] / spread
    deriv = deriv * (1.0 - identity)
    return deriv - identity * deriv.sum(axis=1)[:, None]


def element_tables(count):
    deriv = derivative_matrix(count)
    single = np.eye(count)
    square = np.eye(count * count)
    along_x = np.kron(deriv, square)
    along_y = np.kron(single, np.kron(deriv, single))
    along_z = np.kron(square, deriv)
    laplace = along_x @ along_x + along_y @ along_y + along_z @ along_z
    grid = np.arange(count**3).reshape(count, count, count)
    final = count - 1
    chosen = np.concatenate(
        [
            grid[0].ravel(),
            grid[final].ravel(),
            grid[:, 0].ravel(),
            grid[:, final].ravel(),
            grid[:, :, 0].ravel(),
            grid[:, :, final].ravel(),
        ]
    )
    select = np.zeros((count**3, chosen.size))
    select[chosen, np.arange(chosen.size)] = 1.0
    bottom = np.zeros((count**3, 2 * count * count))
    for first in range(count):
        for middle in range(count):
            for inner in range(count):
                bottom[grid[first, middle, inner], first * count + inner] = (
                    VISCOSITY * deriv[0, middle]
                )
    diffuse = TIME_STEP * VISCOSITY * (laplace.T - PENALTY * (select @ select.T))
    half = count**3 // 2
    small = lambda table: np.asarray(table, ml_dtypes.bfloat16)
    return (
        small(np.concatenate([TIME_STEP * along_x.T, diffuse], axis=1)),
        small(
            TIME_STEP
            * np.concatenate([along_y.T[:half, :half], along_z.T[:half, :half]], axis=1)
        ),
        small(select),
        np.asarray(bottom, np.float32),
    )


def dot(a, b):
    return lax.dot_general(a, b, (((1,), (0,)), ((), ())), preferred_element_type=F32)


def dot_rows(a, b):
    return lax.dot_general(a, b, (((0,), (0,)), ((), ())), preferred_element_type=F32)


def dot_cols(a, b):
    return lax.dot_general(a, b, (((1,), (1,)), ((), ())), preferred_element_type=F32)


def parts(value):
    high = value.astype(BF16)
    return high, (value - high.astype(F32)).astype(BF16)


def silu_grad(value):
    sigma = jax.nn.sigmoid(value)
    return sigma * (1.0 + value * (1.0 - sigma))


def lanes_low(shape):
    return lax.broadcasted_iota(jnp.int32, shape, len(shape) - 1) < 64


def packed_rows(value, high):
    half = value.shape[0] // 2
    turned = pltpu.roll(value[half:], 64, 1)
    low = lanes_low((half, 128))
    packed = jnp.where(low, turned, value[:half]) if high else jnp.where(low, value[:half], turned)
    return packed.astype(BF16)


def swap_halves(value):
    return pltpu.roll(value, 64, 1).astype(BF16)


def spread_rows(packed):
    value = packed.astype(F32)
    return jnp.concatenate([value, pltpu.roll(value, 64, 1)], axis=0)


def remote(src, dst, send, recv, device):
    return pltpu.make_async_remote_copy(
        src_ref=src,
        dst_ref=dst,
        send_sem=send,
        recv_sem=recv,
        device_id=device,
        device_id_type=MESH,
    )


def variants(value, width):
    place = lax.broadcasted_iota(jnp.int32, (32, 8, width), 1)
    flat = value.reshape(32, 8, width)
    along_z = {
        -1: jnp.where(place == 0, 0.0, pltpu.roll(flat, 1, 1)),
        0: flat,
        1: jnp.where(place == 7, 0.0, pltpu.roll(flat, 7, 1)),
    }
    for dz in (-1, 0, 1):
        full = along_z[dz].reshape(16, 2, 8, width)
        none = jnp.zeros((16, 1, 8, width), F32)
        yield -1, dz, jnp.concatenate([none, full[:, :1]], axis=1).reshape(256, width)
        yield 0, dz, full.reshape(256, width)
        yield 1, dz, jnp.concatenate([full[:, 1:], none], axis=1).reshape(256, width)


def step_kernel(
    sims,
    vel_hbm,
    slot_hbm,
    wide_hbm,
    narrow_hbm,
    sel_hbm,
    bottom_hbm,
    enc_hbm,
    conv_hbm,
    head_hbm,
    out_hbm,
    result_hbm,
    small_hbm,
    enc_grad_hbm,
    result,
    vel_ref,
    slot_ref,
    wide_ref,
    narrow_ref,
    sel_ref,
    bottom_ref,
    enc_ref,
    conv_ref,
    head_ref,
    load_sem,
    store_sem,
    perm,
    field,
    partial,
    faces,
    send_x,
    send_y,
    recv_x,
    recv_y,
    halo_send,
    halo_recv,
    h1_ref,
    z1_ref,
    snap_ref,
    target_ref,
    crop_h,
    crop_t,
    all_h,
    shifted,
    dz2_buf,
    all_dz2,
    shifted_low,
    shifted_high,
    taps,
    dh1_buf,
    all_dh1,
    enc_buf,
    enc_out,
    enc_in,
    head_buf,
    all_head,
    grp_send,
    grp_recv,
    work,
    recv_first,
    work_second,
    recv_second,
    sum_send,
    sum_recv,
    small,
    small_recv,
    small_piece,
    small_layers,
    small_ready,
    enc_half,
    enc_recv,
    enc_piece,
    enc_layers,
    enc_ready,
    tail_send,
    tail_recv,
):
    sim = lax.axis_index("sim")
    grp = lax.axis_index("grp")

    sources = [
        (slot_hbm, slot_ref),
        (vel_hbm.at[0], vel_ref.at[0]),
        (vel_hbm.at[1], vel_ref.at[1]),
        (vel_hbm.at[2], vel_ref.at[2]),
        (sel_hbm, sel_ref),
        (wide_hbm, wide_ref),
        (narrow_hbm, narrow_ref),
        (enc_hbm, enc_ref),
        (bottom_hbm, bottom_ref),
        (conv_hbm, conv_ref),
        (head_hbm, head_ref),
    ]
    loads = [
        pltpu.make_async_copy(src, dst, load_sem.at[k]) for k, (src, dst) in enumerate(sources)
    ]
    for copy in loads[:7]:
        copy.start()

    right = (lax.rem(sim + 1, sims), grp)
    left = (lax.rem(sim + sims - 1, sims), grp)
    above = (sim, lax.rem(grp + 1, 4))
    below = (sim, lax.rem(grp + 3, 4))
    peers = [lax.rem(grp + d, 4) for d in (1, 2, 3)]
    plane, depth = sim // 8, lax.rem(sim, 8)
    peers_plane = [lax.rem(plane + d, 8) for d in range(1, 8)]
    peers_depth = [lax.rem(depth + d, 8) for d in range(1, 8)]
    dev_plane = [(p * 8 + depth, grp) for p in peers_plane]
    dev_depth = [(plane * 8 + p, grp) for p in peers_depth]
    mate = grp + 1 - 2 * lax.rem(grp, 2)
    across = lax.rem(grp + 2, 4)
    wide_plane = [
        (lax.rem(plane + d, 8) * 8 + depth, across if turn else grp)
        for turn in (0, 1)
        for d in range(8)
    ][1:]
    friends = dev_depth + wide_plane + [left, right, (sim, lax.rem(mate + 2, 4)), (sim, mate)]
    barrier = pltpu.get_barrier_semaphore()
    for device in friends:
        pl.semaphore_signal(barrier, inc=1, device_id=device, device_id_type=MESH)

    loads[0].wait()
    owner = lax.broadcasted_iota(jnp.int32, (256, 256), 0)
    by_slot = jnp.where(owner == slot_ref[...], 1.0, 0.0).astype(F32)
    by_place = by_slot.T
    for ix in range(2):
        for iy in range(4):
            for j in range(4):
                old = ix * 128 + iy * 32 + j * 8
                new = j * 64 + iy * 16 + ix * 8
                perm[new : new + 8] = by_place[old : old + 8]
    gather = perm[...].astype(BF16)
    for copy in loads[7:]:
        copy.start()
    for c in range(3):
        loads[1 + c].wait()
        high, low = parts(vel_ref[c])
        field[0, c] = dot(gather, high) + dot(gather, low)
    loads[4].wait()
    flights = {}

    def emit(step, c):
        faces[c] = dot(field[step % 2, c].astype(BF16), sel_ref[...])
        along_x = faces[c, :, 0:128].reshape(16, 2, 8, 128)
        along_y = faces[c, :, 128:256].reshape(4, 4, 16, 128)
        send_x[step, 0, c] = packed_rows(along_x[:, 1].reshape(128, 128), True)
        send_x[step, 1, c] = packed_rows(along_x[:, 0].reshape(128, 128), False)
        send_y[step, 0, c] = packed_rows(along_y[:, 3].reshape(64, 128), True)
        send_y[step, 1, c] = packed_rows(along_y[:, 0].reshape(64, 128), False)
        if step == 0 and c == 0:
            pl.semaphore_wait(barrier, len(friends))
        copies = []
        for k, (src, dst, device) in enumerate(
            [
                (send_x.at[step, 0, c], recv_x.at[step, 0, c], right),
                (send_x.at[step, 1, c], recv_x.at[step, 1, c], left),
                (send_y.at[step, 0, c], recv_y.at[step, 0, c], above),
                (send_y.at[step, 1, c], recv_y.at[step, 1, c], below),
            ]
        ):
            copy = remote(
                src, dst, halo_send.at[step, c, k], halo_recv.at[step, c, k], device
            )
            copy.start()
            copies.append(copy)
        flights[step, c] = copies

    def close(step, c):
        now, later = step % 2, (step + 1) % 2
        for copy in flights[step, c]:
            copy.wait()
        along_x = faces[c, :, 0:128].reshape(16, 2, 8, 128)
        along_y = faces[c, :, 128:256].reshape(4, 4, 16, 128)
        along_z = faces[c, :, 256:384].reshape(4, 8, 8, 128)
        from_left = spread_rows(recv_x[step, 0, c]).reshape(16, 1, 8, 128)
        from_right = spread_rows(recv_x[step, 1, c]).reshape(16, 1, 8, 128)
        from_below = spread_rows(recv_y[step, 0, c]).reshape(4, 1, 16, 128)
        from_above = spread_rows(recv_y[step, 1, c]).reshape(4, 1, 16, 128)
        from_below = jnp.where(grp > 0, from_below, 0.0)
        from_above = jnp.where(grp < 3, from_above, 0.0)
        before = jnp.concatenate([from_left, along_x[:, :1]], axis=1).reshape(256, 128)
        after = jnp.concatenate([along_x[:, 1:], from_right], axis=1).reshape(256, 128)
        low = lanes_low((256, 128))
        beside_x = swap_halves(jnp.where(low, after, before))
        before = jnp.concatenate([from_below, along_y[:, :3]], axis=1).reshape(256, 128)
        after = jnp.concatenate([along_y[:, 1:], from_above], axis=1).reshape(256, 128)
        beside_y = swap_halves(jnp.where(low, after, before))
        place = lax.broadcasted_iota(jnp.int32, (32, 8, 128), 1)
        flat_z = along_z.reshape(32, 8, 128)
        behind = jnp.concatenate([along_z[3:], along_z[:3]], axis=0).reshape(32, 8, 128)
        ahead = jnp.concatenate([along_z[1:], along_z[:1]], axis=0).reshape(32, 8, 128)
        before = pltpu.roll(jnp.where(place == 7, behind, flat_z), 1, 1).reshape(256, 128)
        after = pltpu.roll(jnp.where(place == 0, ahead, flat_z), 7, 1).reshape(256, 128)
        beside_z = swap_halves(jnp.where(low, after, before))
        beside = jnp.concatenate([beside_x, beside_y, beside_z], axis=1)
        for h in range(0, 512, 256):
            cols = slice(h, h + 256)
            pull = dot_cols(beside, sel_ref[cols])
            field[later, c, :, cols] = (
                partial[c, :, cols] + (TIME_STEP * VISCOSITY * PENALTY) * pull
            )
        if step + 1 < STEPS:
            emit(step + 1, c)

    for c in range(3):
        emit(0, c)
    for copy in loads[5:7]:
        copy.wait()
    for step in range(STEPS):
        now, later = step % 2, (step + 1) % 2
        for c in range(3):
            for row in range(0, 256, 128):
                rows = slice(row, row + 128)
                mine = field[now, c, rows].astype(BF16)
                for h in range(0, 512, 256):
                    cols = slice(h, h + 256)
                    d_x = dot(mine, wide_ref[:, h : h + 256])
                    spread = dot(mine, wide_ref[:, 512 + h : 768 + h])
                    d_y = dot(mine[:, cols], narrow_ref[:, 0:256])
                    d_z = dot(mine[:, cols], narrow_ref[:, 256:512])
                    advect = field[now, 0, rows, cols] * d_x
                    advect = advect + field[now, 1, rows, cols] * d_y
                    advect = advect + field[now, 2, rows, cols] * d_z
                    partial[c, rows, cols] = field[now, c, rows, cols] + (spread - advect)
        for c in (0, 2, 1) if step + 1 < STEPS else (0, 2):
            close(step, c)

    final = STEPS % 2
    snap_ref[:, 0:512] = field[final, 0].astype(BF16)
    snap_ref[:, 512:1024] = field[final, 2].astype(BF16)
    for copy in loads[7:9]:
        copy.wait()

    def block(index):
        return pl.ds(pl.multiple_of(index * 64, 64), 64)

    def exchange(kind, pairs):
        copies = []
        for d, (src, dst) in enumerate(pairs):
            copy = remote(src, dst, grp_send.at[kind, d], grp_recv.at[kind, d], (sim, peers[d]))
            copy.start()
            copies.append(copy)
        return copies

    z1 = dot(snap_ref[...], enc_ref[...])
    z1_ref[...] = z1
    h1_ref[...] = (z1 * jax.nn.sigmoid(z1)).astype(BF16).reshape(4, 64, 256)
    h_copies = exchange(0, [(h1_ref.at[p], crop_h.at[grp]) for p in peers])
    close(STEPS - 1, 1)
    table_high, table_low = parts(bottom_ref[...])
    stress = []
    for c in (0, 2):
        high, low = parts(field[final, c])
        stress.append(dot(high, table_high) + dot(high, table_low) + dot(low, table_high))
    side = pltpu.roll(stress[1], 64, 1)
    both = jnp.where(lanes_low((256, 128)), stress[0], side).astype(BF16)
    target_ref[...] = both.reshape(4, 64, 128)
    t_copies = exchange(1, [(target_ref.at[p], crop_t.at[grp]) for p in peers])
    a_copies = []
    for d, p in enumerate((mate, across)):
        copy = remote(
            h1_ref, all_h.at[:, grp], grp_send.at[2, d], grp_recv.at[2, d], (sim, p)
        )
        copy.start()
        a_copies.append(copy)
    crop_h[grp] = h1_ref[grp]
    crop_t[grp] = target_ref[grp]
    all_h[:, grp] = h1_ref[...]
    for k in range(9):
        shifted[k, 0:16] = jnp.zeros((16, 256), BF16)
        shifted[k, 272:288] = jnp.zeros((16, 256), BF16)
        for j in range(4):
            shifted_low[k, j, 0:16] = jnp.zeros((16, 128), BF16)
            shifted_low[k, j, 272:288] = jnp.zeros((16, 128), BF16)
            shifted_high[k, j, 0:16] = jnp.zeros((16, 128), BF16)
            shifted_high[k, j, 272:288] = jnp.zeros((16, 128), BF16)
    scatter = perm[...].T.astype(BF16)
    for c in range(3):
        high, low = parts(field[final, c])
        vel_ref[c] = dot(scatter, high) + dot(scatter, low)
    stores = [pltpu.make_async_copy(vel_ref, out_hbm, store_sem.at[0])]
    stores[0].start()

    for copy in h_copies:
        copy.wait()
    for copy in loads[9:]:
        copy.wait()
    value = crop_h[...].reshape(256, 256).astype(F32)
    for dx, dz, moved in variants(value, 256):
        shifted[3 * (dx + 1) + dz + 1, 16:272] = moved.astype(BF16)
    sums = [jnp.zeros((256, 256), F32)] * 2
    for dx in (-1, 0, 1):
        for dy in (-1, 0, 1):
            for dz in (-1, 0, 1):
                tap = 9 * (dx + 1) + 3 * (dy + 1) + dz + 1
                start = 16 * (1 + dy)
                sums[tap % 2] = sums[tap % 2] + dot(
                    shifted[3 * (dx + 1) + dz + 1, start : start + 256], conv_ref[tap]
                )
    z2 = sums[0] + sums[1]
    a_copies[1].wait()
    relay = remote(
        all_h.at[:, across],
        all_h.at[:, across],
        grp_send.at[2, 2],
        grp_recv.at[2, 2],
        (sim, mate),
    )
    relay.start()
    a_copies = [a_copies[0], relay]
    h2 = (z2 * jax.nn.sigmoid(z2)).astype(BF16)
    output = dot(h2, head_ref[...])
    for copy in t_copies:
        copy.wait()
    target = crop_t[...].reshape(256, 128).astype(F32)
    resid = ((output - target) * (LOSS_WEIGHT / 65536.0)).astype(BF16)
    dz2 = (dot_cols(resid, head_ref[...]) * silu_grad(z2)).astype(BF16)
    low = lanes_low((128, 128))
    for j in range(4):
        lanes = slice(128 * (j // 2), 128 * (j // 2) + 128)
        upper, under = dz2[0:128, lanes].astype(F32), dz2[128:256, lanes].astype(F32)
        if j % 2 == 0:
            packed = jnp.where(low, upper, pltpu.roll(under, 64, 1))
        else:
            packed = jnp.where(low, pltpu.roll(upper, 64, 1), under)
        dz2_buf[j] = packed.astype(BF16)
    all_dz2[grp] = dz2_buf[grp]
    z_copies = exchange(3, [(dz2_buf.at[p], all_dz2.at[grp]) for p in peers])
    head_buf[...] = dot_rows(h2, resid).astype(BF16).reshape(4, 64, 128)
    g_copies = exchange(4, [(head_buf.at[p], all_head.at[d]) for d, p in enumerate(peers)])

    for dx, dz, moved in variants(dz2.astype(F32), 256):
        shifted[3 * (dx + 1) + dz + 1, 16:272] = moved.astype(BF16)
    sums = [jnp.zeros((256, 256), F32)] * 2
    for dx in (-1, 0, 1):
        for dy in (-1, 0, 1):
            for dz in (-1, 0, 1):
                tap = 9 * (dx + 1) + 3 * (dy + 1) + dz + 1
                start = 16 * (1 - dy)
                sums[tap % 2] = sums[tap % 2] + dot_cols(
                    shifted[3 * (1 - dx) + 1 - dz, start : start + 256], conv_ref[tap]
                )
    dh1_buf[...] = (sums[0] + sums[1]).astype(BF16).reshape(4, 64, 256)
    all_dh1[grp] = dh1_buf[grp]
    d_copies = exchange(5, [(dh1_buf.at[p], all_dh1.at[grp]) for p in peers])

    for copy in z_copies:
        copy.wait()
    for j in range(4):
        value = all_dz2[j].astype(F32)
        turned = pltpu.roll(value, 64, 1)
        here = jnp.concatenate(
            [jnp.where(low, value, turned), jnp.where(low, turned, value)], axis=0
        )
        for dx, dz, moved in variants(here, 128):
            k = 3 * (dx + 1) + dz + 1
            side = lanes_low((256, 128))
            shifted_low[k, j, 16:272] = jnp.where(side, moved, 0.0).astype(BF16)
            shifted_high[k, j, 16:272] = jnp.where(side, 0.0, moved).astype(BF16)
    for copy in a_copies:
        copy.wait()

    def tap_place(tap):
        dx, dy, dz = tap // 9 - 1, tap // 3 % 3 - 1, tap % 3 - 1
        return 3 * (1 - dx) + 1 - dz, 16 * (1 - dy)

    def conv_grad(part):
        pairs = range(4 * part, min(4 * part + 4, 14))
        for place, pair in enumerate(pairs):
            for j in range(4):
                k, start = tap_place(2 * pair)
                value = shifted_low[k, j, start : start + 256]
                if 2 * pair + 1 < 27:
                    k, start = tap_place(2 * pair + 1)
                    value = value + shifted_high[k, j, start : start + 256]
                taps[j * 256 : j * 256 + 256, place * 128 : place * 128 + 128] = value
        width = 128 * len(pairs)
        grad = dot_rows(taps[:, 0:width], all_h[...].reshape(1024, 256)).astype(BF16)
        if part == PARTS:
            for half in range(2):
                lanes = slice(128 * half, 128 * half + 128)
                small[half * 3 : half * 3 + 3] = grad[0:192, lanes].reshape(3, 4, 16, 128)
            return
        count = 512
        for half in range(2):
            work[part, 32 * half : 32 * half + count // 16] = grad[
                0:count, 128 * half : 128 * half + 128
            ].reshape(count // 16, 16, 128)

    def spread(part, phase, triples):
        copies = []
        for d, (src, dst, device) in enumerate(triples):
            copy = remote(
                src, dst, sum_send.at[part, phase, d], sum_recv.at[part, phase, d], device
            )
            copy.start()
            copies.append(copy)
        return copies

    depth_way = (depth, peers_depth, dev_depth)
    plane_way = (plane, peers_plane, dev_plane)
    ways = [(depth_way, plane_way)] + [(plane_way, depth_way)] * 2
    flying = {}

    def eight(index):
        return pl.ds(pl.multiple_of(index * 8, 8), 8)

    def advance(part, phase):
        (a, first, dev_first), (b, second, dev_second) = ways[part]
        if phase > 0:
            for copy in flying[part]:
                copy.wait()
        if phase == 0:
            triples = [
                (work.at[part, eight(first[d])], recv_first.at[part, d], dev_first[d])
                for d in range(7)
            ]
        if phase == 1:
            total = work[part, eight(a)].astype(F32)
            for d in range(7):
                total = total + recv_first[part, d].astype(F32)
            work_second[part] = total.astype(BF16)
            triples = [
                (work_second.at[part, second[d]], recv_second.at[part, d], dev_second[d])
                for d in range(7)
            ]
        if phase == 2:
            total = work_second[part, b].astype(F32)
            for d in range(7):
                total = total + recv_second[part, d].astype(F32)
            mine = a * 8 + b
            result[part, mine] = total.astype(BF16)
            triples = [
                (result.at[part, mine], result.at[part, mine], dev_second[d]) for d in range(7)
            ]
        if phase == 3:
            mine = eight(a)
            triples = [
                (result.at[part, mine], result.at[part, mine], dev_first[d]) for d in range(7)
            ]
        if phase < 4:
            flying[part] = spread(part, phase, triples)
        else:
            copy = pltpu.make_async_copy(
                result.at[part], result_hbm.at[part], store_sem.at[1 + part]
            )
            copy.start()
            stores.append(copy)

    tail = {}

    def settle(which, phase):
        piece, layers, ready = tails[which]
        if phase > 0:
            for copy in tail[which]:
                copy.wait()

        def spread_small(triples):
            copies = []
            for d, (src, dst, device) in enumerate(triples):
                copy = remote(
                    src,
                    dst,
                    tail_send.at[which, phase, d],
                    tail_recv.at[which, phase, d],
                    device,
                )
                copy.start()
                copies.append(copy)
            return copies

        if phase == 0:
            if which == 0:
                tail[which] = spread_small(
                    [
                        (small.at[peers_plane[d]], small_recv.at[d], dev_plane[d])
                        for d in range(7)
                    ]
                )
            else:
                triples = []
                for turn in (0, 1):
                    side = lax.rem(grp // 2 + turn, 2)
                    for d in range(8):
                        if turn or d:
                            triples.append(
                                (
                                    enc_half.at[side, lax.rem(plane + d, 8)],
                                    enc_recv.at[8 * turn + d - 1],
                                    wide_plane[8 * turn + d - 1],
                                )
                            )
                tail[which] = spread_small(triples)
        if phase == 1:
            if which == 0:
                total = small[plane].astype(F32)
                for d in range(7):
                    total = total + small_recv[d].astype(F32)
            else:
                total = enc_half[grp // 2, plane].astype(F32)
                for d in range(15):
                    total = total + enc_recv[d].astype(F32)
            piece[...] = total.astype(BF16)
            place, devices = depth, dev_depth
            layers[place] = piece[...]
            tail[which] = spread_small(
                [(piece, layers.at[place], devices[d]) for d in range(7)]
            )
        if phase == 2:
            total = layers[0].astype(F32)
            for d in range(1, 8):
                total = total + layers[d].astype(F32)
            place, devices = plane, dev_plane
            ready[place] = total.astype(BF16)
            tail[which] = spread_small(
                [(ready.at[place], ready.at[place], devices[d]) for d in range(7)]
            )
        if phase == 3:
            copy = pltpu.make_async_copy(
                ready, (small_hbm, enc_grad_hbm)[which], store_sem.at[1 + PARTS + which]
            )
            copy.start()
            stores.append(copy)

    tails = (
        (small_piece, small_layers, small_ready),
        (enc_piece, enc_layers, enc_ready),
    )

    for part in (0, 1, 2):
        conv_grad(part)
        advance(part, 0)
    conv_grad(PARTS)
    for copy in g_copies:
        copy.wait()
    total = head_buf[grp].astype(F32)
    for d in range(3):
        total = total + all_head[d].astype(F32)
    small[6] = total.astype(BF16).reshape(4, 16, 128)
    small[7] = jnp.zeros((4, 16, 128), BF16)
    settle(0, 0)

    for copy in d_copies:
        copy.wait()
    dz1 = (all_dh1[...].reshape(256, 256).astype(F32) * silu_grad(z1_ref[...])).astype(BF16)
    for b in range(4):
        grad = dot_rows(dz1, snap_ref[:, b * 256 : b * 256 + 256])
        enc_buf[:, b] = grad.reshape(4, 64, 256)
    theirs = lax.rem(mate, 2)
    ours = lax.rem(grp, 2)
    for side in range(2):
        enc_out[side] = enc_buf[2 * side + theirs].astype(BF16)
    m_copy = remote(enc_out, enc_in, grp_send.at[6, 0], grp_recv.at[6, 0], (sim, mate))
    m_copy.start()
    m_copy.wait()
    for side in range(2):
        for b in range(4):
            total = enc_buf[2 * side + ours, b] + enc_in[side, b].astype(F32)
            for half in range(2):
                enc_half[side, 2 * b + half] = total[:, 128 * half : 128 * half + 128].astype(
                    BF16
                )
    settle(1, 0)
    for part, phase in ORDER:
        if part < PARTS:
            advance(part, phase)
        else:
            settle(part - PARTS, phase)
    for copy in stores:
        copy.wait()


ORDER = [
    (1, 1), (0, 1), (2, 1), (3, 1), (4, 1),
    (1, 2), (0, 2), (2, 2), (3, 2), (4, 2),
    (1, 3), (0, 3), (2, 3), (3, 3), (4, 3),
    (1, 4), (0, 4), (2, 4),
]


def finish_kernel(
    result_hbm,
    small_hbm,
    enc_grad_hbm,
    vel_in,
    conv_hbm,
    enc_hbm,
    head_hbm,
    vel_out,
    result,
    small,
    enc_grad,
    vel_ref,
    conv_ref,
    enc_ref,
    head_ref,
    load_sem,
    store_sem,
):
    pairs = [(vel_in.at[c], vel_ref.at[c]) for c in range(3)]
    pairs += [(result_hbm.at[part], result.at[part]) for part in range(PARTS)]
    pairs += [(small_hbm, small), (enc_grad_hbm, enc_grad)]
    loads = [
        pltpu.make_async_copy(src, dst, load_sem.at[k]) for k, (src, dst) in enumerate(pairs)
    ]
    for copy in loads:
        copy.start()
    stores = []

    def store(src, dst):
        copy = pltpu.make_async_copy(src, dst, store_sem.at[len(stores)])
        copy.start()
        stores.append(copy)

    for c in range(3):
        loads[c].wait()
        store(vel_ref.at[c], vel_out.at[c])
    for part in range(PARTS):
        loads[3 + part].wait()
        for half in range(2):
            lanes = slice(128 * half, 128 * half + 128)
            value = result[part, 32 * half : 32 * half + 32].astype(F32)
            conv_ref[512 * part : 512 * part + 512, lanes] = value.reshape(512, 128)
        span = pl.ds(512 * part, 512)
        store(conv_ref.at[span], conv_hbm.at[span])
    loads[3 + PARTS].wait()
    for half in range(2):
        lanes = slice(128 * half, 128 * half + 128)
        value = small[3 * half : 3 * half + 3].astype(F32).reshape(192, 128)
        conv_ref[512 * PARTS : CONV_ROWS, lanes] = value
    span = pl.ds(512 * PARTS, 192)
    store(conv_ref.at[span], conv_hbm.at[span])
    head_ref[...] = small[6].astype(F32).reshape(64, 128)
    store(head_ref, head_hbm)
    loads[4 + PARTS].wait()
    for b in range(8):
        enc_ref[:, 128 * b : 128 * b + 128] = enc_grad[b].astype(F32)
    store(enc_ref, enc_hbm)
    for copy in stores:
        copy.wait()


VM = pl.BlockSpec(memory_space=pltpu.VMEM)
HB = pl.BlockSpec(memory_space=pltpu.HBM)


def shaped(shape, dtype):
    return jax.ShapeDtypeStruct(shape, dtype)


def body(velocity, slot_of, w_encode, w_conv, w_head):
    tables = element_tables(NP)
    dma = pltpu.SemaphoreType.DMA
    vm = pltpu.VMEM
    inputs = (velocity[0, 0], slot_of[0], *tables, w_encode, w_conv, w_head)
    velocity_next, result, small, enc_grad = pl.pallas_call(
        lambda *refs: step_kernel(lax.axis_size("sim"), *refs),
        name="step",
        out_shape=(
            shaped((3, 256, 512), F32),
            shaped((PARTS, 64, 16, 128), BF16),
            shaped((8, 4, 16, 128), BF16),
            shaped((8, 64, 128), BF16),
        ),
        in_specs=[HB] * len(inputs),
        out_specs=(HB,) * 4,
        scratch_shapes=[
            vm((PARTS, 64, 16, 128), BF16),
            vm((3, 256, 512), F32),
            vm((1, 256), jnp.int32),
            *[vm(table.shape, table.dtype) for table in tables],
            vm((1024, 256), BF16),
            vm((27, 256, 256), BF16),
            vm((256, 128), BF16),
            dma((len(inputs) + 2,)),
            dma((3 + PARTS,)),
            vm((256, 256), F32),
            vm((2, 3, 256, 512), F32),
            vm((3, 256, 512), F32),
            vm((3, 256, 384), F32),
            vm((STEPS, 2, 3, 64, 128), BF16),
            vm((STEPS, 2, 3, 32, 128), BF16),
            vm((STEPS, 2, 3, 64, 128), BF16),
            vm((STEPS, 2, 3, 32, 128), BF16),
            dma((STEPS, 3, 4)),
            dma((STEPS, 3, 4)),
            vm((4, 64, 256), BF16),
            vm((256, 256), F32),
            vm((256, 1024), BF16),
            vm((4, 64, 128), BF16),
            vm((4, 64, 256), BF16),
            vm((4, 64, 128), BF16),
            vm((4, 4, 64, 256), BF16),
            vm((9, 288, 256), BF16),
            vm((4, 128, 128), BF16),
            vm((4, 128, 128), BF16),
            vm((9, 4, 288, 128), BF16),
            vm((9, 4, 288, 128), BF16),
            vm((1024, 512), BF16),
            vm((4, 64, 256), BF16),
            vm((4, 64, 256), BF16),
            vm((4, 4, 64, 256), F32),
            vm((2, 4, 64, 256), BF16),
            vm((2, 4, 64, 256), BF16),
            vm((4, 64, 128), BF16),
            vm((3, 64, 128), BF16),
            dma((7, 3)),
            dma((7, 3)),
            vm((PARTS, 64, 16, 128), BF16),
            vm((PARTS, 7, 8, 16, 128), BF16),
            vm((PARTS, 8, 16, 128), BF16),
            vm((PARTS, 7, 16, 128), BF16),
            dma((PARTS, 4, 7)),
            dma((PARTS, 4, 7)),
            vm((8, 4, 16, 128), BF16),
            vm((7, 4, 16, 128), BF16),
            vm((4, 16, 128), BF16),
            vm((8, 4, 16, 128), BF16),
            vm((8, 4, 16, 128), BF16),
            vm((2, 8, 64, 128), BF16),
            vm((15, 64, 128), BF16),
            vm((64, 128), BF16),
            vm((8, 64, 128), BF16),
            vm((8, 64, 128), BF16),
            dma((2, 3, 15)),
            dma((2, 3, 15)),
        ],
        compiler_params=pltpu.CompilerParams(
            collective_id=0, has_side_effects=True, vmem_limit_bytes=62 * 2**20
        ),
    )(*inputs)
    conv, encode, head, velocity_next = pl.pallas_call(
        finish_kernel,
        name="finish",
        out_shape=(
            shaped((CONV_ROWS, 256), F32),
            shaped((64, 1024), F32),
            shaped((64, 128), F32),
            shaped((3, 256, 512), F32),
        ),
        in_specs=[HB] * 4,
        out_specs=(HB,) * 4,
        scratch_shapes=[
            vm((PARTS, 64, 16, 128), BF16),
            vm((8, 4, 16, 128), BF16),
            vm((8, 64, 128), BF16),
            vm((3, 256, 512), F32),
            vm((CONV_ROWS, 256), F32),
            vm((64, 1024), F32),
            vm((64, 128), F32),
            dma((PARTS + 5,)),
            dma((PARTS + 6,)),
        ],
        compiler_params=pltpu.CompilerParams(vmem_limit_bytes=62 * 2**20),
    )(result, small, enc_grad, velocity_next)
    return (
        velocity_next[None, None],
        encode.T,
        conv.reshape(27, 64, 256).transpose(0, 2, 1),
        head,
    )


def solution(mesh):
    placed = (P("sim", "grp", None, None, None), P("sim", "grp", None), P(), P(), P())
    return jax.shard_map(
        body,
        mesh=mesh,
        in_specs=placed,
        out_specs=(
            P("sim", "grp", None, None, None),
            P(None, "grp"),
            P(None, None, "grp"),
            P("grp", None),
        ),
        check_vma=False,
    )
```

```python
import jax
import jax.numpy as jnp
import ml_dtypes
import numpy as np
from jax import lax
from jax.experimental import pallas as pl
from jax.experimental.pallas import tpu as pltpu
from jax.sharding import PartitionSpec as P

NP = 8
STEPS = 2
VISCOSITY = 0.2
TIME_STEP = 0.005
PENALTY = 100.0
LOSS_WEIGHT = 64.0

MESH = pl.DeviceIdType.MESH
F32 = jnp.float32
BF16 = jnp.bfloat16

CONV_ROWS = 1728
PARTS = 3


def derivative_matrix(count):
    places = np.arange(count)
    points = -np.cos(np.pi * places / (count - 1))
    weights = np.where(places % 2 == 0, 1.0, -1.0)
    weights[0] = weights[0] * 0.5
    weights[count - 1] = weights[count - 1] * 0.5
    identity = np.eye(count)
    spread = points[:, None] - points[None, :] + identity
    deriv = weights[None, :] / weights[:, None] / spread
    deriv = deriv * (1.0 - identity)
    return deriv - identity * deriv.sum(axis=1)[:, None]


def element_tables(count):
    deriv = derivative_matrix(count)
    single = np.eye(count)
    square = np.eye(count * count)
    along_x = np.kron(deriv, square)
    along_y = np.kron(single, np.kron(deriv, single))
    along_z = np.kron(square, deriv)
    laplace = along_x @ along_x + along_y @ along_y + along_z @ along_z
    grid = np.arange(count**3).reshape(count, count, count)
    final = count - 1
    chosen = np.concatenate(
        [
            grid[0].ravel(),
            grid[final].ravel(),
            grid[:, 0].ravel(),
            grid[:, final].ravel(),
            grid[:, :, 0].ravel(),
            grid[:, :, final].ravel(),
        ]
    )
    select = np.zeros((count**3, chosen.size))
    select[chosen, np.arange(chosen.size)] = 1.0
    bottom = np.zeros((count**3, 2 * count * count))
    for first in range(count):
        for middle in range(count):
            for inner in range(count):
                bottom[grid[first, middle, inner], first * count + inner] = (
                    VISCOSITY * deriv[0, middle]
                )
    diffuse = TIME_STEP * VISCOSITY * (laplace.T - PENALTY * (select @ select.T))
    half = count**3 // 2
    small = lambda table: np.asarray(table, ml_dtypes.bfloat16)
    return (
        small(np.concatenate([TIME_STEP * along_x.T, diffuse], axis=1)),
        small(
            TIME_STEP
            * np.concatenate([along_y.T[:half, :half], along_z.T[:half, :half]], axis=1)
        ),
        small(select),
        np.asarray(bottom, np.float32),
    )


def dot(a, b):
    return lax.dot_general(a, b, (((1,), (0,)), ((), ())), preferred_element_type=F32)


def dot_rows(a, b):
    return lax.dot_general(a, b, (((0,), (0,)), ((), ())), preferred_element_type=F32)


def dot_cols(a, b):
    return lax.dot_general(a, b, (((1,), (1,)), ((), ())), preferred_element_type=F32)


def parts(value):
    high = value.astype(BF16)
    return high, (value - high.astype(F32)).astype(BF16)


def silu_grad(value):
    sigma = jax.nn.sigmoid(value)
    return sigma * (1.0 + value * (1.0 - sigma))


def lanes_low(shape):
    return lax.broadcasted_iota(jnp.int32, shape, len(shape) - 1) < 64


def packed_rows(value, high):
    half = value.shape[0] // 2
    turned = pltpu.roll(value[half:], 64, 1)
    low = lanes_low((half, 128))
    packed = jnp.where(low, turned, value[:half]) if high else jnp.where(low, value[:half], turned)
    return packed.astype(BF16)


def swap_halves(value):
    return pltpu.roll(value, 64, 1).astype(BF16)


def spread_rows(packed):
    value = packed.astype(F32)
    return jnp.concatenate([value, pltpu.roll(value, 64, 1)], axis=0)


def remote(src, dst, send, recv, device):
    return pltpu.make_async_remote_copy(
        src_ref=src,
        dst_ref=dst,
        send_sem=send,
        recv_sem=recv,
        device_id=device,
        device_id_type=MESH,
    )


def variants(value, width):
    place = lax.broadcasted_iota(jnp.int32, (32, 8, width), 1)
    flat = value.reshape(32, 8, width)
    along_z = {
        -1: jnp.where(place == 0, 0.0, pltpu.roll(flat, 1, 1)),
        0: flat,
        1: jnp.where(place == 7, 0.0, pltpu.roll(flat, 7, 1)),
    }
    for dz in (-1, 0, 1):
        full = along_z[dz].reshape(16, 2, 8, width)
        none = jnp.zeros((16, 1, 8, width), F32)
        yield -1, dz, jnp.concatenate([none, full[:, :1]], axis=1).reshape(256, width)
        yield 0, dz, full.reshape(256, width)
        yield 1, dz, jnp.concatenate([full[:, 1:], none], axis=1).reshape(256, width)


def step_kernel(
    sims,
    vel_hbm,
    slot_hbm,
    wide_hbm,
    narrow_hbm,
    sel_hbm,
    bottom_hbm,
    enc_hbm,
    conv_hbm,
    head_hbm,
    out_hbm,
    result_hbm,
    small_hbm,
    enc_grad_hbm,
    result,
    vel_ref,
    slot_ref,
    wide_ref,
    narrow_ref,
    sel_ref,
    bottom_ref,
    enc_ref,
    conv_ref,
    head_ref,
    load_sem,
    store_sem,
    perm,
    field,
    partial,
    faces,
    send_x,
    send_y,
    recv_x,
    recv_y,
    halo_send,
    halo_recv,
    h1_ref,
    z1_ref,
    snap_ref,
    target_ref,
    crop_h,
    crop_t,
    all_h,
    shifted,
    dz2_buf,
    all_dz2,
    shifted_low,
    shifted_high,
    taps,
    dh1_buf,
    all_dh1,
    enc_buf,
    enc_out,
    enc_in,
    head_buf,
    all_head,
    grp_send,
    grp_recv,
    work,
    recv_first,
    work_second,
    recv_second,
    sum_send,
    sum_recv,
    small,
    small_recv,
    small_piece,
    small_layers,
    small_ready,
    enc_half,
    enc_recv,
    enc_piece,
    enc_layers,
    enc_ready,
    tail_send,
    tail_recv,
):
    sim = lax.axis_index("sim")
    grp = lax.axis_index("grp")

    sources = [
        (slot_hbm, slot_ref),
        (vel_hbm.at[0], vel_ref.at[0]),
        (vel_hbm.at[1], vel_ref.at[1]),
        (vel_hbm.at[2], vel_ref.at[2]),
        (sel_hbm, sel_ref),
        (wide_hbm, wide_ref),
        (narrow_hbm, narrow_ref),
        (enc_hbm, enc_ref),
        (bottom_hbm, bottom_ref),
        (conv_hbm, conv_ref),
        (head_hbm, head_ref),
    ]
    loads = [
        pltpu.make_async_copy(src, dst, load_sem.at[k]) for k, (src, dst) in enumerate(sources)
    ]
    for copy in loads[:7]:
        copy.start()

    right = (lax.rem(sim + 1, sims), grp)
    left = (lax.rem(sim + sims - 1, sims), grp)
    above = (sim, lax.rem(grp + 1, 4))
    below = (sim, lax.rem(grp + 3, 4))
    peers = [lax.rem(grp + d, 4) for d in (1, 2, 3)]
    plane, depth = sim // 8, lax.rem(sim, 8)
    peers_plane = [lax.rem(plane + d, 8) for d in range(1, 8)]
    peers_depth = [lax.rem(depth + d, 8) for d in range(1, 8)]
    dev_plane = [(p * 8 + depth, grp) for p in peers_plane]
    dev_depth = [(plane * 8 + p, grp) for p in peers_depth]
    mate = grp + 1 - 2 * lax.rem(grp, 2)
    across = lax.rem(grp + 2, 4)
    wide_plane = [
        (lax.rem(plane + d, 8) * 8 + depth, across if turn else grp)
        for turn in (0, 1)
        for d in range(8)
    ][1:]
    friends = dev_depth + wide_plane + [left, right, (sim, lax.rem(mate + 2, 4)), (sim, mate)]
    barrier = pltpu.get_barrier_semaphore()
    for device in friends:
        pl.semaphore_signal(barrier, inc=1, device_id=device, device_id_type=MESH)

    loads[0].wait()
    owner = lax.broadcasted_iota(jnp.int32, (256, 256), 0)
    by_slot = jnp.where(owner == slot_ref[...], 1.0, 0.0).astype(F32)
    by_place = by_slot.T
    for ix in range(2):
        for iy in range(4):
            for j in range(4):
                old = ix * 128 + iy * 32 + j * 8
                new = j * 64 + iy * 16 + ix * 8
                perm[new : new + 8] = by_place[old : old + 8]
    gather = perm[...].astype(BF16)
    for copy in loads[7:]:
        copy.start()
    for c in range(3):
        loads[1 + c].wait()
        high, low = parts(vel_ref[c])
        field[0, c] = dot(gather, high) + dot(gather, low)
    loads[4].wait()
    flights = {}

    def emit(step, c):
        faces[c] = dot(field[step % 2, c].astype(BF16), sel_ref[...])
        along_x = faces[c, :, 0:128].reshape(16, 2, 8, 128)
        along_y = faces[c, :, 128:256].reshape(4, 4, 16, 128)
        send_x[step, 0, c] = packed_rows(along_x[:, 1].reshape(128, 128), True)
        send_x[step, 1, c] = packed_rows(along_x[:, 0].reshape(128, 128), False)
        send_y[step, 0, c] = packed_rows(along_y[:, 3].reshape(64, 128), True)
        send_y[step, 1, c] = packed_rows(along_y[:, 0].reshape(64, 128), False)
        if step == 0 and c == 0:
            pl.semaphore_wait(barrier, len(friends))
        copies = []
        for k, (src, dst, device) in enumerate(
            [
                (send_x.at[step, 0, c], recv_x.at[step, 0, c], right),
                (send_x.at[step, 1, c], recv_x.at[step, 1, c], left),
                (send_y.at[step, 0, c], recv_y.at[step, 0, c], above),
                (send_y.at[step, 1, c], recv_y.at[step, 1, c], below),
            ]
        ):
            copy = remote(
                src, dst, halo_send.at[step, c, k], halo_recv.at[step, c, k], device
            )
            copy.start()
            copies.append(copy)
        flights[step, c] = copies

    def close(step, c):
        now, later = step % 2, (step + 1) % 2
        for copy in flights[step, c]:
            copy.wait()
        along_x = faces[c, :, 0:128].reshape(16, 2, 8, 128)
        along_y = faces[c, :, 128:256].reshape(4, 4, 16, 128)
        along_z = faces[c, :, 256:384].reshape(4, 8, 8, 128)
        from_left = spread_rows(recv_x[step, 0, c]).reshape(16, 1, 8, 128)
        from_right = spread_rows(recv_x[step, 1, c]).reshape(16, 1, 8, 128)
        from_below = spread_rows(recv_y[step, 0, c]).reshape(4, 1, 16, 128)
        from_above = spread_rows(recv_y[step, 1, c]).reshape(4, 1, 16, 128)
        from_below = jnp.where(grp > 0, from_below, 0.0)
        from_above = jnp.where(grp < 3, from_above, 0.0)
        before = jnp.concatenate([from_left, along_x[:, :1]], axis=1).reshape(256, 128)
        after = jnp.concatenate([along_x[:, 1:], from_right], axis=1).reshape(256, 128)
        low = lanes_low((256, 128))
        beside_x = swap_halves(jnp.where(low, after, before))
        before = jnp.concatenate([from_below, along_y[:, :3]], axis=1).reshape(256, 128)
        after = jnp.concatenate([along_y[:, 1:], from_above], axis=1).reshape(256, 128)
        beside_y = swap_halves(jnp.where(low, after, before))
        place = lax.broadcasted_iota(jnp.int32, (32, 8, 128), 1)
        flat_z = along_z.reshape(32, 8, 128)
        behind = jnp.concatenate([along_z[3:], along_z[:3]], axis=0).reshape(32, 8, 128)
        ahead = jnp.concatenate([along_z[1:], along_z[:1]], axis=0).reshape(32, 8, 128)
        before = pltpu.roll(jnp.where(place == 7, behind, flat_z), 1, 1).reshape(256, 128)
        after = pltpu.roll(jnp.where(place == 0, ahead, flat_z), 7, 1).reshape(256, 128)
        beside_z = swap_halves(jnp.where(low, after, before))
        beside = jnp.concatenate([beside_x, beside_y, beside_z], axis=1)
        for h in range(0, 512, 256):
            cols = slice(h, h + 256)
            pull = dot_cols(beside, sel_ref[cols])
            field[later, c, :, cols] = (
                partial[c, :, cols] + (TIME_STEP * VISCOSITY * PENALTY) * pull
            )
        if step + 1 < STEPS:
            emit(step + 1, c)

    for c in range(3):
        emit(0, c)
    for copy in loads[5:7]:
        copy.wait()
    for step in range(STEPS):
        now, later = step % 2, (step + 1) % 2
        for c in range(3):
            for row in range(0, 256, 128):
                rows = slice(row, row + 128)
                mine = field[now, c, rows].astype(BF16)
                for h in range(0, 512, 256):
                    cols = slice(h, h + 256)
                    d_x = dot(mine, wide_ref[:, h : h + 256])
                    spread = dot(mine, wide_ref[:, 512 + h : 768 + h])
                    d_y = dot(mine[:, cols], narrow_ref[:, 0:256])
                    d_z = dot(mine[:, cols], narrow_ref[:, 256:512])
                    advect = field[now, 0, rows, cols] * d_x
                    advect = advect + field[now, 1, rows, cols] * d_y
                    advect = advect + field[now, 2, rows, cols] * d_z
                    partial[c, rows, cols] = field[now, c, rows, cols] + (spread - advect)
        for c in (0, 2, 1) if step + 1 < STEPS else (0, 2):
            close(step, c)

    final = STEPS % 2
    snap_ref[:, 0:512] = field[final, 0].astype(BF16)
    snap_ref[:, 512:1024] = field[final, 2].astype(BF16)
    for copy in loads[7:9]:
        copy.wait()

    def block(index):
        return pl.ds(pl.multiple_of(index * 64, 64), 64)

    def exchange(kind, pairs):
        copies = []
        for d, (src, dst) in enumerate(pairs):
            copy = remote(src, dst, grp_send.at[kind, d], grp_recv.at[kind, d], (sim, peers[d]))
            copy.start()
            copies.append(copy)
        return copies

    z1 = dot(snap_ref[...], enc_ref[...])
    z1_ref[...] = z1
    h1_ref[...] = (z1 * jax.nn.sigmoid(z1)).astype(BF16).reshape(4, 64, 256)
    h_copies = exchange(0, [(h1_ref.at[p], crop_h.at[grp]) for p in peers])
    close(STEPS - 1, 1)
    table_high, table_low = parts(bottom_ref[...])
    stress = []
    for c in (0, 2):
        high, low = parts(field[final, c])
        stress.append(dot(high, table_high) + dot(high, table_low) + dot(low, table_high))
    side = pltpu.roll(stress[1], 64, 1)
    both = jnp.where(lanes_low((256, 128)), stress[0], side).astype(BF16)
    target_ref[...] = both.reshape(4, 64, 128)
    t_copies = exchange(1, [(target_ref.at[p], crop_t.at[grp]) for p in peers])
    a_copies = []
    for d, p in enumerate((mate, across)):
        copy = remote(
            h1_ref, all_h.at[:, grp], grp_send.at[2, d], grp_recv.at[2, d], (sim, p)
        )
        copy.start()
        a_copies.append(copy)
    crop_h[grp] = h1_ref[grp]
    crop_t[grp] = target_ref[grp]
    all_h[:, grp] = h1_ref[...]
    for k in range(9):
        shifted[k, 0:16] = jnp.zeros((16, 256), BF16)
        shifted[k, 272:288] = jnp.zeros((16, 256), BF16)
        for j in range(4):
            shifted_low[k, j, 0:16] = jnp.zeros((16, 128), BF16)
            shifted_low[k, j, 272:288] = jnp.zeros((16, 128), BF16)
            shifted_high[k, j, 0:16] = jnp.zeros((16, 128), BF16)
            shifted_high[k, j, 272:288] = jnp.zeros((16, 128), BF16)
    scatter = perm[...].T.astype(BF16)
    for c in range(3):
        high, low = parts(field[final, c])
        vel_ref[c] = dot(scatter, high) + dot(scatter, low)
    stores = [pltpu.make_async_copy(vel_ref, out_hbm, store_sem.at[0])]
    stores[0].start()

    for copy in h_copies:
        copy.wait()
    for copy in loads[9:]:
        copy.wait()
    value = crop_h[...].reshape(256, 256).astype(F32)
    for dx, dz, moved in variants(value, 256):
        shifted[3 * (dx + 1) + dz + 1, 16:272] = moved.astype(BF16)
    sums = [jnp.zeros((256, 256), F32)] * 2
    for dx in (-1, 0, 1):
        for dy in (-1, 0, 1):
            for dz in (-1, 0, 1):
                tap = 9 * (dx + 1) + 3 * (dy + 1) + dz + 1
                start = 16 * (1 + dy)
                sums[tap % 2] = sums[tap % 2] + dot(
                    shifted[3 * (dx + 1) + dz + 1, start : start + 256], conv_ref[tap]
                )
    z2 = sums[0] + sums[1]
    a_copies[1].wait()
    relay = remote(
        all_h.at[:, across],
        all_h.at[:, across],
        grp_send.at[2, 2],
        grp_recv.at[2, 2],
        (sim, mate),
    )
    relay.start()
    a_copies = [a_copies[0], relay]
    h2 = (z2 * jax.nn.sigmoid(z2)).astype(BF16)
    output = dot(h2, head_ref[...])
    for copy in t_copies:
        copy.wait()
    target = crop_t[...].reshape(256, 128).astype(F32)
    resid = ((output - target) * (LOSS_WEIGHT / 65536.0)).astype(BF16)
    dz2 = (dot_cols(resid, head_ref[...]) * silu_grad(z2)).astype(BF16)
    low = lanes_low((128, 128))
    for j in range(4):
        lanes = slice(128 * (j // 2), 128 * (j // 2) + 128)
        upper, under = dz2[0:128, lanes].astype(F32), dz2[128:256, lanes].astype(F32)
        if j % 2 == 0:
            packed = jnp.where(low, upper, pltpu.roll(under, 64, 1))
        else:
            packed = jnp.where(low, pltpu.roll(upper, 64, 1), under)
        dz2_buf[j] = packed.astype(BF16)
    all_dz2[grp] = dz2_buf[grp]
    z_copies = exchange(3, [(dz2_buf.at[p], all_dz2.at[grp]) for p in peers])
    head_buf[...] = dot_rows(h2, resid).astype(BF16).reshape(4, 64, 128)
    g_copies = exchange(4, [(head_buf.at[p], all_head.at[d]) for d, p in enumerate(peers)])

    for dx, dz, moved in variants(dz2.astype(F32), 256):
        shifted[3 * (dx + 1) + dz + 1, 16:272] = moved.astype(BF16)
    sums = [jnp.zeros((256, 256), F32)] * 2
    for dx in (-1, 0, 1):
        for dy in (-1, 0, 1):
            for dz in (-1, 0, 1):
                tap = 9 * (dx + 1) + 3 * (dy + 1) + dz + 1
                start = 16 * (1 - dy)
                sums[tap % 2] = sums[tap % 2] + dot_cols(
                    shifted[3 * (1 - dx) + 1 - dz, start : start + 256], conv_ref[tap]
                )
    dh1_buf[...] = (sums[0] + sums[1]).astype(BF16).reshape(4, 64, 256)
    all_dh1[grp] = dh1_buf[grp]
    d_copies = exchange(5, [(dh1_buf.at[p], all_dh1.at[grp]) for p in peers])

    for copy in z_copies:
        copy.wait()
    for j in range(4):
        value = all_dz2[j].astype(F32)
        turned = pltpu.roll(value, 64, 1)
        here = jnp.concatenate(
            [jnp.where(low, value, turned), jnp.where(low, turned, value)], axis=0
        )
        for dx, dz, moved in variants(here, 128):
            k = 3 * (dx + 1) + dz + 1
            side = lanes_low((256, 128))
            shifted_low[k, j, 16:272] = jnp.where(side, moved, 0.0).astype(BF16)
            shifted_high[k, j, 16:272] = jnp.where(side, 0.0, moved).astype(BF16)
    for copy in a_copies:
        copy.wait()

    def tap_place(tap):
        dx, dy, dz = tap // 9 - 1, tap // 3 % 3 - 1, tap % 3 - 1
        return 3 * (1 - dx) + 1 - dz, 16 * (1 - dy)

    def conv_grad(part):
        pairs = range(4 * part, min(4 * part + 4, 14))
        for place, pair in enumerate(pairs):
            for j in range(4):
                k, start = tap_place(2 * pair)
                value = shifted_low[k, j, start : start + 256]
                if 2 * pair + 1 < 27:
                    k, start = tap_place(2 * pair + 1)
                    value = value + shifted_high[k, j, start : start + 256]
                taps[j * 256 : j * 256 + 256, place * 128 : place * 128 + 128] = value
        width = 128 * len(pairs)
        grad = dot_rows(taps[:, 0:width], all_h[...].reshape(1024, 256)).astype(BF16)
        if part == PARTS:
            for half in range(2):
                lanes = slice(128 * half, 128 * half + 128)
                small[half * 3 : half * 3 + 3] = grad[0:192, lanes].reshape(3, 4, 16, 128)
            return
        count = 512
        for half in range(2):
            work[part, 32 * half : 32 * half + count // 16] = grad[
                0:count, 128 * half : 128 * half + 128
            ].reshape(count // 16, 16, 128)

    def spread(part, phase, triples):
        copies = []
        for d, (src, dst, device) in enumerate(triples):
            copy = remote(
                src, dst, sum_send.at[part, phase, d], sum_recv.at[part, phase, d], device
            )
            copy.start()
            copies.append(copy)
        return copies

    depth_way = (depth, peers_depth, dev_depth)
    plane_way = (plane, peers_plane, dev_plane)
    ways = [(plane_way, depth_way)] * 3
    flying = {}

    def eight(index):
        return pl.ds(pl.multiple_of(index * 8, 8), 8)

    def advance(part, phase):
        (a, first, dev_first), (b, second, dev_second) = ways[part]
        if phase > 0:
            for copy in flying[part]:
                copy.wait()
        if phase == 0:
            triples = [
                (work.at[part, eight(first[d])], recv_first.at[part, d], dev_first[d])
                for d in range(7)
            ]
        if phase == 1:
            total = work[part, eight(a)].astype(F32)
            for d in range(7):
                total = total + recv_first[part, d].astype(F32)
            work_second[part] = total.astype(BF16)
            triples = [
                (work_second.at[part, second[d]], recv_second.at[part, d], dev_second[d])
                for d in range(7)
            ]
        if phase == 2:
            total = work_second[part, b].astype(F32)
            for d in range(7):
                total = total + recv_second[part, d].astype(F32)
            mine = a * 8 + b
            result[part, mine] = total.astype(BF16)
            triples = [
                (result.at[part, mine], result.at[part, mine], dev_second[d]) for d in range(7)
            ]
        if phase == 3:
            mine = eight(a)
            triples = [
                (result.at[part, mine], result.at[part, mine], dev_first[d]) for d in range(7)
            ]
        if phase < 4:
            flying[part] = spread(part, phase, triples)
        else:
            copy = pltpu.make_async_copy(
                result.at[part], result_hbm.at[part], store_sem.at[1 + part]
            )
            copy.start()
            stores.append(copy)

    tail = {}

    def settle(which, phase):
        piece, layers, ready = tails[which]
        if phase > 0:
            for copy in tail[which]:
                copy.wait()

        def spread_small(triples):
            copies = []
            for d, (src, dst, device) in enumerate(triples):
                copy = remote(
                    src,
                    dst,
                    tail_send.at[which, phase, d],
                    tail_recv.at[which, phase, d],
                    device,
                )
                copy.start()
                copies.append(copy)
            return copies

        if phase == 0:
            if which == 0:
                tail[which] = spread_small(
                    [
                        (small.at[peers_plane[d]], small_recv.at[d], dev_plane[d])
                        for d in range(7)
                    ]
                )
            else:
                triples = []
                for turn in (0, 1):
                    side = lax.rem(grp // 2 + turn, 2)
                    for d in range(8):
                        if turn or d:
                            triples.append(
                                (
                                    enc_half.at[side, lax.rem(plane + d, 8)],
                                    enc_recv.at[8 * turn + d - 1],
                                    wide_plane[8 * turn + d - 1],
                                )
                            )
                tail[which] = spread_small(triples)
        if phase == 1:
            if which == 0:
                total = small[plane].astype(F32)
                for d in range(7):
                    total = total + small_recv[d].astype(F32)
            else:
                total = enc_half[grp // 2, plane].astype(F32)
                for d in range(15):
                    total = total + enc_recv[d].astype(F32)
            piece[...] = total.astype(BF16)
            place, devices = depth, dev_depth
            layers[place] = piece[...]
            tail[which] = spread_small(
                [(piece, layers.at[place], devices[d]) for d in range(7)]
            )
        if phase == 2:
            total = layers[0].astype(F32)
            for d in range(1, 8):
                total = total + layers[d].astype(F32)
            place, devices = plane, dev_plane
            ready[place] = total.astype(BF16)
            tail[which] = spread_small(
                [(ready.at[place], ready.at[place], devices[d]) for d in range(7)]
            )
        if phase == 3:
            copy = pltpu.make_async_copy(
                ready, (small_hbm, enc_grad_hbm)[which], store_sem.at[1 + PARTS + which]
            )
            copy.start()
            stores.append(copy)

    tails = (
        (small_piece, small_layers, small_ready),
        (enc_piece, enc_layers, enc_ready),
    )

    for part in (0, 1, 2):
        conv_grad(part)
        advance(part, 0)
    conv_grad(PARTS)
    for copy in g_copies:
        copy.wait()
    total = head_buf[grp].astype(F32)
    for d in range(3):
        total = total + all_head[d].astype(F32)
    small[6] = total.astype(BF16).reshape(4, 16, 128)
    small[7] = jnp.zeros((4, 16, 128), BF16)
    settle(0, 0)

    for copy in d_copies:
        copy.wait()
    dz1 = (all_dh1[...].reshape(256, 256).astype(F32) * silu_grad(z1_ref[...])).astype(BF16)
    for b in range(4):
        grad = dot_rows(dz1, snap_ref[:, b * 256 : b * 256 + 256])
        enc_buf[:, b] = grad.reshape(4, 64, 256)
    theirs = lax.rem(mate, 2)
    ours = lax.rem(grp, 2)
    for side in range(2):
        enc_out[side] = enc_buf[2 * side + theirs].astype(BF16)
    m_copy = remote(enc_out, enc_in, grp_send.at[6, 0], grp_recv.at[6, 0], (sim, mate))
    m_copy.start()
    m_copy.wait()
    for side in range(2):
        for b in range(4):
            total = enc_buf[2 * side + ours, b] + enc_in[side, b].astype(F32)
            for half in range(2):
                enc_half[side, 2 * b + half] = total[:, 128 * half : 128 * half + 128].astype(
                    BF16
                )
    settle(1, 0)
    for part, phase in ORDER:
        if part < PARTS:
            advance(part, phase)
        else:
            settle(part - PARTS, phase)
    for copy in stores:
        copy.wait()


ORDER = [
    (0, 1), (1, 1), (2, 1), (3, 1), (4, 1),
    (0, 2), (1, 2), (2, 2), (3, 2), (4, 2),
    (0, 3), (1, 3), (2, 3), (3, 3), (4, 3),
    (0, 4), (1, 4), (2, 4),
]


def finish_kernel(
    result_hbm,
    small_hbm,
    enc_grad_hbm,
    vel_in,
    conv_hbm,
    enc_hbm,
    head_hbm,
    vel_out,
    result,
    small,
    enc_grad,
    vel_ref,
    conv_ref,
    enc_ref,
    head_ref,
    load_sem,
    store_sem,
):
    pairs = [(vel_in.at[c], vel_ref.at[c]) for c in range(3)]
    pairs += [(result_hbm.at[part], result.at[part]) for part in range(PARTS)]
    pairs += [(small_hbm, small), (enc_grad_hbm, enc_grad)]
    loads = [
        pltpu.make_async_copy(src, dst, load_sem.at[k]) for k, (src, dst) in enumerate(pairs)
    ]
    for copy in loads:
        copy.start()
    stores = []

    def store(src, dst):
        copy = pltpu.make_async_copy(src, dst, store_sem.at[len(stores)])
        copy.start()
        stores.append(copy)

    for c in range(3):
        loads[c].wait()
        store(vel_ref.at[c], vel_out.at[c])
    for part in range(PARTS):
        loads[3 + part].wait()
        for half in range(2):
            lanes = slice(128 * half, 128 * half + 128)
            value = result[part, 32 * half : 32 * half + 32].astype(F32)
            conv_ref[512 * part : 512 * part + 512, lanes] = value.reshape(512, 128)
        span = pl.ds(512 * part, 512)
        store(conv_ref.at[span], conv_hbm.at[span])
    loads[3 + PARTS].wait()
    for half in range(2):
        lanes = slice(128 * half, 128 * half + 128)
        value = small[3 * half : 3 * half + 3].astype(F32).reshape(192, 128)
        conv_ref[512 * PARTS : CONV_ROWS, lanes] = value
    span = pl.ds(512 * PARTS, 192)
    store(conv_ref.at[span], conv_hbm.at[span])
    head_ref[...] = small[6].astype(F32).reshape(64, 128)
    store(head_ref, head_hbm)
    loads[4 + PARTS].wait()
    for b in range(8):
        enc_ref[:, 128 * b : 128 * b + 128] = enc_grad[b].astype(F32)
    store(enc_ref, enc_hbm)
    for copy in stores:
        copy.wait()


VM = pl.BlockSpec(memory_space=pltpu.VMEM)
HB = pl.BlockSpec(memory_space=pltpu.HBM)


def shaped(shape, dtype):
    return jax.ShapeDtypeStruct(shape, dtype)


def body(velocity, slot_of, w_encode, w_conv, w_head):
    tables = element_tables(NP)
    dma = pltpu.SemaphoreType.DMA
    vm = pltpu.VMEM
    inputs = (velocity[0, 0], slot_of[0], *tables, w_encode, w_conv, w_head)
    velocity_next, result, small, enc_grad = pl.pallas_call(
        lambda *refs: step_kernel(lax.axis_size("sim"), *refs),
        name="step",
        out_shape=(
            shaped((3, 256, 512), F32),
            shaped((PARTS, 64, 16, 128), BF16),
            shaped((8, 4, 16, 128), BF16),
            shaped((8, 64, 128), BF16),
        ),
        in_specs=[HB] * len(inputs),
        out_specs=(HB,) * 4,
        scratch_shapes=[
            vm((PARTS, 64, 16, 128), BF16),
            vm((3, 256, 512), F32),
            vm((1, 256), jnp.int32),
            *[vm(table.shape, table.dtype) for table in tables],
            vm((1024, 256), BF16),
            vm((27, 256, 256), BF16),
            vm((256, 128), BF16),
            dma((len(inputs) + 2,)),
            dma((3 + PARTS,)),
            vm((256, 256), F32),
            vm((2, 3, 256, 512), F32),
            vm((3, 256, 512), F32),
            vm((3, 256, 384), F32),
            vm((STEPS, 2, 3, 64, 128), BF16),
            vm((STEPS, 2, 3, 32, 128), BF16),
            vm((STEPS, 2, 3, 64, 128), BF16),
            vm((STEPS, 2, 3, 32, 128), BF16),
            dma((STEPS, 3, 4)),
            dma((STEPS, 3, 4)),
            vm((4, 64, 256), BF16),
            vm((256, 256), F32),
            vm((256, 1024), BF16),
            vm((4, 64, 128), BF16),
            vm((4, 64, 256), BF16),
            vm((4, 64, 128), BF16),
            vm((4, 4, 64, 256), BF16),
            vm((9, 288, 256), BF16),
            vm((4, 128, 128), BF16),
            vm((4, 128, 128), BF16),
            vm((9, 4, 288, 128), BF16),
            vm((9, 4, 288, 128), BF16),
            vm((1024, 512), BF16),
            vm((4, 64, 256), BF16),
            vm((4, 64, 256), BF16),
            vm((4, 4, 64, 256), F32),
            vm((2, 4, 64, 256), BF16),
            vm((2, 4, 64, 256), BF16),
            vm((4, 64, 128), BF16),
            vm((3, 64, 128), BF16),
            dma((7, 3)),
            dma((7, 3)),
            vm((PARTS, 64, 16, 128), BF16),
            vm((PARTS, 7, 8, 16, 128), BF16),
            vm((PARTS, 8, 16, 128), BF16),
            vm((PARTS, 7, 16, 128), BF16),
            dma((PARTS, 4, 7)),
            dma((PARTS, 4, 7)),
            vm((8, 4, 16, 128), BF16),
            vm((7, 4, 16, 128), BF16),
            vm((4, 16, 128), BF16),
            vm((8, 4, 16, 128), BF16),
            vm((8, 4, 16, 128), BF16),
            vm((2, 8, 64, 128), BF16),
            vm((15, 64, 128), BF16),
            vm((64, 128), BF16),
            vm((8, 64, 128), BF16),
            vm((8, 64, 128), BF16),
            dma((2, 3, 15)),
            dma((2, 3, 15)),
        ],
        compiler_params=pltpu.CompilerParams(
            collective_id=0, has_side_effects=True, vmem_limit_bytes=62 * 2**20
        ),
    )(*inputs)
    conv, encode, head, velocity_next = pl.pallas_call(
        finish_kernel,
        name="finish",
        out_shape=(
            shaped((CONV_ROWS, 256), F32),
            shaped((64, 1024), F32),
            shaped((64, 128), F32),
            shaped((3, 256, 512), F32),
        ),
        in_specs=[HB] * 4,
        out_specs=(HB,) * 4,
        scratch_shapes=[
            vm((PARTS, 64, 16, 128), BF16),
            vm((8, 4, 16, 128), BF16),
            vm((8, 64, 128), BF16),
            vm((3, 256, 512), F32),
            vm((CONV_ROWS, 256), F32),
            vm((64, 1024), F32),
            vm((64, 128), F32),
            dma((PARTS + 5,)),
            dma((PARTS + 6,)),
        ],
        compiler_params=pltpu.CompilerParams(vmem_limit_bytes=62 * 2**20),
    )(result, small, enc_grad, velocity_next)
    return (
        velocity_next[None, None],
        encode.T,
        conv.reshape(27, 64, 256).transpose(0, 2, 1),
        head,
    )


def solution(mesh):
    placed = (P("sim", "grp", None, None, None), P("sim", "grp", None), P(), P(), P())
    return jax.shard_map(
        body,
        mesh=mesh,
        in_specs=placed,
        out_specs=(
            P("sim", "grp", None, None, None),
            P(None, "grp"),
            P(None, None, "grp"),
            P("grp", None),
        ),
        check_vma=False,
    )
```
